128 devices in a mesh: head: 8 (over x, y_hi), ctx: 16 (over y_lo, z, core).
Axes of the slice: x: 4, y: 4 (y_hi: 2, y_lo: 2; y = y_hi * 2 + y_lo), z: 4, core: 2. Of those that a mesh axis runs over, the one named last changes fastest.
Arguments:
- main_query: bfloat16 [2048, 73728], P('ctx', 'head'), may hold values from -400 to 400
- latent: bfloat16 [131072, 576], P('ctx'), may hold values from -20 to 20
- index_query: bfloat16 [2048, 8192], P('ctx', 'head'), may hold values from -400 to 400
- index_key: bfloat16 [131072, 128], P('ctx'), may hold values from -20 to 20
- index_weight: float32 [2048, 64], P('ctx', 'head'), may hold values from -0.1 to 0.1
- selected: int32 [2048, 32], P('ctx'), may hold values from 0 to 2047, as said below
- lengths: int32 [2048], P('ctx'), may hold values from 1985 to 131072
- cotangent: float32 [2048], P('ctx'), may hold values from 64 to 512
Outputs:
- index_query_grad: float32 [2048, 8192], P('ctx', 'head')
- index_weight_grad: float32 [2048, 64], P('ctx', 'head')
- index_key_grad: float32 [131072, 128], P('ctx')
The draws below stay inside these ranges and needn't reach their ends.
Inputs may be any that keep to these rules, and one draw needn't show every extreme that they name: `selected`: each query names 32 distinct blocks in rising order, all holding at least one visible token; its last block holds its last visible token and all others are fully visible. The queries of one ctx index name exactly 64 distinct blocks in all, at most 8 of them among the tokens of any one ctx index, and exactly 8 among those of ctx index 0.
All inputs are finite; a program needn't handle non-finite values.
Results may differ from the reference program's by a relative error of at most 0.0026.
Values may be sent and summed in bfloat16 or wider, within the bound.
A program may use at most 128 MiB of HBM per device.

```python
import math
import jax
import jax.numpy as jnp
from jax import lax

HEADS = 128
LAT = 576
INDEXER_HEADS = 64
INDEXER_HEAD_DIM = 128
BLK = 64
TOPB = 32
POOL = 64
MOST = 8
Q_DEV = 128
KEY_DEV = 8192
QUERIES = 2048
SEQ = 131072


def selection(key):
    base_key = jax.random.fold_in(key, 1013)
    devices = SEQ // KEY_DEV
    blocks_each = KEY_DEV // BLK

    def pool_of(requester):
        subkey = jax.random.fold_in(base_key, requester)
        chosen = jax.random.permutation(jax.random.fold_in(subkey, 1), (devices - 1) * MOST) < POOL - MOST
        counts = jnp.concatenate([jnp.full((1,), MOST, jnp.int32), jnp.sum(chosen.reshape(devices - 1, MOST).astype(jnp.int32), axis=1)])

        def owner_order(owner):
            return jax.random.permutation(jax.random.fold_in(subkey, 100 + owner), blocks_each)
        orders = jax.vmap(owner_order)(jnp.arange(devices, dtype=jnp.int32))
        blocks = orders[:, :MOST] + jnp.arange(devices, dtype=jnp.int32)[:, None] * blocks_each
        kept_slots = jnp.arange(MOST, dtype=jnp.int32)[None, :] < counts[:, None]
        flattened = jnp.where(kept_slots, blocks, devices * blocks_each).reshape(-1)
        return jnp.sort(flattened)[:POOL]

    def queries_of(requester, pool_blocks):
        subkey = jax.random.fold_in(base_key, 5000 + requester)
        shuffle = jax.random.permutation(jax.random.fold_in(subkey, 1), Q_DEV)
        rank_last = TOPB - 1 + shuffle % (POOL - TOPB + 1)
        rank_first = shuffle % (TOPB - 1)
        random_scores = jax.random.randint(jax.random.fold_in(subkey, 2), (Q_DEV, POOL), 0, 2 ** 20) * POOL + jnp.arange(POOL, dtype=jnp.int32)[None, :]
        pool_ranks = jnp.arange(POOL, dtype=jnp.int32)[None, :]
        eligible = (pool_ranks < rank_last[:, None]) & (pool_ranks != rank_first[:, None])
        unused, picked = lax.top_k(jnp.where(eligible, random_scores, -1), TOPB - 2)
        all_ranks = jnp.concatenate([picked, rank_first[:, None], rank_last[:, None]], axis=1)
        chosen_blocks = jnp.sort(pool_blocks[all_ranks], axis=1)
        offset = jax.random.randint(jax.random.fold_in(subkey, 3), (Q_DEV,), 1, BLK + 1)
        limits = pool_blocks[rank_last] * BLK + offset
        return (chosen_blocks, limits)
    requesters = jnp.arange(devices, dtype=jnp.int32)
    pools = jax.vmap(pool_of)(requesters)
    chosen_all, limits_all = jax.vmap(queries_of)(requesters, pools)
    return (chosen_all.reshape(-1, TOPB).astype(jnp.int32), limits_all.reshape(-1).astype(jnp.int32))


def draw_selected(key, part):
    return selection(key)[0]


def draw_lengths(key, part):
    return selection(key)[1]


def paired_rows(key, rows, width):
    return jnp.clip(jax.random.normal(key, (rows, width)), -6.0, 6.0)


def draw_latent(key, part):
    return paired_rows(jax.random.fold_in(key, 11), SEQ, LAT).astype(jnp.bfloat16)


def draw_index_key(key, part):
    return paired_rows(jax.random.fold_in(key, 31), SEQ, INDEXER_HEAD_DIM).astype(jnp.bfloat16)


def draw_index_weight(key, part):
    spread = (INDEXER_HEADS * INDEXER_HEAD_DIM) ** (-0.5)
    drawn = jnp.clip(jax.random.normal(jax.random.fold_in(key, 41), (QUERIES, INDEXER_HEADS)), -6.0, 6.0) * spread
    return jnp.clip(drawn, -0.1, 0.1)


def draw_main_query(key, part):
    shape = (QUERIES, HEADS * LAT)
    return jnp.clip(jax.random.normal(jax.random.fold_in(key, 21), shape), -6.0, 6.0).astype(jnp.bfloat16)


def draw_index_query(key, part):
    shape = (QUERIES, INDEXER_HEADS * INDEXER_HEAD_DIM)
    return jnp.clip(jax.random.normal(jax.random.fold_in(key, 51), shape), -6.0, 6.0).astype(jnp.bfloat16)


def shard_levels(own_key, shape, pieces, smallest, largest):
    def one(axis_at, blocks):
        heights = jax.random.uniform(jax.random.fold_in(jax.random.fold_in(own_key, 6), axis_at), (blocks,), jnp.float32, smallest / len(pieces), largest / len(pieces))
        return jnp.repeat(jnp.exp(heights), shape[axis_at] // blocks).reshape((-1,) + (1,) * (len(shape) - axis_at - 1))

    factor_of = one(*pieces[0])
    for cut in pieces[1:]:
        factor_of = factor_of * one(*cut)
    return factor_of


def setup_inputs(seed: int = 0) -> dict:
    streams_of = jax.random.split(jax.random.key(seed), 9)
    main_query = draw_main_query(jax.random.fold_in(streams_of[8], 71), 0)
    latent = draw_latent(jax.random.fold_in(streams_of[8], 71), 0)
    index_query = draw_index_query(jax.random.fold_in(streams_of[8], 71), 0)
    index_key = draw_index_key(jax.random.fold_in(streams_of[8], 71), 0)
    index_weight = draw_index_weight(jax.random.fold_in(streams_of[8], 71), 0)
    selected = draw_selected(jax.random.fold_in(streams_of[8], 71), 0)
    lengths = draw_lengths(jax.random.fold_in(streams_of[8], 71), 0)
    cotangent = jnp.clip(jnp.exp(math.log(512.0) - 2.0794415 * jax.random.uniform(streams_of[7], (QUERIES,), jnp.float32) ** shard_levels(streams_of[7], (QUERIES,), ((0, 16),), -0.2, 0.2)), 64.0, 512.0)
    return dict(main_query=main_query, latent=latent, index_query=index_query, index_key=index_key, index_weight=index_weight, selected=selected, lengths=lengths, cotangent=cotangent)


logit_scale = 192.0 ** -0.5


def masked_softmax(values, visible):
    highest = jnp.max(jnp.where(visible, values, -jnp.inf), axis=-1, keepdims=True)
    weights = jnp.where(visible, jnp.exp(values - highest), 0.0)
    return weights / jnp.sum(weights, axis=-1, keepdims=True)


def reference(main_query, latent, index_query, index_key, index_weight, selected, lengths, cotangent):
    query_count = main_query.shape[0]
    group_width = 16
    group_count = query_count // group_width
    offsets = jnp.arange(BLK, dtype=jnp.int32)

    def one_group(running, group_index):
        start = (group_index * group_width).astype(jnp.int32)

        def take(array):
            return lax.dynamic_slice_in_dim(array, start, group_width, 0)

        chosen_blocks = take(selected)
        limits = take(lengths)
        tokens = (chosen_blocks[:, :, None] * BLK + offsets[None, None, :]).reshape(group_width, TOPB * BLK).astype(jnp.int32)
        visible = tokens < limits[:, None]
        latent_tokens = latent[tokens].astype(jnp.float32)
        query_rows = take(main_query).reshape(group_width, HEADS, LAT).astype(jnp.float32)
        score_matrix = jnp.einsum("iwm,ium->iwu", query_rows, latent_tokens) * logit_scale
        target = jnp.sum(masked_softmax(score_matrix, visible[:, None, :]), axis=1) / HEADS
        indexer_rows = index_key[tokens].astype(jnp.float32)
        indexer_block = take(index_query).reshape(group_width, INDEXER_HEADS, INDEXER_HEAD_DIM).astype(jnp.float32)
        weights = take(index_weight)
        raw_logits = jnp.einsum("lpa,lqa->lpq", indexer_block, indexer_rows)
        rectified = jnp.maximum(raw_logits, 0.0)
        index_scores = jnp.einsum("bj,bjk->bk", weights, rectified)
        chosen = masked_softmax(index_scores, visible)
        grad_scores = take(cotangent)[:, None] * (chosen - target)
        weight_grad = jnp.einsum("bjk,bk->bj", rectified, grad_scores)
        link_weights = jnp.where(raw_logits > 0, grad_scores[:, None, :] * weights[:, :, None], 0.0)
        link_weights = lax.optimization_barrier(link_weights.astype(jnp.bfloat16)).astype(jnp.float32)
        query_gradient = jnp.einsum("nwh,nhm->nwm", link_weights, indexer_rows).reshape(group_width, INDEXER_HEADS * INDEXER_HEAD_DIM)
        key_factors = jnp.einsum("yvx,yvc->yxc", link_weights, indexer_block)
        running = running.at[tokens.reshape(-1)].add(key_factors.reshape(-1, INDEXER_HEAD_DIM))
        return running, (query_gradient, weight_grad)

    key_grad, (query_gradient, weight_grad) = lax.scan(one_group, jnp.zeros((SEQ, INDEXER_HEAD_DIM), jnp.float32), jnp.arange(group_count, dtype=jnp.int32))
    return query_gradient.reshape(query_count, INDEXER_HEADS * INDEXER_HEAD_DIM), weight_grad.reshape(query_count, INDEXER_HEADS), key_grad
```

```python
import functools
import math

import jax
import jax.numpy as jnp
from jax import lax
from jax.experimental import pallas as pl
from jax.experimental.pallas import tpu as pltpu
from jax.sharding import PartitionSpec as P

HEADS = 128
BLK = 64
POOL = 64
NH = 8
NC = 16
LAT = 576
WIDTH = 128
QROWS = 16
SETB = POOL // NH
SETT = SETB * BLK
HALF = LAT // 2
SLOT = HALF + BLK
SETROWS = LAT * (SETT // 128) + SETT
UNION = POOL * BLK
IHEADS = 64

MESH = pl.DeviceIdType.MESH
ANY = pl.ANY
VM = pltpu.VMEM
DMA = pltpu.SemaphoreType.DMA

scale2 = 192.0 ** (-0.5) * math.log2(math.e)


def roll64(x):
    return pltpu.roll(x, 64, 1)


def start_barrier(me_h, me_c):
    barrier = pltpu.get_barrier_semaphore()
    for o in range(1, NH):
        pl.semaphore_signal(
            barrier, inc=1, device_id=(lax.rem(me_h + o, NH), me_c), device_id_type=MESH
        )
    for o in range(1, NC):
        pl.semaphore_signal(
            barrier, inc=1, device_id=(me_h, lax.rem(me_c + o, NC)), device_id_type=MESH
        )
    pl.semaphore_wait(barrier, NH + NC - 2)


def remote(src, dst, ssem, rsem, device):
    return pltpu.make_async_remote_copy(
        src_ref=src, dst_ref=dst, send_sem=ssem, recv_sem=rsem, device_id=device, device_id_type=MESH
    )


def gather_sets(own, out, half, me_h, me_c, ssem, rsem, lsem):
    right = (lax.rem(me_h + 2, NH), me_c)
    left = (lax.rem(me_h + 6, NH), me_c)
    flip = me_h + 1 - 2 * lax.rem(me_h, 2)
    partner = (flip, me_c)

    def flipped(h):
        return h + 1 - 2 * lax.rem(h, 2)

    started = []

    def go(src, dst, i, device):
        c = remote(src, dst, ssem.at[i], rsem.at[i], device)
        c.start()
        started.append(c)
        return c

    mine = pltpu.make_async_copy(own, out.at[me_h], lsem)
    mine.start()
    cy = go(own, out.at[me_h], 0, partner)
    cr = go(own, out.at[me_h], 1, right)
    cl = go(own, out.at[me_h], 2, left)
    remote(own, out.at[flip], ssem.at[0], rsem.at[0], partner).wait_recv()
    go(out.at[flip], out.at[flip], 3, right)
    go(out.at[flip], out.at[flip], 4, left)
    hl = lax.rem(me_h + 6, NH)
    hr = lax.rem(me_h + 2, NH)
    lo = pl.ds(0, half)
    hi = pl.ds(half, half)
    remote(own, out.at[hl], ssem.at[1], rsem.at[1], right).wait_recv()
    go(out.at[hl, lo], out.at[hl, lo], 5, right)
    remote(own, out.at[hr], ssem.at[2], rsem.at[2], left).wait_recv()
    go(out.at[hr, hi], out.at[hr, hi], 6, left)
    remote(own, out.at[flipped(hl)], ssem.at[3], rsem.at[3], right).wait_recv()
    go(out.at[flipped(hl), lo], out.at[flipped(hl), lo], 7, right)
    remote(own, out.at[flipped(hr)], ssem.at[4], rsem.at[4], left).wait_recv()
    go(out.at[flipped(hr), hi], out.at[flipped(hr), hi], 8, left)
    far = lax.rem(me_h + 4, NH)
    remote(out.at[far, lo], out.at[far, lo], ssem.at[5], rsem.at[5], right).wait_recv()
    remote(out.at[far, hi], out.at[far, hi], ssem.at[6], rsem.at[6], left).wait_recv()
    ff = flipped(far)
    remote(out.at[ff, lo], out.at[ff, lo], ssem.at[7], rsem.at[7], right).wait_recv()
    remote(out.at[ff, hi], out.at[ff, hi], ssem.at[8], rsem.at[8], left).wait_recv()
    mine.wait()
    for c in started:
        c.wait_send()


def iota(shape, dim):
    return lax.broadcasted_iota(jnp.int32, shape, dim)


def plan(sel, req_ref, tab_ref):
    hi = lax.shift_right_logical(sel, 7)
    lo = lax.bitwise_and(sel, 127)
    rows = sel.shape[0]
    owner_hot = jnp.concatenate(
        [jnp.where(iota((NC, 128), 0) == hi[i : i + 1, :], 1.0, 0.0) for i in range(rows)], axis=1
    ).astype(jnp.bfloat16)
    local_hot = jnp.concatenate(
        [jnp.where(iota((128, 128), 0) == lo[i : i + 1, :], 1.0, 0.0) for i in range(rows)], axis=1
    ).astype(jnp.bfloat16)
    counts = lax.dot_general(
        owner_hot, local_hot, (((1,), (1,)), ((), ())), preferred_element_type=jnp.float32
    )
    present = jnp.where(counts > 0.5, 1.0, 0.0)
    upper = jnp.where(iota((128, 128), 0) <= iota((128, 128), 1), 1.0, 0.0).astype(jnp.bfloat16)
    rank = jnp.dot(present.astype(jnp.bfloat16), upper, preferred_element_type=jnp.float32)
    total = rank[:, 127:128]
    lane = iota((NC, 128), 1)
    sub = iota((NC, 128), 0)
    spread = jnp.sum(jnp.where(lane == sub, total, 0.0), axis=0, keepdims=True)
    before = jnp.sum(jnp.where(lane < sub, jnp.broadcast_to(spread, (NC, 128)), 0.0), axis=1, keepdims=True)
    pos = (before + rank - 1.0).astype(jnp.int32)
    slot = lax.bitwise_and(pos, 7)
    step = lax.shift_right_logical(pos, 3).astype(jnp.float32)
    lane_f = lane.astype(jnp.float32)
    there = present > 0.5
    req = jnp.zeros((NC, 128), jnp.float32)
    ids = jnp.zeros((NC, 128), jnp.float32)
    owners = jnp.zeros((NC, 128), jnp.float32)
    sub_f = sub.astype(jnp.float32)
    for k in range(NH):
        hit = there & (slot == k)
        local = jnp.sum(jnp.where(hit, lane_f, 0.0), axis=1, keepdims=True)
        at = jnp.sum(jnp.where(hit, step, 0.0), axis=1, keepdims=True)
        has = jnp.sum(jnp.where(hit, 1.0, 0.0), axis=1, keepdims=True)
        req = jnp.where(lane == k, local, req)
        here = jnp.where(lane_f == at + float(SETB * k), has, 0.0)
        ids = ids + here * (sub_f * 128.0 + local)
        owners = owners + here * sub_f
        back = jnp.where(has > 0.5, at, float(SETB))
        row = jnp.sum(jnp.where(lane == sub, back, 0.0), axis=0, keepdims=True)
        tab_ref[8 + k : 9 + k, :] = row.astype(jnp.int32)
    tab_ref[0:1, :] = jnp.sum(ids, axis=0, keepdims=True).astype(jnp.int32)
    tab_ref[1:2, :] = jnp.sum(owners, axis=0, keepdims=True).astype(jnp.int32)
    tab_ref[2:8, :] = jnp.zeros((6, 128), jnp.int32)
    req_ref[...] = jnp.broadcast_to(req.astype(jnp.int32)[:, None, :], (NC, 8, 128))


def plan_kernel(sel_ref, req_ref, tab_ref):
    plan(sel_ref[...], req_ref, tab_ref)


def make_plan(sel_t):
    vm_spec = pl.BlockSpec(memory_space=VM)
    return pl.pallas_call(
        plan_kernel,
        name="plan",
        out_shape=(
            jax.ShapeDtypeStruct((NC, 8, 128), jnp.int32),
            jax.ShapeDtypeStruct((16, 128), jnp.int32),
        ),
        in_specs=[vm_spec],
        out_specs=(vm_spec, vm_spec),
        compiler_params=pltpu.CompilerParams(vmem_limit_bytes=32 << 20),
    )(sel_t)


def fetch_kernel(
    tab_s, req, lat_hbm, ik_hbm, mq_hbm, iq_hbm, w_hbm,
    set_out, mq_out, iq_out, w_out, asked_out,
    lat_v, ik_v, stage, recv, own, asked, asked_s,
    q_send, q_recv, i_send, i_recv, w_send, w_recv, r_send, r_recv, b_send, b_recv, g_send, g_recv, loc, l_sem,
):
    me_h = lax.axis_index("head")
    me_c = lax.axis_index("ctx")
    loads = [pltpu.make_async_copy(ik_hbm, ik_v, loc.at[1])] + [
        pltpu.make_async_copy(lat_hbm.at[:, pl.ds(i * 128, 128)], lat_v.at[i], l_sem.at[i])
        for i in range(lat_v.shape[0])
    ]
    for c in loads:
        c.start()
    my_q = pl.ds(pl.multiple_of(me_h * QROWS, QROWS), QROWS)
    own_copies = [
        pltpu.make_async_copy(mq_hbm.at[my_q], mq_out.at[me_h], loc.at[2]),
        pltpu.make_async_copy(iq_hbm.at[my_q], iq_out.at[me_h], loc.at[3]),
        pltpu.make_async_copy(w_hbm, w_out.at[me_h], loc.at[4]),
    ]
    for c in own_copies:
        c.start()
    start_barrier(me_h, me_c)
    sends = []
    own_req = pltpu.make_async_copy(req.at[me_c], asked.at[me_c], loc.at[6])
    own_req.start()
    for o in range(1, NC):
        c = lax.rem(me_c + o, NC)
        s = remote(req.at[c], asked.at[me_c], r_send.at[o], r_recv.at[o], (me_h, c))
        s.start()
        sends.append(s)
    for o in range(1, NH):
        h = lax.rem(me_h + o, NH)
        s = remote(
            mq_hbm.at[pl.ds(pl.multiple_of(h * QROWS, QROWS), QROWS)],
            mq_out.at[me_h], q_send.at[o], q_recv.at[o], (h, me_c),
        )
        s.start()
        sends.append(s)
        s = remote(
            iq_hbm.at[pl.ds(pl.multiple_of(h * QROWS, QROWS), QROWS)],
            iq_out.at[me_h], i_send.at[o], i_recv.at[o], (h, me_c),
        )
        s.start()
        sends.append(s)
        s = remote(w_hbm, w_out.at[me_h], w_send.at[o], w_recv.at[o], (h, me_c))
        s.start()
        sends.append(s)
    own_req.wait()
    for o in range(1, NC):
        c = lax.rem(me_c + NC - o, NC)
        remote(req.at[c], asked.at[c], r_send.at[o], r_recv.at[o], (me_h, c)).wait_recv()
    asked_out[...] = asked[:, 0, :]
    asked_copy = pltpu.make_async_copy(asked_out, asked_s, loc.at[7])
    asked_copy.start()
    for c in loads:
        c.wait()
    asked_copy.wait()
    first = iota((HALF, 128), 1) < 64
    for o in range(1, NC + 1):
        r = lax.rem(me_c + o, NC)
        b = asked_s[r, me_h]
        odd = jnp.full((HALF, 128), lax.bitwise_and(b, 1), jnp.int32) == 1
        pair = lax.shift_right_logical(b, 1)
        top = lat_v[pair, 0:HALF, :].astype(jnp.float32)
        bot = lat_v[pair, HALF:LAT, :].astype(jnp.float32)
        packed = jnp.where(
            first, jnp.where(odd, roll64(top), top), jnp.where(odd, bot, roll64(bot))
        ).astype(jnp.bfloat16)
        keys = ik_v[b]
        if o < NC:
            stage[o, 0:HALF, :] = packed
            stage[o, HALF:SLOT, :] = keys
            s = remote(stage.at[o], recv.at[me_c], b_send.at[o], b_recv.at[o], (me_h, r))
            s.start()
            sends.append(s)
        else:
            recv[me_c, 0:HALF, :] = packed
            recv[me_c, HALF:SLOT, :] = keys
    for o in range(1, NC):
        c = lax.rem(me_c + NC - o, NC)
        remote(stage.at[o], recv.at[c], b_send.at[o], b_recv.at[o], (me_h, c)).wait_recv()
    for i in range(SETB // 2):
        ca = tab_s[1, me_h * SETB + 2 * i]
        cb = tab_s[1, me_h * SETB + 2 * i + 1]
        a = recv[ca, 0:HALF, :].astype(jnp.float32)
        b = recv[cb, 0:HALF, :].astype(jnp.float32)
        own[i * LAT : i * LAT + HALF, :] = jnp.where(first, a, roll64(b)).astype(jnp.bfloat16)
        own[i * LAT + HALF : (i + 1) * LAT, :] = jnp.where(first, roll64(a), b).astype(jnp.bfloat16)
        base = LAT * (SETT // 128) + 2 * i * BLK
        own[base : base + BLK, :] = recv[ca, HALF:SLOT, :]
        own[base + BLK : base + 2 * BLK, :] = recv[cb, HALF:SLOT, :]
    gather_sets(own, set_out, SETROWS // 2, me_h, me_c, g_send, g_recv, loc.at[8])
    for o in range(1, NH):
        h = lax.rem(me_h + NH - o, NH)
        rows = pl.ds(0, QROWS)
        remote(mq_hbm.at[rows], mq_out.at[h], q_send.at[o], q_recv.at[o], (h, me_c)).wait_recv()
        remote(iq_hbm.at[rows], iq_out.at[h], i_send.at[o], i_recv.at[o], (h, me_c)).wait_recv()
        remote(w_hbm, w_out.at[h], w_send.at[o], w_recv.at[o], (h, me_c)).wait_recv()
    for c in own_copies:
        c.wait()
    for s in sends:
        s.wait_send()


def fetch(tab, req, lat_t, index_key, main_query, index_query, weight_t):
    any_spec = pl.BlockSpec(memory_space=ANY)
    vm_spec = pl.BlockSpec(memory_space=VM)
    bf, i32 = jnp.bfloat16, jnp.int32
    return pl.pallas_call(
        fetch_kernel,
        name="fetch",
        out_shape=(
            jax.ShapeDtypeStruct((NH, SETROWS, 128), bf),
            jax.ShapeDtypeStruct((NH, QROWS, main_query.shape[1]), bf),
            jax.ShapeDtypeStruct((NH, QROWS, index_query.shape[1]), bf),
            jax.ShapeDtypeStruct((NH, 8, 128), jnp.float32),
            jax.ShapeDtypeStruct((16, 128), i32),
        ),
        in_specs=[pl.BlockSpec(memory_space=pltpu.SMEM), vm_spec] + [any_spec] * 5,
        out_specs=(any_spec,) * 4 + (vm_spec,),
        scratch_shapes=[
            VM((lat_t.shape[1] // 128, LAT, 128), bf),
            VM(index_key.shape, bf),
            VM((NC, SLOT, 128), bf),
            VM((NC, SLOT, 128), bf),
            VM((SETROWS, 128), bf),
            VM((NC, 8, 128), i32),
            pltpu.SMEM((16, 128), i32),
            DMA((NH,)), DMA((NH,)), DMA((NH,)), DMA((NH,)), DMA((NH,)), DMA((NH,)),
            DMA((NC,)), DMA((NC,)), DMA((NC,)), DMA((NC,)),
            DMA((9,)), DMA((9,)), DMA((9,)), DMA((lat_t.shape[1] // 128,)),
        ],
        compiler_params=pltpu.CompilerParams(
            collective_id=0, has_side_effects=True, vmem_limit_bytes=32 << 20
        ),
    )(tab, req, lat_t, index_key, main_query, index_query, weight_t)


def core_kernel(
    tab_s, set_ref, mq_ref, iq_ref, w_ref, sel_ref, len_ref, cot_ref,
    ug_ref, iqg_ref, wg_ref,
    s_ref, pre_ref, edge_ref, bias_ref, tgt_ref, idx_ref, grad_ref, meta_ref, wq_ref, selb_ref, wb_ref, iqr_ref, qt_ref, ugt_ref, wcol_ref,
):
    me = lax.axis_index("head")
    mine = pl.ds(pl.multiple_of(me * QROWS, QROWS), QROWS)
    f32, bf = jnp.float32, jnp.bfloat16
    top = sel_ref.shape[0]
    meta_ref[...] = jnp.zeros((128, 128), f32)
    meta_ref[0:top, :] = sel_ref[...].astype(f32)
    meta_ref[top : top + 1, :] = len_ref[...].astype(f32)
    meta_ref[top + 1 : top + 2, :] = cot_ref[...]
    meta_ref[64 : 64 + IHEADS, :] = w_ref[...].reshape(IHEADS, 128)
    meta_ref[...] = meta_ref[...].T
    row = meta_ref[mine, :]
    for i in range(top):
        selb_ref[i] = jnp.broadcast_to(row[:, i : i + 1], (QROWS, 128))
    limit = jnp.broadcast_to(row[:, top : top + 1], (QROWS, 128))
    cot = row[:, top + 1 : top + 2]
    for j in range(IHEADS):
        wb_ref[j] = jnp.broadcast_to(row[:, 64 + j : 65 + j], (QROWS, 128))
    lane = iota((QROWS, 128), 1)

    def mask_tile(i, carry):
        b0 = tab_s[0, 2 * i]
        b1 = tab_s[0, 2 * i + 1]
        block = jnp.where(lane < 64, b0, b1)
        block_f = block.astype(f32)
        hit = selb_ref[0] == block_f
        for q in range(1, top):
            hit = hit | (selb_ref[q] == block_f)
        token = (block * BLK + lax.bitwise_and(lane, 63)).astype(f32)
        ok = hit & (token < limit)
        bias_ref[:, pl.ds(pl.multiple_of(i * 128, 128), 128)] = jnp.where(ok, 0.0, -jnp.inf)
        return carry

    lax.fori_loop(0, UNION // 128, mask_tile, 0)

    for h in range(NH):
        for k in range(8):
            iqr_ref[(h * 8 + k) * QROWS : (h * 8 + k + 1) * QROWS, :] = iq_ref[h, :, k * 128 : (k + 1) * 128]
    KEY0 = LAT * (SETT // 128)
    for h in range(NH):
        pre_ref[:, h * SETT : (h + 1) * SETT] = lax.dot_general(
            iqr_ref[...], set_ref[h, KEY0 : KEY0 + SETT, :], (((1,), (1,)), ((), ())), preferred_element_type=f32
        )
    CH = 512

    def index_chunk(i, carry):
        cols = pl.ds(pl.multiple_of(i * CH, CH), CH)
        acc = jnp.zeros((QROWS, CH), f32)
        for j in range(IHEADS):
            w = jnp.concatenate([wb_ref[j]] * (CH // 128), axis=1)
            acc = acc + w * jnp.maximum(pre_ref[j * QROWS : (j + 1) * QROWS, cols], 0.0)
        idx_ref[:, cols] = acc + bias_ref[:, cols]
        return carry

    lax.fori_loop(0, UNION // CH, index_chunk, 0)

    tgt_ref[...] = jnp.zeros((QROWS, UNION), f32)
    per = mq_ref.shape[2] // LAT

    def head_group(g, carry):
        for k in range(per):
            qt_ref[k * QROWS : (k + 1) * QROWS, :] = mq_ref[g, :, k * LAT : (k + 1) * LAT]
        for h in range(NH):
            for t in range(SETT // 256):
                keys = jnp.concatenate(
                    [set_ref[h, (2 * t + q) * LAT : (2 * t + q + 1) * LAT, :] for q in range(2)], axis=1
                )
                at = h * SETT + t * 256
                s_ref[:, at : at + 256] = jnp.dot(qt_ref[...], keys, preferred_element_type=f32)
        recips = []
        for k in range(per):
            rows = slice(k * QROWS, (k + 1) * QROWS)
            high = jnp.full((QROWS, 128), -jnp.inf, f32)
            for t in range(UNION // 128):
                cols = slice(t * 128, (t + 1) * 128)
                v = s_ref[rows, cols] + bias_ref[:, cols]
                s_ref[rows, cols] = v
                high = jnp.maximum(high, v)
            top_v = jnp.broadcast_to(jnp.max(high, axis=1, keepdims=True), (QROWS, 128))
            den = jnp.zeros((QROWS, 128), f32)
            for t in range(UNION // 128):
                cols = slice(t * 128, (t + 1) * 128)
                p = jnp.exp2((s_ref[rows, cols] - top_v) * scale2)
                s_ref[rows, cols] = p
                den = den + p
            recips.append(jnp.broadcast_to(1.0 / jnp.sum(den, axis=1, keepdims=True), (QROWS, 128)))
        for t in range(UNION // 128):
            cols = slice(t * 128, (t + 1) * 128)
            acc = tgt_ref[:, cols]
            for k in range(per):
                acc = acc + s_ref[k * QROWS : (k + 1) * QROWS, cols] * recips[k]
            tgt_ref[:, cols] = acc
        return carry

    lax.fori_loop(0, NH, head_group, 0)

    v = idx_ref[...]
    e = jnp.exp(v - jnp.max(v, axis=1, keepdims=True))
    chosen = e / jnp.sum(e, axis=1, keepdims=True)
    grad_ref[...] = cot * (chosen - tgt_ref[...] * (1.0 / HEADS))

    def back_head(j, carry):
        rows = pl.ds(pl.multiple_of(j * QROWS, QROWS), QROWS)
        w = wb_ref[j]
        total = jnp.zeros((QROWS, 128), f32)
        for t in range(UNION // 128):
            cols = slice(t * 128, (t + 1) * 128)
            pre = pre_ref[rows, cols]
            grad = grad_ref[:, cols]
            total = total + jnp.maximum(pre, 0.0) * grad
            edge_ref[rows, cols] = jnp.where(pre > 0.0, grad * w, 0.0).astype(bf)
        wcol_ref[j] = jnp.broadcast_to(jnp.sum(total, axis=1, keepdims=True), (QROWS, 128))
        return carry

    lax.fori_loop(0, IHEADS, back_head, 0)
    lane64 = iota((QROWS, 128), 1)
    wrow = jnp.zeros((QROWS, 128), f32)
    for j in range(IHEADS):
        wrow = jnp.where(lane64 == j, wcol_ref[j], wrow)
    wq_ref[...] = jnp.zeros((128, 128), f32)
    wq_ref[mine, :] = wrow
    wg_ref[...] = wq_ref[...].T[0:IHEADS, :].reshape(NH, 8, 128)

    iq_t = iqr_ref[...].T
    for h in range(NH):
        part = edge_ref[:, h * SETT : (h + 1) * SETT]
        ug_ref[h] = jnp.dot(iq_t, part, preferred_element_type=f32).T
    for g in range(NH):
        rows = slice(g * 128, (g + 1) * 128)
        acc = jnp.zeros((128, 128), f32)
        for h in range(NH):
            acc = acc + jnp.dot(
                edge_ref[rows, h * SETT : (h + 1) * SETT], set_ref[h, KEY0 : KEY0 + SETT, :], preferred_element_type=f32
            )
        for k in range(8):
            iqg_ref[g, :, k * 128 : (k + 1) * 128] = acc[k * QROWS : (k + 1) * QROWS, :]


def core(tab, sets, mq, iq, w, sel_t, lengths, cot):
    f32, bf = jnp.float32, jnp.bfloat16
    vm_spec = pl.BlockSpec(memory_space=VM)
    rows = IHEADS * QROWS
    return pl.pallas_call(
        core_kernel,
        name="core",
        out_shape=(
            jax.ShapeDtypeStruct((NH, SETT, 128), f32),
            jax.ShapeDtypeStruct((NH, QROWS, 1024), f32),
            jax.ShapeDtypeStruct((NH, 8, 128), f32),
        ),
        in_specs=[pl.BlockSpec(memory_space=pltpu.SMEM)] + [vm_spec] * 7,
        out_specs=(vm_spec,) * 3,
        scratch_shapes=[
            VM((256, UNION), f32),
            VM((rows, UNION), f32),
            VM((rows, UNION), bf),
            VM((QROWS, UNION), f32),
            VM((QROWS, UNION), f32),
            VM((QROWS, UNION), f32),
            VM((QROWS, UNION), f32),
            VM((128, 128), f32),
            VM((128, 128), f32),
            VM((32, QROWS, 128), f32),
            VM((IHEADS, QROWS, 128), f32),
            VM((rows, 128), bf),
            VM((256, LAT), bf),
            VM((128, SETT), f32),
            VM((IHEADS, QROWS, 128), f32),
        ],
        compiler_params=pltpu.CompilerParams(vmem_limit_bytes=58 << 20),
    )(tab, sets, mq, iq, w, sel_t, lengths, cot)


def return_kernel(
    tab_s, ug_hbm, iqg_hbm, wg_hbm,
    iqg_out, wg_out, kg_out,
    urecv, sums, slots, brecv, own, wrecv,
    u_send, u_recv, i_send, i_recv, w_send, w_recv, b_send, b_recv, g_send, g_recv, loc,
):
    me_h = lax.axis_index("head")
    me_c = lax.axis_index("ctx")
    own_copies = [
        pltpu.make_async_copy(ug_hbm.at[me_h], urecv.at[me_h], loc.at[0]),
        pltpu.make_async_copy(
            iqg_hbm.at[me_h], iqg_out.at[pl.ds(pl.multiple_of(me_h * QROWS, QROWS), QROWS)], loc.at[1]
        ),
        pltpu.make_async_copy(wg_hbm.at[me_h], wrecv.at[me_h], loc.at[2]),
    ]
    for c in own_copies:
        c.start()
    start_barrier(me_h, me_c)
    sends = []
    for o in range(1, NH):
        h = lax.rem(me_h + o, NH)
        s = remote(ug_hbm.at[h], urecv.at[me_h], u_send.at[o], u_recv.at[o], (h, me_c))
        s.start()
        sends.append(s)
    for o in range(1, NH):
        h = lax.rem(me_h + o, NH)
        s = remote(
            iqg_hbm.at[h], iqg_out.at[pl.ds(pl.multiple_of(me_h * QROWS, QROWS), QROWS)],
            i_send.at[o], i_recv.at[o], (h, me_c),
        )
        s.start()
        sends.append(s)
        s = remote(wg_hbm.at[h], wrecv.at[me_h], w_send.at[o], w_recv.at[o], (h, me_c))
        s.start()
        sends.append(s)
    own_copies[0].wait()
    for o in range(1, NH):
        h = lax.rem(me_h + NH - o, NH)
        remote(ug_hbm.at[h], urecv.at[h], u_send.at[o], u_recv.at[o], (h, me_c)).wait_recv()
    for j in range(SETB):
        acc = urecv[0, j * BLK : (j + 1) * BLK, :]
        for h in range(1, NH):
            acc = acc + urecv[h, j * BLK : (j + 1) * BLK, :]
        sums[j] = acc
    sums[SETB] = jnp.zeros((BLK, 128), jnp.float32)
    for o in range(1, NC + 1):
        c = lax.rem(me_c + o, NC)
        value = sums[tab_s[8 + me_h, c]]
        if o < NC:
            slots[o] = value
            s = remote(slots.at[o], brecv.at[me_c], b_send.at[o], b_recv.at[o], (me_h, c))
            s.start()
            sends.append(s)
        else:
            brecv[me_c] = value
    for o in range(1, NC):
        c = lax.rem(me_c + NC - o, NC)
        remote(slots.at[o], brecv.at[c], b_send.at[o], b_recv.at[o], (me_h, c)).wait_recv()
    for r in range(NC):
        own[r * BLK : (r + 1) * BLK, :] = brecv[r].astype(own.dtype)
    gather_sets(own, kg_out, NC * BLK // 2, me_h, me_c, g_send, g_recv, loc.at[3])
    for o in range(1, NH):
        h = lax.rem(me_h + NH - o, NH)
        remote(
            iqg_hbm.at[h], iqg_out.at[pl.ds(pl.multiple_of(h * QROWS, QROWS), QROWS)],
            i_send.at[o], i_recv.at[o], (h, me_c),
        ).wait_recv()
        remote(wg_hbm.at[h], wrecv.at[h], w_send.at[o], w_recv.at[o], (h, me_c)).wait_recv()
    own_copies[1].wait()
    own_copies[2].wait()
    acc = wrecv[0]
    for h in range(1, NH):
        acc = acc + wrecv[h]
    wg_out[...] = acc
    for s in sends:
        s.wait_send()


SENT = jnp.float32


def give_back(tab, ug, iqg, wg):
    f32 = jnp.float32
    any_spec = pl.BlockSpec(memory_space=ANY)
    return pl.pallas_call(
        return_kernel,
        name="give_back",
        out_shape=(
            jax.ShapeDtypeStruct((NH * QROWS, 1024), f32),
            jax.ShapeDtypeStruct((8, 128), f32),
            jax.ShapeDtypeStruct((NH, NC * BLK, 128), SENT),
        ),
        in_specs=[pl.BlockSpec(memory_space=pltpu.SMEM)] + [any_spec] * 3,
        out_specs=(any_spec, pl.BlockSpec(memory_space=VM), any_spec),
        scratch_shapes=[
            VM((NH, SETT, 128), f32),
            VM((SETB + 1, BLK, 128), f32),
            VM((NC, BLK, 128), f32),
            VM((NC, BLK, 128), f32),
            VM((NC * BLK, 128), SENT),
            VM((NH, 8, 128), f32),
            DMA((NH,)), DMA((NH,)), DMA((NH,)), DMA((NH,)), DMA((NH,)), DMA((NH,)),
            DMA((NC,)), DMA((NC,)),
            DMA((9,)), DMA((9,)), DMA((4,)),
        ],
        compiler_params=pltpu.CompilerParams(
            collective_id=1, has_side_effects=True, vmem_limit_bytes=32 << 20
        ),
    )(tab, ug, iqg, wg)


def scatter_kernel(asked_s, kg_ref, out_ref):
    out_ref[...] = jnp.zeros(out_ref.shape, jnp.float32)

    def one(i, carry):
        h = lax.shift_right_logical(i, 4)
        r = lax.bitwise_and(i, 15)
        b = asked_s[r, h]
        rows = pl.ds(pl.multiple_of(b * BLK, BLK), BLK)
        out_ref[rows, :] = out_ref[rows, :] + kg_ref[h, pl.ds(pl.multiple_of(r * BLK, BLK), BLK), :].astype(jnp.float32)
        return carry

    lax.fori_loop(0, NH * NC, one, 0)


def scatter(asked, kg, tokens):
    return pl.pallas_call(
        scatter_kernel,
        name="scatter",
        out_shape=jax.ShapeDtypeStruct((tokens, 128), jnp.float32),
        in_specs=[pl.BlockSpec(memory_space=pltpu.SMEM), pl.BlockSpec(memory_space=VM)],
        out_specs=pl.BlockSpec(memory_space=VM),
        compiler_params=pltpu.CompilerParams(vmem_limit_bytes=32 << 20),
    )(asked, kg)


def shards(main_query, latent, index_query, index_key, index_weight, selected, lengths, cotangent):
    sel_t = selected.T
    req, tab = make_plan(sel_t)
    sets, mq, iq, w, asked = fetch(
        tab, req, latent.T, index_key.reshape(-1, BLK, WIDTH), main_query, index_query, index_weight.T
    )
    ug, iqg, wg = core(tab, sets, mq, iq, w, sel_t, lengths[None, :], cotangent[None, :])
    query_grad, weight_grad, kg = give_back(tab, ug, iqg, wg)
    key_grad = scatter(asked, kg, latent.shape[0])
    return query_grad, weight_grad.T, key_grad


def solution(mesh):
    return jax.shard_map(
        shards,
        mesh=mesh,
        in_specs=(
            P("ctx", "head"),
            P("ctx", None),
            P("ctx", "head"),
            P("ctx", None),
            P("ctx", "head"),
            P("ctx", None),
            P("ctx"),
            P("ctx"),
        ),
        out_specs=(P("ctx", "head"), P("ctx", "head"), P("ctx", None)),
        check_vma=False,
    )
```

```python
import functools
import math

import jax
import jax.numpy as jnp
from jax import lax
from jax.experimental import pallas as pl
from jax.experimental.pallas import tpu as pltpu
from jax.sharding import PartitionSpec as P

HEADS = 128
BLK = 64
POOL = 64
NH = 8
NC = 16
LAT = 576
WIDTH = 128
QROWS = 16
SETB = POOL // NH
SETT = SETB * BLK
HALF = LAT // 2
SLOT = HALF + BLK
UNION = POOL * BLK
IHEADS = 64

MESH = pl.DeviceIdType.MESH
ANY = pltpu.HBM
VM = pltpu.VMEM
DMA = pltpu.SemaphoreType.DMA

HIDDEN = -1e30
scale2 = 192.0 ** (-0.5) * math.log2(math.e)


def roll64(x):
    return pltpu.roll(x, 64, 1)


def start_barrier(me_h, me_c):
    barrier = pltpu.get_barrier_semaphore()
    for o in range(1, NH):
        pl.semaphore_signal(
            barrier, inc=1, device_id=(lax.rem(me_h + o, NH), me_c), device_id_type=MESH
        )
    for o in range(1, NC):
        pl.semaphore_signal(
            barrier, inc=1, device_id=(me_h, lax.rem(me_c + o, NC)), device_id_type=MESH
        )
    pl.semaphore_wait(barrier, NH + NC - 2)


def remote(src, dst, ssem, rsem, device):
    return pltpu.make_async_remote_copy(
        src_ref=src, dst_ref=dst, send_sem=ssem, recv_sem=rsem, device_id=device, device_id_type=MESH
    )


def gather_sets(pieces, me_h, me_c, ssem, rsem, lsem, between=None):
    right = (lax.rem(me_h + 2, NH), me_c)
    left = (lax.rem(me_h + 6, NH), me_c)
    flip = me_h + 1 - 2 * lax.rem(me_h, 2)
    partner = (flip, me_c)
    hl = lax.rem(me_h + 6, NH)
    hr = lax.rem(me_h + 2, NH)
    far = lax.rem(me_h + 4, NH)

    def flipped(h):
        return h + 1 - 2 * lax.rem(h, 2)

    count = len(pieces)
    sent = []

    def part(n, which):
        own, out, start, rows = pieces[n]
        half = rows // 32 * 16
        if which == 0:
            return start, rows
        return (start, half) if which == 1 else (start + half, rows - half)

    def copy(n, i, h, which, device, first=False):
        own, out, _, _ = pieces[n]
        start, rows = part(n, which)
        dst = out.at[h, pl.ds(start, rows)]
        src = own.at[pl.ds(start, rows)] if first else dst
        return remote(src, dst, ssem.at[i * count + n], rsem.at[i * count + n], device)

    def go(i, h, which, device, first=False):
        for n in range(count):
            c = copy(n, i, h, which, device, first)
            c.start()
            sent.append(c)

    def wait(i, h, which, device):
        for n in range(count):
            copy(n, i, h, which, device).wait_recv()

    locals_ = [
        pltpu.make_async_copy(own.at[pl.ds(start, rows)], out.at[me_h, pl.ds(start, rows)], lsem.at[n])
        for n, (own, out, start, rows) in enumerate(pieces)
    ]
    for c in locals_:
        c.start()
    go(0, me_h, 0, partner, True)
    go(1, me_h, 0, right, True)
    go(2, me_h, 0, left, True)
    yield
    wait(0, flip, 0, partner)
    go(3, flip, 0, right)
    go(4, flip, 0, left)
    yield
    wait(1, hl, 0, right)
    go(5, hl, 1, right)
    wait(2, hr, 0, left)
    go(6, hr, 2, left)
    yield
    wait(3, flipped(hl), 0, right)
    go(7, flipped(hl), 1, right)
    wait(4, flipped(hr), 0, left)
    go(8, flipped(hr), 2, left)
    yield
    wait(5, far, 1, right)
    wait(6, far, 2, left)
    wait(7, flipped(far), 1, right)
    wait(8, flipped(far), 2, left)
    for c in locals_:
        c.wait()
    for c in sent:
        c.wait_send()


def finish(*stages):
    left = list(stages)
    while left:
        for g in list(left):
            if next(g, 0) == 0:
                left.remove(g)


def iota(shape, dim):
    return lax.broadcasted_iota(jnp.int32, shape, dim)


def plan(sel, req_ref, tab_ref):
    hi = lax.shift_right_logical(sel, 7)
    lo = lax.bitwise_and(sel, 127)
    rows = sel.shape[0]
    owner_hot = jnp.concatenate(
        [jnp.where(iota((NC, 128), 0) == hi[i : i + 1, :], 1.0, 0.0) for i in range(rows)], axis=1
    ).astype(jnp.bfloat16)
    local_hot = jnp.concatenate(
        [jnp.where(iota((128, 128), 0) == lo[i : i + 1, :], 1.0, 0.0) for i in range(rows)], axis=1
    ).astype(jnp.bfloat16)
    counts = lax.dot_general(
        owner_hot, local_hot, (((1,), (1,)), ((), ())), preferred_element_type=jnp.float32
    )
    present = jnp.where(counts > 0.5, 1.0, 0.0)
    upper = jnp.where(iota((128, 128), 0) <= iota((128, 128), 1), 1.0, 0.0).astype(jnp.bfloat16)
    rank = jnp.dot(present.astype(jnp.bfloat16), upper, preferred_element_type=jnp.float32)
    total = rank[:, 127:128]
    lane = iota((NC, 128), 1)
    sub = iota((NC, 128), 0)
    spread = jnp.sum(jnp.where(lane == sub, total, 0.0), axis=0, keepdims=True)
    before = jnp.sum(jnp.where(lane < sub, jnp.broadcast_to(spread, (NC, 128)), 0.0), axis=1, keepdims=True)
    pos = (before + rank - 1.0).astype(jnp.int32)
    slot = lax.bitwise_and(pos, 7)
    step = lax.shift_right_logical(pos, 3).astype(jnp.float32)
    lane_f = lane.astype(jnp.float32)
    there = present > 0.5
    req = jnp.zeros((NC, 128), jnp.float32)
    ids = jnp.zeros((NC, 128), jnp.float32)
    owners = jnp.zeros((NC, 128), jnp.float32)
    sub_f = sub.astype(jnp.float32)
    for k in range(NH):
        hit = there & (slot == k)
        local = jnp.sum(jnp.where(hit, lane_f, 0.0), axis=1, keepdims=True)
        at = jnp.sum(jnp.where(hit, step, 0.0), axis=1, keepdims=True)
        has = jnp.sum(jnp.where(hit, 1.0, 0.0), axis=1, keepdims=True)
        req = jnp.where(lane == k, local, req)
        here = jnp.where(lane_f == at + float(SETB * k), has, 0.0)
        ids = ids + here * (sub_f * 128.0 + local)
        owners = owners + here * sub_f
        back = jnp.where(has > 0.5, at, float(SETB))
        row = jnp.sum(jnp.where(lane == sub, back, 0.0), axis=0, keepdims=True)
        tab_ref[8 + k : 9 + k, :] = row.astype(jnp.int32)
    tab_ref[0:1, :] = jnp.sum(ids, axis=0, keepdims=True).astype(jnp.int32)
    tab_ref[1:2, :] = jnp.sum(owners, axis=0, keepdims=True).astype(jnp.int32)
    tab_ref[2:8, :] = jnp.zeros((6, 128), jnp.int32)
    req_ref[...] = jnp.broadcast_to(req.astype(jnp.int32)[:, None, :], (NC, 8, 128))


def plan_kernel(sel_ref, req_ref, tab_ref):
    plan(sel_ref[...], req_ref, tab_ref)


def make_plan(sel_t):
    vm_spec = pl.BlockSpec(memory_space=VM)
    return pl.pallas_call(
        plan_kernel,
        name="plan",
        out_shape=(
            jax.ShapeDtypeStruct((NC, 8, 128), jnp.int32),
            jax.ShapeDtypeStruct((16, 128), jnp.int32),
        ),
        in_specs=[vm_spec],
        out_specs=(vm_spec, vm_spec),
        compiler_params=pltpu.CompilerParams(vmem_limit_bytes=60 << 20),
    )(sel_t)


SPLIT = HALF // 2


def fetch_kernel(
    tab_s, req, lat_hbm, ik_hbm, mq_hbm, iq_hbm, w_hbm,
    kt_out, ik_out, mq_out, iq_out, w_out, asked_out,
    lat_v, ik_v, stage, recv_a, recv_b, own, own_ik, asked, asked_s,
    q_send, q_recv, i_send, i_recv, w_send, w_recv, r_send, r_recv, b_send, b_recv, c_send, c_recv,
    g_send, g_recv, h_send, h_recv, loc, loc_a, loc_b, l_sem,
):
    me_h = lax.axis_index("head")
    me_c = lax.axis_index("ctx")
    loads = [pltpu.make_async_copy(ik_hbm, ik_v, loc.at[1])] + [
        pltpu.make_async_copy(lat_hbm.at[:, pl.ds(i * 128, 128)], lat_v.at[i], l_sem.at[i])
        for i in range(lat_v.shape[0])
    ]
    for c in loads:
        c.start()
    my_q = pl.ds(pl.multiple_of(me_h * QROWS, QROWS), QROWS)
    own_copies = [
        pltpu.make_async_copy(mq_hbm.at[my_q], mq_out.at[me_h], loc.at[2]),
        pltpu.make_async_copy(iq_hbm.at[my_q], iq_out.at[me_h], loc.at[3]),
        pltpu.make_async_copy(w_hbm, w_out.at[me_h], loc.at[4]),
    ]
    for c in own_copies:
        c.start()
    start_barrier(me_h, me_c)
    sends = []
    own_req = pltpu.make_async_copy(req.at[me_c], asked.at[me_c], loc.at[6])
    own_req.start()
    for o in range(1, NC):
        c = lax.rem(me_c + o, NC)
        s = remote(req.at[c], asked.at[me_c], r_send.at[o], r_recv.at[o], (me_h, c))
        s.start()
        sends.append(s)

    def send_queries(o):
        h = lax.rem(me_h + o, NH)
        rows = pl.ds(pl.multiple_of(h * QROWS, QROWS), QROWS)
        for src, dst, ss, rs in (
            (mq_hbm.at[rows], mq_out, q_send, q_recv),
            (iq_hbm.at[rows], iq_out, i_send, i_recv),
            (w_hbm, w_out, w_send, w_recv),
        ):
            s = remote(src, dst.at[me_h], ss.at[o], rs.at[o], (h, me_c))
            s.start()
            sends.append(s)

    for o in (2, 6, 4):
        send_queries(o)
    own_req.wait()
    for o in range(1, NC):
        c = lax.rem(me_c + NC - o, NC)
        remote(req.at[c], asked.at[c], r_send.at[o], r_recv.at[o], (me_h, c)).wait_recv()
    asked_out[...] = asked[:, 0, :]
    asked_copy = pltpu.make_async_copy(asked_out, asked_s, loc.at[7])
    asked_copy.start()
    for c in loads:
        c.wait()
    asked_copy.wait()
    first = iota((HALF, 128), 1) < 64
    lower = pl.ds(0, SPLIT)
    upper = pl.ds(SPLIT, SLOT - SPLIT)
    late = []
    for o in range(1, NC + 1):
        r = lax.rem(me_c + o, NC)
        b = asked_s[r, me_h]
        odd = jnp.full((HALF, 128), lax.bitwise_and(b, 1), jnp.int32) == 1
        pair = lax.shift_right_logical(b, 1)
        top = lat_v[pair, 0:HALF, :].astype(jnp.float32)
        bot = lat_v[pair, HALF:LAT, :].astype(jnp.float32)
        packed = jnp.where(
            first, jnp.where(odd, roll64(top), top), jnp.where(odd, bot, roll64(bot))
        ).astype(jnp.bfloat16)
        keys = ik_v[b]
        if o < NC:
            stage[o, 0:HALF, :] = packed
            stage[o, HALF:SLOT, :] = keys
            s = remote(stage.at[o, lower], recv_a.at[me_c], b_send.at[o], b_recv.at[o], (me_h, r))
            s.start()
            sends.append(s)
            late.append(remote(stage.at[o, upper], recv_b.at[me_c], c_send.at[o], c_recv.at[o], (me_h, r)))
        else:
            recv_a[me_c] = packed[0:SPLIT]
            recv_b[me_c, 0 : HALF - SPLIT, :] = packed[SPLIT:HALF]
            recv_b[me_c, HALF - SPLIT : SLOT - SPLIT, :] = keys
    for s in late:
        s.start()
        sends.append(s)
    owners = [tab_s[1, me_h * SETB + j] for j in range(SETB)]

    def merge(lo, hi, recv):
        here = iota((hi - lo, 128), 1) < 64
        for i in range(SETB // 2):
            cols = slice(i * 128, (i + 1) * 128)
            a = recv[owners[2 * i], 0 : hi - lo, :].astype(jnp.float32)
            b = recv[owners[2 * i + 1], 0 : hi - lo, :].astype(jnp.float32)
            own[lo:hi, cols] = jnp.where(here, a, roll64(b)).astype(jnp.bfloat16)
            own[HALF + lo : HALF + hi, cols] = jnp.where(here, roll64(a), b).astype(jnp.bfloat16)

    for o in range(1, NC):
        c = lax.rem(me_c + NC - o, NC)
        remote(stage.at[o, lower], recv_a.at[c], b_send.at[o], b_recv.at[o], (me_h, c)).wait_recv()
    merge(0, SPLIT, recv_a)
    ga = gather_sets(
        [(own, kt_out, 0, SPLIT), (own, kt_out, HALF, SPLIT)], me_h, me_c, g_send, g_recv, loc_a
    )
    next(ga)
    for o in range(1, NC):
        c = lax.rem(me_c + NC - o, NC)
        remote(stage.at[o, upper], recv_b.at[c], c_send.at[o], c_recv.at[o], (me_h, c)).wait_recv()
    merge(SPLIT, HALF, recv_b)
    for j in range(SETB):
        own_ik[j * BLK : (j + 1) * BLK, :] = recv_b[owners[j], HALF - SPLIT : SLOT - SPLIT, :]
    gb = gather_sets(
        [(own, kt_out, SPLIT, HALF - SPLIT), (own, kt_out, HALF + SPLIT, HALF - SPLIT), (own_ik, ik_out, 0, SETT)],
        me_h, me_c, h_send, h_recv, loc_b,
    )
    next(gb)
    for o in (1, 7, 3, 5):
        send_queries(o)
    finish(ga, gb)
    for o in range(1, NH):
        h = lax.rem(me_h + NH - o, NH)
        rows = pl.ds(0, QROWS)
        remote(mq_hbm.at[rows], mq_out.at[h], q_send.at[o], q_recv.at[o], (h, me_c)).wait_recv()
        remote(iq_hbm.at[rows], iq_out.at[h], i_send.at[o], i_recv.at[o], (h, me_c)).wait_recv()
        remote(w_hbm, w_out.at[h], w_send.at[o], w_recv.at[o], (h, me_c)).wait_recv()
    for c in own_copies:
        c.wait()
    for s in sends:
        s.wait_send()


def fetch(tab, req, lat_t, index_key, main_query, index_query, weight_t):
    any_spec = pl.BlockSpec(memory_space=ANY)
    vm_spec = pl.BlockSpec(memory_space=VM)
    bf, i32 = jnp.bfloat16, jnp.int32
    return pl.pallas_call(
        fetch_kernel,
        name="fetch",
        out_shape=(
            jax.ShapeDtypeStruct((NH, LAT, SETT), bf),
            jax.ShapeDtypeStruct((NH, SETT, 128), bf),
            jax.ShapeDtypeStruct((NH, QROWS, main_query.shape[1]), bf),
            jax.ShapeDtypeStruct((NH, QROWS, index_query.shape[1]), bf),
            jax.ShapeDtypeStruct((NH, 8, 128), jnp.float32),
            jax.ShapeDtypeStruct((16, 128), i32),
        ),
        in_specs=[pl.BlockSpec(memory_space=pltpu.SMEM), vm_spec] + [any_spec] * 5,
        out_specs=(any_spec,) * 5 + (vm_spec,),
        scratch_shapes=[
            VM((lat_t.shape[1] // 128, LAT, 128), bf),
            VM(index_key.shape, bf),
            VM((NC, SLOT, 128), bf),
            VM((NC, SPLIT, 128), bf),
            VM((NC, SLOT - SPLIT, 128), bf),
            VM((LAT, SETT), bf),
            VM((SETT, 128), bf),
            VM((NC, 8, 128), i32),
            pltpu.SMEM((16, 128), i32),
            DMA((NH,)), DMA((NH,)), DMA((NH,)), DMA((NH,)), DMA((NH,)), DMA((NH,)),
            DMA((NC,)), DMA((NC,)), DMA((NC,)), DMA((NC,)), DMA((NC,)), DMA((NC,)),
            DMA((18,)), DMA((18,)), DMA((27,)), DMA((27,)), DMA((9,)), DMA((3,)), DMA((3,)),
            DMA((lat_t.shape[1] // 128,)),
        ],
        compiler_params=pltpu.CompilerParams(
            collective_id=0, has_side_effects=True, vmem_limit_bytes=60 << 20
        ),
    )(tab, req, lat_t, index_key, main_query, index_query, weight_t)


AUG = LAT + QROWS
TILE = 256


def core_kernel(
    tab_s, kt_hbm, ik_hbm, mq_ref, iq_ref, w_ref, sel_ref, len_ref, cot_ref,
    ug_ref, iqg_ref, wg_ref,
    kt_ref, ik_ref, sa_ref, sb_ref, ma_ref, mb_ref, qt_ref, pre_ref, ea_ref, eb_ref, bias_ref, tgt_ref, idx_ref,
    grad_ref, meta_ref, wq_ref, selb_ref, wb_ref, iqr_ref, wcol_ref, iqg_acc, sem_k, sem_i,
):
    me = lax.axis_index("head")
    mine = pl.ds(pl.multiple_of(me * QROWS, QROWS), QROWS)
    f32, bf = jnp.float32, jnp.bfloat16
    i_loads, k_loads = [], []
    for h in range(NH):
        i_loads.append(pltpu.make_async_copy(ik_hbm.at[h], ik_ref.at[pl.ds(h * SETT, SETT)], sem_i.at[h]))
        k_loads.append(
            pltpu.make_async_copy(
                kt_hbm.at[h], kt_ref.at[pl.ds(0, LAT), pl.ds(h * SETT, SETT)], sem_k.at[h]
            )
        )
    for c in i_loads + k_loads:
        c.start()
    top = sel_ref.shape[0]
    meta_ref[...] = jnp.zeros((128, 128), f32)
    meta_ref[0:top, :] = sel_ref[...].astype(f32)
    meta_ref[top : top + 1, :] = len_ref[...].astype(f32)
    meta_ref[top + 1 : top + 2, :] = cot_ref[...]
    meta_ref[64 : 64 + IHEADS, :] = w_ref[...].reshape(IHEADS, 128)
    meta_ref[...] = meta_ref[...].T
    row = meta_ref[mine, :]
    for i in range(top):
        selb_ref[i] = jnp.broadcast_to(row[:, i : i + 1], (QROWS, 128))
    limit = jnp.broadcast_to(row[:, top : top + 1], (QROWS, 128))
    cot = row[:, top + 1 : top + 2]
    for j in range(IHEADS):
        wb_ref[j] = jnp.broadcast_to(row[:, 64 + j : 65 + j], (QROWS, 128))
    lane = iota((QROWS, 128), 1)

    def mask_tile(i, carry):
        block = jnp.where(lane < 64, tab_s[0, 2 * i], tab_s[0, 2 * i + 1])
        block_f = block.astype(f32)
        hit = selb_ref[0] == block_f
        for q in range(1, top):
            hit = hit | (selb_ref[q] == block_f)
        token = (block * BLK + lax.bitwise_and(lane, 63)).astype(f32)
        ok = hit & (token < limit)
        cols = pl.ds(pl.multiple_of(i * 128, 128), 128)
        off = jnp.where(ok, 0.0, HIDDEN)
        bias_ref[:, cols] = off
        kt_ref[LAT:AUG, cols] = off.astype(bf)
        return carry

    lax.fori_loop(0, UNION // 128, mask_tile, 0)

    for h in range(NH):
        for k in range(8):
            iqr_ref[(h * 8 + k) * QROWS : (h * 8 + k + 1) * QROWS, :] = iq_ref[h, :, k * 128 : (k + 1) * 128]
    for c in i_loads:
        c.wait()

    def index_chunk(i, carry):
        cols = pl.ds(pl.multiple_of(i * SETT, SETT), SETT)
        acc = jnp.zeros((QROWS, SETT), f32)
        for b in range(4):
            rows = slice(b * 256, (b + 1) * 256)
            pre = lax.dot_general(
                iqr_ref[rows, :], ik_ref[cols, :], (((1,), (1,)), ((), ())), preferred_element_type=f32
            )
            pre_ref[rows, cols] = pre
            for j in range(16):
                w = jnp.concatenate([wb_ref[b * 16 + j]] * (SETT // 128), axis=1)
                acc = acc + w * jnp.maximum(pre[j * QROWS : (j + 1) * QROWS, :], 0.0)
        idx_ref[:, cols] = acc + bias_ref[:, cols]
        return carry

    lax.fori_loop(0, NH, index_chunk, 0)

    tgt_ref[...] = jnp.zeros((QROWS, UNION), f32)
    per = mq_ref.shape[2] // LAT
    hot = jnp.where(iota((QROWS, QROWS), 0) == iota((QROWS, QROWS), 1), 1.0, 0.0).astype(bf)
    for k in range(per):
        qt_ref[k * QROWS : (k + 1) * QROWS, LAT:AUG] = hot
    for c in k_loads:
        c.wait()

    def load_queries(g):
        for k in range(per):
            qt_ref[k * QROWS : (k + 1) * QROWS, 0:LAT] = mq_ref[g, :, k * LAT : (k + 1) * LAT]

    def score_tile(t, s_ref, m_ref):
        cols = slice(t * TILE, (t + 1) * TILE)
        s = jnp.dot(qt_ref[...], kt_ref[:, cols], preferred_element_type=f32)
        s_ref[:, cols] = s
        m = jnp.maximum(s[:, 0:128], s[:, 128:256])
        m_ref[...] = m if t == 0 else jnp.maximum(m_ref[...], m)

    def soften(k, s_ref, m_ref):
        rows = slice(k * QROWS, (k + 1) * QROWS)
        high = jnp.max(m_ref[rows, :], axis=1, keepdims=True) * scale2
        high = jnp.broadcast_to(high, (QROWS, 128))
        den = jnp.zeros((QROWS, 128), f32)
        for t in range(UNION // 128):
            cols = slice(t * 128, (t + 1) * 128)
            p = jnp.exp2(s_ref[rows, cols] * scale2 - high)
            s_ref[rows, cols] = p
            den = den + p
        return jnp.broadcast_to(1.0 / jnp.sum(den, axis=1, keepdims=True), (QROWS, 128))

    def add_up(recips, s_ref, lo):
        for t in range(UNION // 128):
            cols = slice(t * 128, (t + 1) * 128)
            acc = tgt_ref[:, cols]
            for q, r in enumerate(recips):
                acc = acc + s_ref[(lo + q) * QROWS : (lo + q + 1) * QROWS, cols] * r
            tgt_ref[:, cols] = acc

    def both(s_ref, m_ref, next_s, next_m):
        recips = []
        for k in range(per):
            recips.append(soften(k, s_ref, m_ref))
            if next_s is not None:
                score_tile(k, next_s, next_m)
            if k % 8 == 7:
                add_up(recips, s_ref, k - 7)
                recips = []

    load_queries(0)
    for t in range(UNION // TILE):
        score_tile(t, sa_ref, ma_ref)

    def two_groups(i, carry):
        load_queries(2 * i + 1)
        both(sa_ref, ma_ref, sb_ref, mb_ref)
        load_queries(2 * i + 2)
        both(sb_ref, mb_ref, sa_ref, ma_ref)
        return carry

    lax.fori_loop(0, NH // 2 - 1, two_groups, 0)
    load_queries(NH - 1)
    both(sa_ref, ma_ref, sb_ref, mb_ref)
    both(sb_ref, mb_ref, None, None)

    v = idx_ref[...]
    e = jnp.exp(v - jnp.max(v, axis=1, keepdims=True))
    chosen = e / jnp.sum(e, axis=1, keepdims=True)
    grad_ref[...] = cot * (chosen - tgt_ref[...] * (1.0 / HEADS))

    wcol_ref[...] = jnp.zeros(wcol_ref.shape, f32)
    iqg_acc[...] = jnp.zeros(iqg_acc.shape, f32)
    iq_t = iqr_ref[...].T

    def edges(h, e_ref):
        cols = pl.ds(pl.multiple_of(h * SETT, SETT), SETT)
        grad = grad_ref[:, cols]
        for j in range(IHEADS):
            rows = slice(j * QROWS, (j + 1) * QROWS)
            pre = pre_ref[rows, cols]
            w = jnp.concatenate([wb_ref[j]] * (SETT // 128), axis=1)
            part = jnp.maximum(pre, 0.0) * grad
            wcol_ref[j] = wcol_ref[j] + sum(part[:, t * 128 : (t + 1) * 128] for t in range(SETT // 128))
            e_ref[rows, :] = jnp.where(pre > 0.0, grad * w, 0.0).astype(bf)

    def products(h, e_ref):
        part = jnp.dot(iq_t, e_ref[...], preferred_element_type=f32).T.reshape(SETB, 2, BLK // 2, 128)
        for q in range(2):
            ug_ref[q, h] = part[:, q].reshape(SETT // 2, 128)
        keys = ik_ref[pl.ds(pl.multiple_of(h * SETT, SETT), SETT), :]
        for b in range(4):
            rows = slice(b * 256, (b + 1) * 256)
            iqg_acc[rows, :] = iqg_acc[rows, :] + jnp.dot(e_ref[rows, :], keys, preferred_element_type=f32)

    edges(0, ea_ref)

    def two_sets(i, carry):
        edges(2 * i + 1, eb_ref)
        products(2 * i, ea_ref)
        edges(2 * i + 2, ea_ref)
        products(2 * i + 1, eb_ref)
        return carry

    lax.fori_loop(0, NH // 2 - 1, two_sets, 0)
    edges(NH - 1, eb_ref)
    products(NH - 2, ea_ref)
    products(NH - 1, eb_ref)
    wrow = jnp.zeros((QROWS, 128), f32)
    for j in range(IHEADS):
        wrow = jnp.where(lane == j, jnp.sum(wcol_ref[j], axis=1, keepdims=True), wrow)
    wq_ref[...] = jnp.zeros((128, 128), f32)
    wq_ref[mine, :] = wrow
    wg_ref[...] = wq_ref[...].T[0:IHEADS, :].reshape(NH, 8, 128)
    for g in range(NH):
        for k in range(8):
            j = g * 8 + k
            iqg_ref[g, :, k * 128 : (k + 1) * 128] = iqg_acc[j * QROWS : (j + 1) * QROWS, :]


def core(tab, kt, ik, mq, iq, w, sel_t, lengths, cot):
    f32, bf = jnp.float32, jnp.bfloat16
    vm_spec = pl.BlockSpec(memory_space=VM)
    rows = IHEADS * QROWS
    return pl.pallas_call(
        core_kernel,
        name="core",
        out_shape=(
            jax.ShapeDtypeStruct((2, NH, SETT // 2, 128), f32),
            jax.ShapeDtypeStruct((NH, QROWS, 1024), f32),
            jax.ShapeDtypeStruct((NH, 8, 128), f32),
        ),
        in_specs=[pl.BlockSpec(memory_space=pltpu.SMEM), pl.BlockSpec(memory_space=ANY), pl.BlockSpec(memory_space=ANY)]
        + [vm_spec] * 6,
        out_specs=(vm_spec,) * 3,
        scratch_shapes=[
            VM((AUG, UNION), bf),
            VM((UNION, 128), bf),
            VM((256, UNION), f32),
            VM((256, UNION), f32),
            VM((256, 128), f32),
            VM((256, 128), f32),
            VM((256, AUG), bf),
            VM((rows, UNION), f32),
            VM((rows, SETT), bf),
            VM((rows, SETT), bf),
            VM((QROWS, UNION), f32),
            VM((QROWS, UNION), f32),
            VM((QROWS, UNION), f32),
            VM((QROWS, UNION), f32),
            VM((128, 128), f32),
            VM((128, 128), f32),
            VM((32, QROWS, 128), f32),
            VM((IHEADS, QROWS, 128), f32),
            VM((rows, 128), bf),
            VM((IHEADS, QROWS, 128), f32),
            VM((rows, 128), f32),
            DMA((NH,)),
            DMA((NH,)),
        ],
        compiler_params=pltpu.CompilerParams(vmem_limit_bytes=60 << 20),
    )(tab, kt, ik, mq, iq, w, sel_t, lengths, cot)


HB = BLK // 2


def return_kernel(
    tab_s, ug_hbm, iqg_hbm, wg_hbm,
    iqg_out, wg_out, kg_out,
    urecv, sums, slots, brecv, own, wrecv,
    u_send, u_recv, i_send, i_recv, w_send, w_recv, b_send, b_recv, g_send, g_recv, h_send, h_recv, loc, loc_a, loc_b,
):
    me_h = lax.axis_index("head")
    me_c = lax.axis_index("ctx")
    my_q = pl.ds(pl.multiple_of(me_h * QROWS, QROWS), QROWS)
    own_copies = [
        pltpu.make_async_copy(ug_hbm.at[0, me_h], urecv.at[0, me_h], loc.at[0]),
        pltpu.make_async_copy(ug_hbm.at[1, me_h], urecv.at[1, me_h], loc.at[1]),
        pltpu.make_async_copy(iqg_hbm.at[me_h], iqg_out.at[my_q], loc.at[2]),
        pltpu.make_async_copy(wg_hbm.at[me_h], wrecv.at[me_h], loc.at[3]),
    ]
    for c in own_copies:
        c.start()
    start_barrier(me_h, me_c)
    sends = []

    def send_sums(q):
        for o in (1, 7, 3, 5, 2, 6, 4):
            h = lax.rem(me_h + o, NH)
            s = remote(
                ug_hbm.at[q, h], urecv.at[q, me_h], u_send.at[q * NH + o], u_recv.at[q * NH + o], (h, me_c)
            )
            s.start()
            sends.append(s)

    def take_sums(q):
        own_copies[q].wait()
        for o in range(1, NH):
            h = lax.rem(me_h + NH - o, NH)
            remote(
                ug_hbm.at[q, h], urecv.at[q, h], u_send.at[q * NH + o], u_recv.at[q * NH + o], (h, me_c)
            ).wait_recv()

    def send_blocks(q):
        for j in range(SETB):
            rows = slice(j * HB, (j + 1) * HB)
            acc = urecv[q, 0, rows, :]
            for h in range(1, NH):
                acc = acc + urecv[q, h, rows, :]
            sums[q, j] = acc
        sums[q, SETB] = jnp.zeros((HB, 128), jnp.float32)
        for o in range(1, NC + 1):
            c = lax.rem(me_c + o, NC)
            value = sums[q, tab_s[8 + me_h, c]]
            if o < NC:
                slots[q, o] = value
                s = remote(
                    slots.at[q, o], brecv.at[q, me_c], b_send.at[q * NC + o], b_recv.at[q * NC + o], (me_h, c)
                )
                s.start()
                sends.append(s)
            else:
                brecv[q, me_c] = value

    def take_blocks(q):
        for o in range(1, NC):
            c = lax.rem(me_c + NC - o, NC)
            remote(
                slots.at[q, o], brecv.at[q, c], b_send.at[q * NC + o], b_recv.at[q * NC + o], (me_h, c)
            ).wait_recv()
        for r in range(NC):
            at = (q * NC + r) * HB
            own[at : at + HB, :] = brecv[q, r].astype(own.dtype)

    rows = NC * HB
    send_sums(0)
    take_sums(0)
    send_sums(1)
    send_blocks(0)
    take_blocks(0)
    ga = gather_sets([(own, kg_out, 0, rows)], me_h, me_c, g_send, g_recv, loc_a)
    next(ga)
    take_sums(1)
    send_blocks(1)
    for o in range(1, NH):
        h = lax.rem(me_h + o, NH)
        s = remote(iqg_hbm.at[h], iqg_out.at[my_q], i_send.at[o], i_recv.at[o], (h, me_c))
        s.start()
        sends.append(s)
        s = remote(wg_hbm.at[h], wrecv.at[me_h], w_send.at[o], w_recv.at[o], (h, me_c))
        s.start()
        sends.append(s)
    next(ga)
    take_blocks(1)
    gb = gather_sets([(own, kg_out, rows, rows)], me_h, me_c, h_send, h_recv, loc_b)
    next(gb)
    finish(ga, gb)
    for o in range(1, NH):
        h = lax.rem(me_h + NH - o, NH)
        remote(
            iqg_hbm.at[h], iqg_out.at[pl.ds(pl.multiple_of(h * QROWS, QROWS), QROWS)],
            i_send.at[o], i_recv.at[o], (h, me_c),
        ).wait_recv()
        remote(wg_hbm.at[h], wrecv.at[h], w_send.at[o], w_recv.at[o], (h, me_c)).wait_recv()
    own_copies[2].wait()
    own_copies[3].wait()
    acc = wrecv[0]
    for h in range(1, NH):
        acc = acc + wrecv[h]
    wg_out[...] = acc
    for s in sends:
        s.wait_send()


SENT = jnp.bfloat16


def give_back(tab, ug, iqg, wg):
    f32 = jnp.float32
    any_spec = pl.BlockSpec(memory_space=ANY)
    return pl.pallas_call(
        return_kernel,
        name="give_back",
        out_shape=(
            jax.ShapeDtypeStruct((NH * QROWS, 1024), f32),
            jax.ShapeDtypeStruct((8, 128), f32),
            jax.ShapeDtypeStruct((NH, NC * BLK, 128), SENT),
        ),
        in_specs=[pl.BlockSpec(memory_space=pltpu.SMEM)] + [any_spec] * 3,
        out_specs=(any_spec, pl.BlockSpec(memory_space=VM), any_spec),
        scratch_shapes=[
            VM((2, NH, SETT // 2, 128), f32),
            VM((2, SETB + 1, HB, 128), f32),
            VM((2, NC, HB, 128), f32),
            VM((2, NC, HB, 128), f32),
            VM((NC * BLK, 128), SENT),
            VM((NH, 8, 128), f32),
            DMA((2 * NH,)), DMA((2 * NH,)), DMA((NH,)), DMA((NH,)), DMA((NH,)), DMA((NH,)),
            DMA((2 * NC,)), DMA((2 * NC,)),
            DMA((9,)), DMA((9,)), DMA((9,)), DMA((9,)), DMA((4,)), DMA((1,)), DMA((1,)),
        ],
        compiler_params=pltpu.CompilerParams(
            collective_id=1, has_side_effects=True, vmem_limit_bytes=60 << 20
        ),
    )(tab, ug, iqg, wg)


def scatter_kernel(asked_s, kg_ref, out_ref):
    out_ref[...] = jnp.zeros(out_ref.shape, jnp.float32)

    def one(i, carry):
        h = lax.shift_right_logical(i, 4)
        r = lax.bitwise_and(i, 15)
        b = asked_s[r, h]
        for q in range(2):
            rows = pl.ds(pl.multiple_of(b * BLK + q * HB, HB), HB)
            part = kg_ref[h, pl.ds(pl.multiple_of((q * NC + r) * HB, HB), HB), :]
            out_ref[rows, :] = out_ref[rows, :] + part.astype(jnp.float32)
        return carry

    lax.fori_loop(0, NH * NC, one, 0)


def scatter(asked, kg, tokens):
    return pl.pallas_call(
        scatter_kernel,
        name="scatter",
        out_shape=jax.ShapeDtypeStruct((tokens, 128), jnp.float32),
        in_specs=[pl.BlockSpec(memory_space=pltpu.SMEM), pl.BlockSpec(memory_space=VM)],
        out_specs=pl.BlockSpec(memory_space=VM),
        compiler_params=pltpu.CompilerParams(vmem_limit_bytes=60 << 20),
    )(asked, kg)


def shards(main_query, latent, index_query, index_key, index_weight, selected, lengths, cotangent):
    sel_t = selected.T
    req, tab = make_plan(sel_t)
    kt, ik, mq, iq, w, asked = fetch(
        tab, req, latent.T, index_key.reshape(-1, BLK, WIDTH), main_query, index_query, index_weight.T
    )
    ug, iqg, wg = core(tab, kt, ik, mq, iq, w, sel_t, lengths[None, :], cotangent[None, :])
    query_grad, weight_grad, kg = give_back(tab, ug, iqg, wg)
    key_grad = scatter(asked, kg, latent.shape[0])
    return query_grad, weight_grad.T, key_grad


def solution(mesh):
    return jax.shard_map(
        shards,
        mesh=mesh,
        in_specs=(
            P("ctx", "head"),
            P("ctx", None),
            P("ctx", "head"),
            P("ctx", None),
            P("ctx", "head"),
            P("ctx", None),
            P("ctx"),
            P("ctx"),
        ),
        out_specs=(P("ctx", "head"), P("ctx", "head"), P("ctx", None)),
        check_vma=False,
    )
```

```python
import functools
import math

import jax
import jax.numpy as jnp
from jax import lax
from jax.experimental import pallas as pl
from jax.experimental.pallas import tpu as pltpu
from jax.sharding import PartitionSpec as P

HEADS = 128
BLK = 64
POOL = 64
NH = 8
NC = 16
LAT = 576
WIDTH = 128
QROWS = 16
SETB = POOL // NH
SETT = SETB * BLK
HALF = LAT // 2
SLOT = HALF + BLK
UNION = POOL * BLK
IHEADS = 64

MESH = pl.DeviceIdType.MESH
ANY = pltpu.HBM
VM = pltpu.VMEM
DMA = pltpu.SemaphoreType.DMA

HIDDEN = -1e30
scale2 = 192.0 ** (-0.5) * math.log2(math.e)


def roll64(x):
    return pltpu.roll(x, 64, 1)


def start_barrier(me_h, me_c):
    barrier = pltpu.get_barrier_semaphore()
    for o in range(1, NH):
        pl.semaphore_signal(
            barrier, inc=1, device_id=(lax.rem(me_h + o, NH), me_c), device_id_type=MESH
        )
    for o in range(1, NC):
        pl.semaphore_signal(
            barrier, inc=1, device_id=(me_h, lax.rem(me_c + o, NC)), device_id_type=MESH
        )
    pl.semaphore_wait(barrier, NH + NC - 2)


def remote(src, dst, ssem, rsem, device):
    return pltpu.make_async_remote_copy(
        src_ref=src, dst_ref=dst, send_sem=ssem, recv_sem=rsem, device_id=device, device_id_type=MESH
    )


def gather_sets(pieces, me_h, me_c, ssem, rsem, lsem, between=None):
    right = (lax.rem(me_h + 2, NH), me_c)
    left = (lax.rem(me_h + 6, NH), me_c)
    flip = me_h + 1 - 2 * lax.rem(me_h, 2)
    partner = (flip, me_c)
    hl = lax.rem(me_h + 6, NH)
    hr = lax.rem(me_h + 2, NH)
    far = lax.rem(me_h + 4, NH)

    def flipped(h):
        return h + 1 - 2 * lax.rem(h, 2)

    count = len(pieces)
    sent = []

    def part(n, which):
        own, out, start, rows = pieces[n]
        half = rows // 32 * 16
        if which == 0:
            return start, rows
        return (start, half) if which == 1 else (start + half, rows - half)

    def copy(n, i, h, which, device, first=False):
        own, out, _, _ = pieces[n]
        start, rows = part(n, which)
        dst = out(h, start, rows)
        src = own.at[pl.ds(start, rows)] if first else dst
        return remote(src, dst, ssem.at[i * count + n], rsem.at[i * count + n], device)

    def go(i, h, which, device, first=False):
        for n in range(count):
            c = copy(n, i, h, which, device, first)
            c.start()
            sent.append(c)

    def wait(i, h, which, device):
        for n in range(count):
            copy(n, i, h, which, device).wait_recv()

    locals_ = [
        pltpu.make_async_copy(own.at[pl.ds(start, rows)], out(me_h, start, rows), lsem.at[n])
        for n, (own, out, start, rows) in enumerate(pieces)
    ]
    for c in locals_:
        c.start()
    go(0, me_h, 0, partner, True)
    go(1, me_h, 0, right, True)
    go(2, me_h, 0, left, True)
    yield
    wait(0, flip, 0, partner)
    go(3, flip, 0, right)
    go(4, flip, 0, left)
    yield
    wait(1, hl, 0, right)
    go(5, hl, 1, right)
    wait(2, hr, 0, left)
    go(6, hr, 2, left)
    yield
    wait(3, flipped(hl), 0, right)
    go(7, flipped(hl), 1, right)
    wait(4, flipped(hr), 0, left)
    go(8, flipped(hr), 2, left)
    yield
    wait(5, far, 1, right)
    wait(6, far, 2, left)
    wait(7, flipped(far), 1, right)
    wait(8, flipped(far), 2, left)
    for c in locals_:
        c.wait()
    for c in sent:
        c.wait_send()


def finish(*stages):
    left = list(stages)
    while left:
        for g in list(left):
            if next(g, 0) == 0:
                left.remove(g)


def iota(shape, dim):
    return lax.broadcasted_iota(jnp.int32, shape, dim)


def plan(sel, req_ref, tab_ref):
    hi = lax.shift_right_logical(sel, 7)
    lo = lax.bitwise_and(sel, 127)
    rows = sel.shape[0]
    owner_hot = jnp.concatenate(
        [jnp.where(iota((NC, 128), 0) == hi[i : i + 1, :], 1.0, 0.0) for i in range(rows)], axis=1
    ).astype(jnp.bfloat16)
    local_hot = jnp.concatenate(
        [jnp.where(iota((128, 128), 0) == lo[i : i + 1, :], 1.0, 0.0) for i in range(rows)], axis=1
    ).astype(jnp.bfloat16)
    counts = lax.dot_general(
        owner_hot, local_hot, (((1,), (1,)), ((), ())), preferred_element_type=jnp.float32
    )
    present = jnp.where(counts > 0.5, 1.0, 0.0)
    upper = jnp.where(iota((128, 128), 0) <= iota((128, 128), 1), 1.0, 0.0).astype(jnp.bfloat16)
    rank = jnp.dot(present.astype(jnp.bfloat16), upper, preferred_element_type=jnp.float32)
    total = rank[:, 127:128]
    lane = iota((NC, 128), 1)
    sub = iota((NC, 128), 0)
    spread = jnp.sum(jnp.where(lane == sub, total, 0.0), axis=0, keepdims=True)
    before = jnp.sum(jnp.where(lane < sub, jnp.broadcast_to(spread, (NC, 128)), 0.0), axis=1, keepdims=True)
    pos = (before + rank - 1.0).astype(jnp.int32)
    slot = lax.bitwise_and(pos, 7)
    step = lax.shift_right_logical(pos, 3).astype(jnp.float32)
    lane_f = lane.astype(jnp.float32)
    there = present > 0.5
    req = jnp.zeros((NC, 128), jnp.float32)
    ids = jnp.zeros((NC, 128), jnp.float32)
    owners = jnp.zeros((NC, 128), jnp.float32)
    sub_f = sub.astype(jnp.float32)
    for k in range(NH):
        hit = there & (slot == k)
        local = jnp.sum(jnp.where(hit, lane_f, 0.0), axis=1, keepdims=True)
        at = jnp.sum(jnp.where(hit, step, 0.0), axis=1, keepdims=True)
        has = jnp.sum(jnp.where(hit, 1.0, 0.0), axis=1, keepdims=True)
        req = jnp.where(lane == k, local, req)
        here = jnp.where(lane_f == at + float(SETB * k), has, 0.0)
        ids = ids + here * (sub_f * 128.0 + local)
        owners = owners + here * sub_f
        back = jnp.where(has > 0.5, at, float(SETB))
        row = jnp.sum(jnp.where(lane == sub, back, 0.0), axis=0, keepdims=True)
        tab_ref[8 + k : 9 + k, :] = row.astype(jnp.int32)
    tab_ref[0:1, :] = jnp.sum(ids, axis=0, keepdims=True).astype(jnp.int32)
    tab_ref[1:2, :] = jnp.sum(owners, axis=0, keepdims=True).astype(jnp.int32)
    tab_ref[2:8, :] = jnp.zeros((6, 128), jnp.int32)
    req_ref[...] = jnp.broadcast_to(req.astype(jnp.int32)[:, None, :], (NC, 8, 128))


def plan_kernel(sel_ref, req_ref, tab_ref):
    plan(sel_ref[...], req_ref, tab_ref)


def make_plan(sel_t):
    vm_spec = pl.BlockSpec(memory_space=VM)
    return pl.pallas_call(
        plan_kernel,
        name="plan",
        out_shape=(
            jax.ShapeDtypeStruct((NC, 8, 128), jnp.int32),
            jax.ShapeDtypeStruct((16, 128), jnp.int32),
        ),
        in_specs=[vm_spec],
        out_specs=(vm_spec, vm_spec),
        compiler_params=pltpu.CompilerParams(vmem_limit_bytes=60 << 20),
    )(sel_t)


SPLIT = SLOT // 2
FIRST = SPLIT - BLK
AUG = LAT + QROWS
TILE = 256


def forward_kernel(
    tab_s, req, sel_ref, len_ref, cot_ref, lat_hbm, ik_hbm, mq_hbm, iq_hbm, w_hbm,
    grad_ref, iqr_ref, wrow_ref, asked_out, ik_out,
    lat_v, ik_v, stage, recv_a, recv_b, own, own_ik, asked, asked_s,
    kt_ref, ik_ref, mq_ref, iq_ref, w_ref,
    sa_ref, sb_ref, ma_ref, mb_ref, qt_ref, bias_ref, tgt_ref, idx_ref, meta_ref, selb_ref, wb_ref,
    q_send, q_recv, i_send, i_recv, w_send, w_recv, r_send, r_recv, b_send, b_recv, c_send, c_recv,
    g_send, g_recv, h_send, h_recv, loc, loc_a, loc_b, l_sem,
):
    f32, bf = jnp.float32, jnp.bfloat16
    me_h = lax.axis_index("head")
    me_c = lax.axis_index("ctx")
    loads = [pltpu.make_async_copy(ik_hbm, ik_v, loc.at[1])] + [
        pltpu.make_async_copy(lat_hbm.at[:, pl.ds(i * 128, 128)], lat_v.at[i], l_sem.at[i])
        for i in range(lat_v.shape[0])
    ]
    for c in loads:
        c.start()
    mine = pl.ds(pl.multiple_of(me_h * QROWS, QROWS), QROWS)
    own_mq = pltpu.make_async_copy(mq_hbm.at[mine], mq_ref.at[me_h], loc.at[2])
    own_iq = pltpu.make_async_copy(iq_hbm.at[mine], iq_ref.at[me_h], loc.at[3])
    own_w = pltpu.make_async_copy(w_hbm, w_ref.at[me_h], loc.at[4])
    own_mq.start()
    own_iq.start()
    own_w.start()
    start_barrier(me_h, me_c)
    sends = []
    own_req = pltpu.make_async_copy(req.at[me_c], asked.at[me_c], loc.at[6])
    own_req.start()
    for o in range(1, NC):
        c = lax.rem(me_c + o, NC)
        s = remote(req.at[c], asked.at[me_c], r_send.at[o], r_recv.at[o], (me_h, c))
        s.start()
        sends.append(s)

    def query_copy(o, back=False):
        h = lax.rem(me_h + (NH - o if back else o), NH)
        rows = pl.ds(0, QROWS) if back else pl.ds(pl.multiple_of(h * QROWS, QROWS), QROWS)
        return remote(mq_hbm.at[rows], mq_ref.at[h if back else me_h], q_send.at[o], q_recv.at[o], (h, me_c))

    def send_queries(o):
        s = query_copy(o)
        s.start()
        sends.append(s)

    for o in range(1, NH):
        h = lax.rem(me_h + o, NH)
        rows = pl.ds(pl.multiple_of(h * QROWS, QROWS), QROWS)
        for src, dst, ss, rs in ((iq_hbm.at[rows], iq_ref, i_send, i_recv), (w_hbm, w_ref, w_send, w_recv)):
            s = remote(src, dst.at[me_h], ss.at[o], rs.at[o], (h, me_c))
            s.start()
            sends.append(s)
    for o in (2, 6, 4):
        send_queries(o)
    own_req.wait()
    for o in range(1, NC):
        c = lax.rem(me_c + NC - o, NC)
        remote(req.at[c], asked.at[c], r_send.at[o], r_recv.at[o], (me_h, c)).wait_recv()
    asked_out[...] = asked[:, 0, :]
    asked_copy = pltpu.make_async_copy(asked_out, asked_s, loc.at[7])
    asked_copy.start()
    for c in loads:
        c.wait()
    asked_copy.wait()
    first = iota((HALF, 128), 1) < 64
    lower = pl.ds(0, SPLIT)
    upper = pl.ds(SPLIT, SLOT - SPLIT)
    late = []
    for o in range(1, NC + 1):
        r = lax.rem(me_c + o, NC)
        b = asked_s[r, me_h]
        odd = jnp.full((HALF, 128), lax.bitwise_and(b, 1), jnp.int32) == 1
        pair = lax.shift_right_logical(b, 1)
        top = lat_v[pair, 0:HALF, :].astype(f32)
        bot = lat_v[pair, HALF:LAT, :].astype(f32)
        packed = jnp.where(
            first, jnp.where(odd, roll64(top), top), jnp.where(odd, bot, roll64(bot))
        ).astype(bf)
        keys = ik_v[b]
        if o < NC:
            stage[o, 0:BLK, :] = keys
            stage[o, BLK:SLOT, :] = packed
            s = remote(stage.at[o, lower], recv_a.at[me_c], b_send.at[o], b_recv.at[o], (me_h, r))
            s.start()
            sends.append(s)
            late.append(remote(stage.at[o, upper], recv_b.at[me_c], c_send.at[o], c_recv.at[o], (me_h, r)))
        else:
            recv_a[me_c, 0:BLK, :] = keys
            recv_a[me_c, BLK:SPLIT, :] = packed[0:FIRST]
            recv_b[me_c] = packed[FIRST:HALF]
    for s in late:
        s.start()
        sends.append(s)
    owners = [tab_s[1, me_h * SETB + j] for j in range(SETB)]

    own_w.wait()
    own_iq.wait()
    for o in range(1, NH):
        h = lax.rem(me_h + NH - o, NH)
        remote(iq_hbm.at[pl.ds(0, QROWS)], iq_ref.at[h], i_send.at[o], i_recv.at[o], (h, me_c)).wait_recv()
        remote(w_hbm, w_ref.at[h], w_send.at[o], w_recv.at[o], (h, me_c)).wait_recv()
    top = sel_ref.shape[0]
    meta_ref[...] = jnp.zeros((128, 128), f32)
    meta_ref[0:top, :] = sel_ref[...].astype(f32)
    meta_ref[top : top + 1, :] = len_ref[...].astype(f32)
    meta_ref[top + 1 : top + 2, :] = cot_ref[...]
    meta_ref[64 : 64 + IHEADS, :] = w_ref[...].reshape(IHEADS, 128)
    meta_ref[...] = meta_ref[...].T
    row = meta_ref[mine, :]
    wrow_ref[...] = row
    for i in range(top):
        selb_ref[i] = jnp.broadcast_to(row[:, i : i + 1], (QROWS, 128))
    limit = jnp.broadcast_to(row[:, top : top + 1], (QROWS, 128))
    cot = row[:, top + 1 : top + 2]
    for j in range(IHEADS):
        wb_ref[j] = jnp.broadcast_to(row[:, 64 + j : 65 + j], (QROWS, 128))
    lane = iota((QROWS, 128), 1)

    def mask_tile(i, carry):
        block = jnp.where(lane < 64, tab_s[0, 2 * i], tab_s[0, 2 * i + 1])
        block_f = block.astype(f32)
        hit = selb_ref[0] == block_f
        for q in range(1, top):
            hit = hit | (selb_ref[q] == block_f)
        token = (block * BLK + lax.bitwise_and(lane, 63)).astype(f32)
        ok = hit & (token < limit)
        cols = pl.ds(pl.multiple_of(i * 128, 128), 128)
        off = jnp.where(ok, 0.0, HIDDEN)
        bias_ref[:, cols] = off
        kt_ref[LAT:AUG, cols] = off.astype(bf)
        return carry

    lax.fori_loop(0, UNION // 128, mask_tile, 0)
    for h in range(NH):
        for k in range(8):
            iqr_ref[(h * 8 + k) * QROWS : (h * 8 + k + 1) * QROWS, :] = iq_ref[h, :, k * 128 : (k + 1) * 128]
    hot = jnp.where(iota((QROWS, QROWS), 0) == iota((QROWS, QROWS), 1), 1.0, 0.0).astype(bf)
    per = mq_ref.shape[2] // LAT
    for k in range(per):
        qt_ref[k * QROWS : (k + 1) * QROWS, LAT:AUG] = hot

    def merge(recv, skip, lo, hi):
        here = iota((hi - lo, 128), 1) < 64
        for i in range(SETB // 2):
            cols = slice(i * 128, (i + 1) * 128)
            a = recv[owners[2 * i], skip : skip + hi - lo, :].astype(f32)
            b = recv[owners[2 * i + 1], skip : skip + hi - lo, :].astype(f32)
            own[lo:hi, cols] = jnp.where(here, a, roll64(b)).astype(bf)
            own[HALF + lo : HALF + hi, cols] = jnp.where(here, roll64(a), b).astype(bf)

    def kt_of(h, start, rows):
        return kt_ref.at[pl.ds(start, rows), pl.ds(pl.multiple_of(h * SETT, SETT), SETT)]

    def ik_of(h, start, rows):
        return ik_ref.at[h, pl.ds(start, rows)]

    for o in range(1, NC):
        c = lax.rem(me_c + NC - o, NC)
        remote(stage.at[o, lower], recv_a.at[c], b_send.at[o], b_recv.at[o], (me_h, c)).wait_recv()
    merge(recv_a, BLK, 0, FIRST)
    for j in range(SETB):
        own_ik[j * BLK : (j + 1) * BLK, :] = recv_a[owners[j], 0:BLK, :]
    ga = gather_sets(
        [(own_ik, ik_of, 0, SETT), (own, kt_of, 0, FIRST), (own, kt_of, HALF, FIRST)],
        me_h, me_c, g_send, g_recv, loc_a,
    )
    next(ga)
    for o in range(1, NC):
        c = lax.rem(me_c + NC - o, NC)
        remote(stage.at[o, upper], recv_b.at[c], c_send.at[o], c_recv.at[o], (me_h, c)).wait_recv()
    merge(recv_b, 0, FIRST, HALF)
    next(ga)
    gb = gather_sets(
        [(own, kt_of, FIRST, HALF - FIRST), (own, kt_of, HALF + FIRST, HALF - FIRST)],
        me_h, me_c, h_send, h_recv, loc_b,
    )
    next(gb)
    next(ga)
    next(gb)
    next(ga)
    next(gb)
    for o in (1, 7, 3, 5):
        send_queries(o)
    finish(ga)

    def index_chunk(i, carry):
        cols = pl.ds(pl.multiple_of(i * SETT, SETT), SETT)
        acc = jnp.zeros((QROWS, SETT), f32)
        for b in range(4):
            rows = slice(b * 256, (b + 1) * 256)
            pre = lax.dot_general(
                iqr_ref[rows, :], ik_ref[i], (((1,), (1,)), ((), ())), preferred_element_type=f32
            )
            for j in range(16):
                w = jnp.concatenate([wb_ref[b * 16 + j]] * (SETT // 128), axis=1)
                acc = acc + w * jnp.maximum(pre[j * QROWS : (j + 1) * QROWS, :], 0.0)
        idx_ref[:, cols] = acc + bias_ref[:, cols]
        return carry

    lax.fori_loop(0, NH // 2, index_chunk, 0)
    next(gb)
    lax.fori_loop(NH // 2, NH, index_chunk, 0)
    keys_out = pltpu.make_async_copy(ik_ref, ik_out, loc.at[5])
    keys_out.start()
    v = idx_ref[...]
    e = jnp.exp(v - jnp.max(v, axis=1, keepdims=True))
    idx_ref[...] = e / jnp.sum(e, axis=1, keepdims=True)
    tgt_ref[...] = jnp.zeros((QROWS, UNION), f32)
    finish(gb)

    def load_queries(g):
        for k in range(per):
            qt_ref[k * QROWS : (k + 1) * QROWS, 0:LAT] = mq_ref[g, :, k * LAT : (k + 1) * LAT]

    def arrive(n):
        o = lax.rem(2 * n, NH) + lax.div(n, NH // 2)
        query_copy(o, True).wait_recv()
        load_queries(lax.rem(me_h + NH - o, NH))

    def score_tile(t, s_ref, m_ref):
        cols = slice(t * TILE, (t + 1) * TILE)
        s = jnp.dot(qt_ref[...], kt_ref[:, cols], preferred_element_type=f32)
        s_ref[:, cols] = s
        m = jnp.maximum(s[:, 0:128], s[:, 128:256])
        m_ref[...] = m if t == 0 else jnp.maximum(m_ref[...], m)

    def soften(k, s_ref, m_ref):
        rows = slice(k * QROWS, (k + 1) * QROWS)
        high = jnp.max(m_ref[rows, :], axis=1, keepdims=True) * scale2
        high = jnp.broadcast_to(high, (QROWS, 128))
        den = jnp.zeros((QROWS, 128), f32)
        for t in range(UNION // 128):
            cols = slice(t * 128, (t + 1) * 128)
            p = jnp.exp2(s_ref[rows, cols] * scale2 - high)
            s_ref[rows, cols] = p
            den = den + p
        return jnp.broadcast_to(1.0 / jnp.sum(den, axis=1, keepdims=True), (QROWS, 128))

    def add_up(recips, s_ref, lo):
        for t in range(UNION // 128):
            cols = slice(t * 128, (t + 1) * 128)
            acc = tgt_ref[:, cols]
            for q, r in enumerate(recips):
                acc = acc + s_ref[(lo + q) * QROWS : (lo + q + 1) * QROWS, cols] * r
            tgt_ref[:, cols] = acc

    def both(s_ref, m_ref, next_s, next_m):
        recips = []
        for k in range(per):
            recips.append(soften(k, s_ref, m_ref))
            if next_s is not None:
                score_tile(k, next_s, next_m)
            if k % 8 == 7:
                add_up(recips, s_ref, k - 7)
                recips = []

    own_mq.wait()
    load_queries(me_h)
    for t in range(UNION // TILE):
        score_tile(t, sa_ref, ma_ref)

    def two_groups(i, carry):
        arrive(2 * i + 1)
        both(sa_ref, ma_ref, sb_ref, mb_ref)
        arrive(2 * i + 2)
        both(sb_ref, mb_ref, sa_ref, ma_ref)
        return carry

    lax.fori_loop(0, NH // 2 - 1, two_groups, 0)
    arrive(NH - 1)
    both(sa_ref, ma_ref, sb_ref, mb_ref)
    both(sb_ref, mb_ref, None, None)
    grad_ref[...] = cot * (idx_ref[...] - tgt_ref[...] * (1.0 / HEADS))
    keys_out.wait()
    for s in sends:
        s.wait_send()


def forward(tab, req, sel_t, lengths, cot, lat_t, index_key, main_query, index_query, weight_t):
    any_spec = pl.BlockSpec(memory_space=ANY)
    vm_spec = pl.BlockSpec(memory_space=VM)
    f32, bf, i32 = jnp.float32, jnp.bfloat16, jnp.int32
    rows = IHEADS * QROWS
    return pl.pallas_call(
        forward_kernel,
        name="forward",
        out_shape=(
            jax.ShapeDtypeStruct((QROWS, UNION), f32),
            jax.ShapeDtypeStruct((rows, 128), bf),
            jax.ShapeDtypeStruct((QROWS, 128), f32),
            jax.ShapeDtypeStruct((16, 128), i32),
            jax.ShapeDtypeStruct((NH, SETT, 128), bf),
        ),
        in_specs=[pl.BlockSpec(memory_space=pltpu.SMEM)] + [vm_spec] * 4 + [any_spec] * 5,
        out_specs=(vm_spec,) * 4 + (any_spec,),
        scratch_shapes=[
            VM((lat_t.shape[1] // 128, LAT, 128), bf),
            VM(index_key.shape, bf),
            VM((NC, SLOT, 128), bf),
            VM((NC, SPLIT, 128), bf),
            VM((NC, SLOT - SPLIT, 128), bf),
            VM((LAT, SETT), bf),
            VM((SETT, 128), bf),
            VM((NC, 8, 128), i32),
            pltpu.SMEM((16, 128), i32),
            VM((AUG, UNION), bf),
            VM((NH, SETT, 128), bf),
            VM((NH, QROWS, main_query.shape[1]), bf),
            VM((NH, QROWS, index_query.shape[1]), bf),
            VM((NH, 8, 128), f32),
            VM((256, UNION), f32),
            VM((256, UNION), f32),
            VM((256, 128), f32),
            VM((256, 128), f32),
            VM((256, AUG), bf),
            VM((QROWS, UNION), f32),
            VM((QROWS, UNION), f32),
            VM((QROWS, UNION), f32),
            VM((128, 128), f32),
            VM((32, QROWS, 128), f32),
            VM((IHEADS, QROWS, 128), f32),
            DMA((NH,)), DMA((NH,)), DMA((NH,)), DMA((NH,)), DMA((NH,)), DMA((NH,)),
            DMA((NC,)), DMA((NC,)), DMA((NC,)), DMA((NC,)), DMA((NC,)), DMA((NC,)),
            DMA((27,)), DMA((27,)), DMA((18,)), DMA((18,)), DMA((9,)), DMA((3,)), DMA((3,)),
            DMA((lat_t.shape[1] // 128,)),
        ],
        compiler_params=pltpu.CompilerParams(
            collective_id=0, has_side_effects=True, vmem_limit_bytes=60 << 20
        ),
    )(tab, req, sel_t, lengths, cot, lat_t, index_key, main_query, index_query, weight_t)


def back_kernel(
    grad_ref, iqr_ref, row_ref, ik_ref,
    ug_ref, iqg_ref, wg_ref,
    ea_ref, eb_ref, wq_ref, wb_ref, wcol_ref, iqg_acc,
):
    me = lax.axis_index("head")
    mine = pl.ds(pl.multiple_of(me * QROWS, QROWS), QROWS)
    f32, bf = jnp.float32, jnp.bfloat16
    lane = iota((QROWS, 128), 1)
    row = row_ref[...]
    for j in range(IHEADS):
        wb_ref[j] = jnp.broadcast_to(row[:, 64 + j : 65 + j], (QROWS, 128))
    wcol_ref[...] = jnp.zeros(wcol_ref.shape, f32)
    iqg_acc[...] = jnp.zeros(iqg_acc.shape, f32)
    iq_t = iqr_ref[...].T

    def edges(h, e_ref):
        cols = pl.ds(pl.multiple_of(h * SETT, SETT), SETT)
        grad = grad_ref[:, cols]
        for b in range(4):
            pre_b = lax.dot_general(
                iqr_ref[b * 256 : (b + 1) * 256, :], ik_ref[h], (((1,), (1,)), ((), ())), preferred_element_type=f32
            )
            for q in range(16):
                j = b * 16 + q
                pre = pre_b[q * QROWS : (q + 1) * QROWS, :]
                w = jnp.concatenate([wb_ref[j]] * (SETT // 128), axis=1)
                part = jnp.maximum(pre, 0.0) * grad
                wcol_ref[j] = wcol_ref[j] + sum(part[:, t * 128 : (t + 1) * 128] for t in range(SETT // 128))
                e_ref[j * QROWS : (j + 1) * QROWS, :] = jnp.where(pre > 0.0, grad * w, 0.0).astype(bf)

    def products(h, e_ref):
        part = jnp.dot(iq_t, e_ref[...], preferred_element_type=f32).T.reshape(SETB, 2, BLK // 2, 128)
        for q in range(2):
            ug_ref[q, h] = part[:, q].reshape(SETT // 2, 128)
        for b in range(4):
            rows = slice(b * 256, (b + 1) * 256)
            iqg_acc[rows, :] = iqg_acc[rows, :] + jnp.dot(e_ref[rows, :], ik_ref[h], preferred_element_type=f32)

    edges(0, ea_ref)

    def two_sets(i, carry):
        edges(2 * i + 1, eb_ref)
        products(2 * i, ea_ref)
        edges(2 * i + 2, ea_ref)
        products(2 * i + 1, eb_ref)
        return carry

    lax.fori_loop(0, NH // 2 - 1, two_sets, 0)
    edges(NH - 1, eb_ref)
    products(NH - 2, ea_ref)
    products(NH - 1, eb_ref)
    wrow = jnp.zeros((QROWS, 128), f32)
    for j in range(IHEADS):
        wrow = jnp.where(lane == j, jnp.sum(wcol_ref[j], axis=1, keepdims=True), wrow)
    wq_ref[...] = jnp.zeros((128, 128), f32)
    wq_ref[mine, :] = wrow
    wg_ref[...] = wq_ref[...].T[0:IHEADS, :].reshape(NH, 8, 128)
    for g in range(NH):
        for k in range(8):
            j = g * 8 + k
            iqg_ref[g, :, k * 128 : (k + 1) * 128] = iqg_acc[j * QROWS : (j + 1) * QROWS, :]


def back(grad, iqr, row, ik):
    f32, bf = jnp.float32, jnp.bfloat16
    vm_spec = pl.BlockSpec(memory_space=VM)
    rows = IHEADS * QROWS
    return pl.pallas_call(
        back_kernel,
        name="back",
        out_shape=(
            jax.ShapeDtypeStruct((2, NH, SETT // 2, 128), f32),
            jax.ShapeDtypeStruct((NH, QROWS, 1024), f32),
            jax.ShapeDtypeStruct((NH, 8, 128), f32),
        ),
        in_specs=[vm_spec] * 4,
        out_specs=(vm_spec,) * 3,
        scratch_shapes=[
            VM((rows, SETT), bf),
            VM((rows, SETT), bf),
            VM((128, 128), f32),
            VM((IHEADS, QROWS, 128), f32),
            VM((IHEADS, QROWS, 128), f32),
            VM((rows, 128), f32),
        ],
        compiler_params=pltpu.CompilerParams(vmem_limit_bytes=60 << 20),
    )(grad, iqr, row, ik)


HB = BLK // 2


def return_kernel(
    tab_s, ug_hbm, iqg_hbm, wg_hbm,
    iqg_out, wg_out, kg_out,
    urecv, sums, slots, brecv, own, wrecv,
    u_send, u_recv, i_send, i_recv, w_send, w_recv, b_send, b_recv, g_send, g_recv, h_send, h_recv, loc, loc_a, loc_b,
):
    me_h = lax.axis_index("head")
    me_c = lax.axis_index("ctx")
    my_q = pl.ds(pl.multiple_of(me_h * QROWS, QROWS), QROWS)
    own_copies = [
        pltpu.make_async_copy(ug_hbm.at[0, me_h], urecv.at[0, me_h], loc.at[0]),
        pltpu.make_async_copy(ug_hbm.at[1, me_h], urecv.at[1, me_h], loc.at[1]),
        pltpu.make_async_copy(iqg_hbm.at[me_h], iqg_out.at[my_q], loc.at[2]),
        pltpu.make_async_copy(wg_hbm.at[me_h], wrecv.at[me_h], loc.at[3]),
    ]
    for c in own_copies:
        c.start()
    start_barrier(me_h, me_c)
    sends = []

    def send_sums(q):
        for o in (1, 7, 3, 5, 2, 6, 4):
            h = lax.rem(me_h + o, NH)
            s = remote(
                ug_hbm.at[q, h], urecv.at[q, me_h], u_send.at[q * NH + o], u_recv.at[q * NH + o], (h, me_c)
            )
            s.start()
            sends.append(s)

    def take_sums(q):
        own_copies[q].wait()
        for o in range(1, NH):
            h = lax.rem(me_h + NH - o, NH)
            remote(
                ug_hbm.at[q, h], urecv.at[q, h], u_send.at[q * NH + o], u_recv.at[q * NH + o], (h, me_c)
            ).wait_recv()

    def send_blocks(q):
        for j in range(SETB):
            rows = slice(j * HB, (j + 1) * HB)
            acc = urecv[q, 0, rows, :]
            for h in range(1, NH):
                acc = acc + urecv[q, h, rows, :]
            sums[q, j] = acc
        sums[q, SETB] = jnp.zeros((HB, 128), jnp.float32)
        for o in range(1, NC + 1):
            c = lax.rem(me_c + o, NC)
            value = sums[q, tab_s[8 + me_h, c]]
            if o < NC:
                slots[q, o] = value
                s = remote(
                    slots.at[q, o], brecv.at[q, me_c], b_send.at[q * NC + o], b_recv.at[q * NC + o], (me_h, c)
                )
                s.start()
                sends.append(s)
            else:
                brecv[q, me_c] = value

    def take_blocks(q):
        for o in range(1, NC):
            c = lax.rem(me_c + NC - o, NC)
            remote(
                slots.at[q, o], brecv.at[q, c], b_send.at[q * NC + o], b_recv.at[q * NC + o], (me_h, c)
            ).wait_recv()
        for r in range(NC):
            at = (q * NC + r) * HB
            own[at : at + HB, :] = brecv[q, r].astype(own.dtype)

    rows = NC * HB

    def kg_of(h, start, count):
        return kg_out.at[h, pl.ds(start, count)]

    send_sums(0)
    take_sums(0)
    send_sums(1)
    send_blocks(0)
    take_blocks(0)
    ga = gather_sets([(own, kg_of, 0, rows)], me_h, me_c, g_send, g_recv, loc_a)
    next(ga)
    take_sums(1)
    send_blocks(1)
    for o in range(1, NH):
        h = lax.rem(me_h + o, NH)
        s = remote(iqg_hbm.at[h], iqg_out.at[my_q], i_send.at[o], i_recv.at[o], (h, me_c))
        s.start()
        sends.append(s)
        s = remote(wg_hbm.at[h], wrecv.at[me_h], w_send.at[o], w_recv.at[o], (h, me_c))
        s.start()
        sends.append(s)
    next(ga)
    take_blocks(1)
    gb = gather_sets([(own, kg_of, rows, rows)], me_h, me_c, h_send, h_recv, loc_b)
    next(gb)
    finish(ga, gb)
    for o in range(1, NH):
        h = lax.rem(me_h + NH - o, NH)
        remote(
            iqg_hbm.at[h], iqg_out.at[pl.ds(pl.multiple_of(h * QROWS, QROWS), QROWS)],
            i_send.at[o], i_recv.at[o], (h, me_c),
        ).wait_recv()
        remote(wg_hbm.at[h], wrecv.at[h], w_send.at[o], w_recv.at[o], (h, me_c)).wait_recv()
    own_copies[2].wait()
    own_copies[3].wait()
    acc = wrecv[0]
    for h in range(1, NH):
        acc = acc + wrecv[h]
    wg_out[...] = acc
    for s in sends:
        s.wait_send()


SENT = jnp.bfloat16


def give_back(tab, ug, iqg, wg):
    f32 = jnp.float32
    any_spec = pl.BlockSpec(memory_space=ANY)
    return pl.pallas_call(
        return_kernel,
        name="give_back",
        out_shape=(
            jax.ShapeDtypeStruct((NH * QROWS, 1024), f32),
            jax.ShapeDtypeStruct((8, 128), f32),
            jax.ShapeDtypeStruct((NH, NC * BLK, 128), SENT),
        ),
        in_specs=[pl.BlockSpec(memory_space=pltpu.SMEM)] + [any_spec] * 3,
        out_specs=(any_spec, pl.BlockSpec(memory_space=VM), any_spec),
        scratch_shapes=[
            VM((2, NH, SETT // 2, 128), f32),
            VM((2, SETB + 1, HB, 128), f32),
            VM((2, NC, HB, 128), f32),
            VM((2, NC, HB, 128), f32),
            VM((NC * BLK, 128), SENT),
            VM((NH, 8, 128), f32),
            DMA((2 * NH,)), DMA((2 * NH,)), DMA((NH,)), DMA((NH,)), DMA((NH,)), DMA((NH,)),
            DMA((2 * NC,)), DMA((2 * NC,)),
            DMA((9,)), DMA((9,)), DMA((9,)), DMA((9,)), DMA((4,)), DMA((1,)), DMA((1,)),
        ],
        compiler_params=pltpu.CompilerParams(
            collective_id=1, has_side_effects=True, vmem_limit_bytes=60 << 20
        ),
    )(tab, ug, iqg, wg)


def scatter_kernel(asked_s, kg_ref, out_ref):
    out_ref[...] = jnp.zeros(out_ref.shape, jnp.float32)

    def one(i, carry):
        h = lax.shift_right_logical(i, 4)
        r = lax.bitwise_and(i, 15)
        b = asked_s[r, h]
        for q in range(2):
            rows = pl.ds(pl.multiple_of(b * BLK + q * HB, HB), HB)
            part = kg_ref[h, pl.ds(pl.multiple_of((q * NC + r) * HB, HB), HB), :]
            out_ref[rows, :] = out_ref[rows, :] + part.astype(jnp.float32)
        return carry

    lax.fori_loop(0, NH * NC, one, 0)


def scatter(asked, kg, tokens):
    return pl.pallas_call(
        scatter_kernel,
        name="scatter",
        out_shape=jax.ShapeDtypeStruct((tokens, 128), jnp.float32),
        in_specs=[pl.BlockSpec(memory_space=pltpu.SMEM), pl.BlockSpec(memory_space=VM)],
        out_specs=pl.BlockSpec(memory_space=VM),
        compiler_params=pltpu.CompilerParams(vmem_limit_bytes=60 << 20),
    )(asked, kg)


def shards(main_query, latent, index_query, index_key, index_weight, selected, lengths, cotangent):
    sel_t = selected.T
    req, tab = make_plan(sel_t)
    grad, iqr, row, asked, ik = forward(
        tab, req, sel_t, lengths[None, :], cotangent[None, :],
        latent.T, index_key.reshape(-1, BLK, WIDTH), main_query, index_query, index_weight.T,
    )
    ug, iqg, wg = back(grad, iqr, row, ik)
    query_grad, weight_grad, kg = give_back(tab, ug, iqg, wg)
    key_grad = scatter(asked, kg, latent.shape[0])
    return query_grad, weight_grad.T, key_grad


def solution(mesh):
    return jax.shard_map(
        shards,
        mesh=mesh,
        in_specs=(
            P("ctx", "head"),
            P("ctx", None),
            P("ctx", "head"),
            P("ctx", None),
            P("ctx", "head"),
            P("ctx", None),
            P("ctx"),
            P("ctx"),
        ),
        out_specs=(P("ctx", "head"), P("ctx", "head"), P("ctx", None)),
        check_vma=False,
    )
```

```python
import functools
import math

import jax
import jax.numpy as jnp
from jax import lax
from jax.experimental import pallas as pl
from jax.experimental.pallas import tpu as pltpu
from jax.sharding import PartitionSpec as P

HEADS = 128
BLK = 64
POOL = 64
NH = 8
NC = 16
LAT = 576
WIDTH = 128
QROWS = 16
SETB = POOL // NH
SETT = SETB * BLK
HALF = LAT // 2
SLOT = HALF + BLK
UNION = POOL * BLK
IHEADS = 64

MESH = pl.DeviceIdType.MESH
ANY = pltpu.HBM
VM = pltpu.VMEM
DMA = pltpu.SemaphoreType.DMA

HIDDEN = -1e30
scale2 = 192.0 ** (-0.5) * math.log2(math.e)


def roll64(x):
    return pltpu.roll(x, 64, 1)


def start_barrier(me_h, me_c):
    barrier = pltpu.get_barrier_semaphore()
    for o in range(1, NH):
        pl.semaphore_signal(
            barrier, inc=1, device_id=(lax.rem(me_h + o, NH), me_c), device_id_type=MESH
        )
    for o in range(1, NC):
        pl.semaphore_signal(
            barrier, inc=1, device_id=(me_h, lax.rem(me_c + o, NC)), device_id_type=MESH
        )
    pl.semaphore_wait(barrier, NH + NC - 2)


def remote(src, dst, ssem, rsem, device):
    return pltpu.make_async_remote_copy(
        src_ref=src, dst_ref=dst, send_sem=ssem, recv_sem=rsem, device_id=device, device_id_type=MESH
    )


def gather_sets(pieces, me_h, me_c, ssem, rsem, lsem, between=None):
    right = (lax.rem(me_h + 2, NH), me_c)
    left = (lax.rem(me_h + 6, NH), me_c)
    flip = me_h + 1 - 2 * lax.rem(me_h, 2)
    partner = (flip, me_c)
    hl = lax.rem(me_h + 6, NH)
    hr = lax.rem(me_h + 2, NH)
    far = lax.rem(me_h + 4, NH)

    def flipped(h):
        return h + 1 - 2 * lax.rem(h, 2)

    count = len(pieces)
    sent = []

    def part(n, which):
        own, out, start, rows = pieces[n]
        half = rows // 32 * 16
        if which == 0:
            return start, rows
        return (start, half) if which == 1 else (start + half, rows - half)

    def copy(n, i, h, which, device, first=False):
        own, out, _, _ = pieces[n]
        start, rows = part(n, which)
        dst = out(h, start, rows)
        src = own.at[pl.ds(start, rows)] if first else dst
        return remote(src, dst, ssem.at[i * count + n], rsem.at[i * count + n], device)

    def go(i, h, which, device, first=False):
        for n in range(count):
            c = copy(n, i, h, which, device, first)
            c.start()
            sent.append(c)

    def wait(i, h, which, device):
        for n in range(count):
            copy(n, i, h, which, device).wait_recv()

    locals_ = [
        pltpu.make_async_copy(own.at[pl.ds(start, rows)], out(me_h, start, rows), lsem.at[n])
        for n, (own, out, start, rows) in enumerate(pieces)
    ]
    for c in locals_:
        c.start()
    go(0, me_h, 0, partner, True)
    go(1, me_h, 0, right, True)
    go(2, me_h, 0, left, True)
    yield
    wait(0, flip, 0, partner)
    go(3, flip, 0, right)
    go(4, flip, 0, left)
    yield
    wait(1, hl, 0, right)
    go(5, hl, 1, right)
    wait(2, hr, 0, left)
    go(6, hr, 2, left)
    yield
    wait(3, flipped(hl), 0, right)
    go(7, flipped(hl), 1, right)
    wait(4, flipped(hr), 0, left)
    go(8, flipped(hr), 2, left)
    yield
    wait(5, far, 1, right)
    wait(6, far, 2, left)
    wait(7, flipped(far), 1, right)
    wait(8, flipped(far), 2, left)
    for c in locals_:
        c.wait()
    for c in sent:
        c.wait_send()


def finish(*stages):
    left = list(stages)
    while left:
        for g in list(left):
            if next(g, 0) == 0:
                left.remove(g)


def iota(shape, dim):
    return lax.broadcasted_iota(jnp.int32, shape, dim)


def plan(sel, req_ref, tab_ref):
    hi = lax.shift_right_logical(sel, 7)
    lo = lax.bitwise_and(sel, 127)
    rows = sel.shape[0]
    owner_hot = jnp.concatenate(
        [jnp.where(iota((NC, 128), 0) == hi[i : i + 1, :], 1.0, 0.0) for i in range(rows)], axis=1
    ).astype(jnp.bfloat16)
    local_hot = jnp.concatenate(
        [jnp.where(iota((128, 128), 0) == lo[i : i + 1, :], 1.0, 0.0) for i in range(rows)], axis=1
    ).astype(jnp.bfloat16)
    counts = lax.dot_general(
        owner_hot, local_hot, (((1,), (1,)), ((), ())), preferred_element_type=jnp.float32
    )
    present = jnp.where(counts > 0.5, 1.0, 0.0)
    upper = jnp.where(iota((128, 128), 0) <= iota((128, 128), 1), 1.0, 0.0).astype(jnp.bfloat16)
    rank = jnp.dot(present.astype(jnp.bfloat16), upper, preferred_element_type=jnp.float32)
    total = rank[:, 127:128]
    lane = iota((NC, 128), 1)
    sub = iota((NC, 128), 0)
    spread = jnp.sum(jnp.where(lane == sub, total, 0.0), axis=0, keepdims=True)
    before = jnp.sum(jnp.where(lane < sub, jnp.broadcast_to(spread, (NC, 128)), 0.0), axis=1, keepdims=True)
    pos = (before + rank - 1.0).astype(jnp.int32)
    slot = lax.bitwise_and(pos, 7)
    step = lax.shift_right_logical(pos, 3).astype(jnp.float32)
    lane_f = lane.astype(jnp.float32)
    there = present > 0.5
    req = jnp.zeros((NC, 128), jnp.float32)
    ids = jnp.zeros((NC, 128), jnp.float32)
    owners = jnp.zeros((NC, 128), jnp.float32)
    sub_f = sub.astype(jnp.float32)
    for k in range(NH):
        hit = there & (slot == k)
        local = jnp.sum(jnp.where(hit, lane_f, 0.0), axis=1, keepdims=True)
        at = jnp.sum(jnp.where(hit, step, 0.0), axis=1, keepdims=True)
        has = jnp.sum(jnp.where(hit, 1.0, 0.0), axis=1, keepdims=True)
        req = jnp.where(lane == k, local, req)
        here = jnp.where(lane_f == at + float(SETB * k), has, 0.0)
        ids = ids + here * (sub_f * 128.0 + local)
        owners = owners + here * sub_f
        back = jnp.where(has > 0.5, at, float(SETB))
        row = jnp.sum(jnp.where(lane == sub, back, 0.0), axis=0, keepdims=True)
        tab_ref[8 + k : 9 + k, :] = row.astype(jnp.int32)
    tab_ref[0:1, :] = jnp.sum(ids, axis=0, keepdims=True).astype(jnp.int32)
    tab_ref[1:2, :] = jnp.sum(owners, axis=0, keepdims=True).astype(jnp.int32)
    tab_ref[2:8, :] = jnp.zeros((6, 128), jnp.int32)
    req_ref[...] = jnp.broadcast_to(req.astype(jnp.int32)[:, None, :], (NC, 8, 128))


def plan_kernel(sel_ref, req_ref, tab_ref):
    plan(sel_ref[...], req_ref, tab_ref)


def make_plan(sel_t):
    vm_spec = pl.BlockSpec(memory_space=VM)
    return pl.pallas_call(
        plan_kernel,
        name="plan",
        out_shape=(
            jax.ShapeDtypeStruct((NC, 8, 128), jnp.int32),
            jax.ShapeDtypeStruct((16, 128), jnp.int32),
        ),
        in_specs=[vm_spec],
        out_specs=(vm_spec, vm_spec),
        compiler_params=pltpu.CompilerParams(vmem_limit_bytes=60 << 20),
    )(sel_t)


SPLIT = SLOT // 2
FIRST = SPLIT - BLK
AUG = LAT + QROWS
TILE = 256


def forward_kernel(
    tab_s, req, sel_ref, len_ref, cot_ref, lat_hbm, ik_hbm, mq_hbm, iq_hbm, w_hbm,
    grad_ref, iqr_ref, wrow_ref, asked_out, ik_out,
    lat_v, ik_v, stage, recv_a, recv_b, own, own_ik, asked, asked_s,
    kt_ref, ik_ref, mq_ref, iq_ref, w_ref,
    sa_ref, sb_ref, ma_ref, mb_ref, qt_ref, bias_ref, tgt_ref, idx_ref, meta_ref, selb_ref, wb_ref,
    q_send, q_recv, i_send, i_recv, w_send, w_recv, r_send, r_recv, b_send, b_recv, c_send, c_recv,
    g_send, g_recv, h_send, h_recv, loc, loc_a, loc_b, l_sem,
):
    f32, bf = jnp.float32, jnp.bfloat16
    me_h = lax.axis_index("head")
    me_c = lax.axis_index("ctx")
    loads = [pltpu.make_async_copy(ik_hbm, ik_v, loc.at[1])] + [
        pltpu.make_async_copy(lat_hbm.at[:, pl.ds(i * 128, 128)], lat_v.at[i], l_sem.at[i])
        for i in range(lat_v.shape[0])
    ]
    for c in loads:
        c.start()
    mine = pl.ds(pl.multiple_of(me_h * QROWS, QROWS), QROWS)
    own_mq = pltpu.make_async_copy(mq_hbm.at[mine], mq_ref.at[me_h], loc.at[2])
    own_iq = pltpu.make_async_copy(iq_hbm.at[mine], iq_ref.at[me_h], loc.at[3])
    own_w = pltpu.make_async_copy(w_hbm, w_ref.at[me_h], loc.at[4])
    own_mq.start()
    own_iq.start()
    own_w.start()
    start_barrier(me_h, me_c)
    sends = []
    own_req = pltpu.make_async_copy(req.at[me_c], asked.at[me_c], loc.at[6])
    own_req.start()
    for o in range(1, NC):
        c = lax.rem(me_c + o, NC)
        s = remote(req.at[c], asked.at[me_c], r_send.at[o], r_recv.at[o], (me_h, c))
        s.start()
        sends.append(s)

    def peer_of(n, back=False):
        k = lax.rem(n, 4)
        dx = k + lax.div(k, 2) * (5 - 2 * k)
        dy = lax.div(n, 4)
        x = lax.div(me_h, 2) + (4 - dx if back else dx)
        y = lax.rem(me_h, 2) + dy
        return 2 * lax.rem(x, 4) + lax.rem(y, 2)

    def query_copy(n, back=False):
        h = peer_of(jnp.int32(n), back)
        rows = pl.ds(0, QROWS) if back else pl.ds(pl.multiple_of(h * QROWS, QROWS), QROWS)
        return remote(mq_hbm.at[rows], mq_ref.at[h if back else me_h], q_send.at[n], q_recv.at[n], (h, me_c))

    def send_queries(n):
        s = query_copy(n)
        s.start()
        sends.append(s)

    for o in range(1, NH):
        h = lax.rem(me_h + o, NH)
        rows = pl.ds(pl.multiple_of(h * QROWS, QROWS), QROWS)
        for src, dst, ss, rs in ((iq_hbm.at[rows], iq_ref, i_send, i_recv), (w_hbm, w_ref, w_send, w_recv)):
            s = remote(src, dst.at[me_h], ss.at[o], rs.at[o], (h, me_c))
            s.start()
            sends.append(s)
    for n in (1, 2, 3):
        send_queries(n)
    own_req.wait()
    for o in range(1, NC):
        c = lax.rem(me_c + NC - o, NC)
        remote(req.at[c], asked.at[c], r_send.at[o], r_recv.at[o], (me_h, c)).wait_recv()
    asked_out[...] = asked[:, 0, :]
    asked_copy = pltpu.make_async_copy(asked_out, asked_s, loc.at[7])
    asked_copy.start()
    for c in loads:
        c.wait()
    asked_copy.wait()
    first = iota((HALF, 128), 1) < 64
    lower = pl.ds(0, SPLIT)
    upper = pl.ds(SPLIT, SLOT - SPLIT)
    late = []
    for o in range(1, NC + 1):
        r = lax.rem(me_c + o, NC)
        b = asked_s[r, me_h]
        odd = jnp.full((HALF, 128), lax.bitwise_and(b, 1), jnp.int32) == 1
        pair = lax.shift_right_logical(b, 1)
        top = lat_v[pair, 0:HALF, :].astype(f32)
        bot = lat_v[pair, HALF:LAT, :].astype(f32)
        packed = jnp.where(
            first, jnp.where(odd, roll64(top), top), jnp.where(odd, bot, roll64(bot))
        ).astype(bf)
        keys = ik_v[b]
        if o < NC:
            stage[o, 0:BLK, :] = keys
            stage[o, BLK:SLOT, :] = packed
            s = remote(stage.at[o, lower], recv_a.at[me_c], b_send.at[o], b_recv.at[o], (me_h, r))
            s.start()
            sends.append(s)
            late.append(remote(stage.at[o, upper], recv_b.at[me_c], c_send.at[o], c_recv.at[o], (me_h, r)))
        else:
            recv_a[me_c, 0:BLK, :] = keys
            recv_a[me_c, BLK:SPLIT, :] = packed[0:FIRST]
            recv_b[me_c] = packed[FIRST:HALF]
    for s in late:
        s.start()
        sends.append(s)
    owners = [tab_s[1, me_h * SETB + j] for j in range(SETB)]

    own_w.wait()
    own_iq.wait()
    for o in range(1, NH):
        h = lax.rem(me_h + NH - o, NH)
        remote(iq_hbm.at[pl.ds(0, QROWS)], iq_ref.at[h], i_send.at[o], i_recv.at[o], (h, me_c)).wait_recv()
        remote(w_hbm, w_ref.at[h], w_send.at[o], w_recv.at[o], (h, me_c)).wait_recv()
    top = sel_ref.shape[0]
    meta_ref[...] = jnp.zeros((128, 128), f32)
    meta_ref[0:top, :] = sel_ref[...].astype(f32)
    meta_ref[top : top + 1, :] = len_ref[...].astype(f32)
    meta_ref[top + 1 : top + 2, :] = cot_ref[...]
    meta_ref[64 : 64 + IHEADS, :] = w_ref[...].reshape(IHEADS, 128)
    meta_ref[...] = meta_ref[...].T
    row = meta_ref[mine, :]
    wrow_ref[...] = row
    for i in range(top):
        selb_ref[i] = jnp.broadcast_to(row[:, i : i + 1], (QROWS, 128))
    limit = jnp.broadcast_to(row[:, top : top + 1], (QROWS, 128))
    cot = row[:, top + 1 : top + 2]
    for j in range(IHEADS):
        wb_ref[j] = jnp.broadcast_to(row[:, 64 + j : 65 + j], (QROWS, 128))
    lane = iota((QROWS, 128), 1)

    def mask_tile(i, carry):
        block = jnp.where(lane < 64, tab_s[0, 2 * i], tab_s[0, 2 * i + 1])
        block_f = block.astype(f32)
        hit = selb_ref[0] == block_f
        for q in range(1, top):
            hit = hit | (selb_ref[q] == block_f)
        token = (block * BLK + lax.bitwise_and(lane, 63)).astype(f32)
        ok = hit & (token < limit)
        cols = pl.ds(pl.multiple_of(i * 128, 128), 128)
        off = jnp.where(ok, 0.0, HIDDEN)
        bias_ref[:, cols] = off
        kt_ref[LAT:AUG, cols] = off.astype(bf)
        return carry

    lax.fori_loop(0, UNION // 128, mask_tile, 0)
    for h in range(NH):
        for k in range(8):
            iqr_ref[(h * 8 + k) * QROWS : (h * 8 + k + 1) * QROWS, :] = iq_ref[h, :, k * 128 : (k + 1) * 128]
    hot = jnp.where(iota((QROWS, QROWS), 0) == iota((QROWS, QROWS), 1), 1.0, 0.0).astype(bf)
    per = mq_ref.shape[2] // LAT
    for k in range(per):
        qt_ref[k * QROWS : (k + 1) * QROWS, LAT:AUG] = hot

    def merge(recv, skip, lo, hi):
        here = iota((hi - lo, 128), 1) < 64
        for i in range(SETB // 2):
            cols = slice(i * 128, (i + 1) * 128)
            a = recv[owners[2 * i], skip : skip + hi - lo, :].astype(f32)
            b = recv[owners[2 * i + 1], skip : skip + hi - lo, :].astype(f32)
            own[lo:hi, cols] = jnp.where(here, a, roll64(b)).astype(bf)
            own[HALF + lo : HALF + hi, cols] = jnp.where(here, roll64(a), b).astype(bf)

    def kt_of(h, start, rows):
        return kt_ref.at[pl.ds(start, rows), pl.ds(pl.multiple_of(h * SETT, SETT), SETT)]

    def ik_of(h, start, rows):
        return ik_ref.at[h, pl.ds(start, rows)]

    for o in range(1, NC):
        c = lax.rem(me_c + NC - o, NC)
        remote(stage.at[o, lower], recv_a.at[c], b_send.at[o], b_recv.at[o], (me_h, c)).wait_recv()
    merge(recv_a, BLK, 0, FIRST)
    for j in range(SETB):
        own_ik[j * BLK : (j + 1) * BLK, :] = recv_a[owners[j], 0:BLK, :]
    ga = gather_sets(
        [(own_ik, ik_of, 0, SETT), (own, kt_of, 0, FIRST), (own, kt_of, HALF, FIRST)],
        me_h, me_c, g_send, g_recv, loc_a,
    )
    next(ga)
    for o in range(1, NC):
        c = lax.rem(me_c + NC - o, NC)
        remote(stage.at[o, upper], recv_b.at[c], c_send.at[o], c_recv.at[o], (me_h, c)).wait_recv()
    merge(recv_b, 0, FIRST, HALF)
    next(ga)
    gb = gather_sets(
        [(own, kt_of, FIRST, HALF - FIRST), (own, kt_of, HALF + FIRST, HALF - FIRST)],
        me_h, me_c, h_send, h_recv, loc_b,
    )
    next(gb)
    next(ga)
    next(gb)
    send_queries(4)
    next(ga)
    next(gb)
    finish(ga)

    def index_chunk(i, carry):
        cols = pl.ds(pl.multiple_of(i * SETT, SETT), SETT)
        acc = jnp.zeros((QROWS, SETT), f32)
        for b in range(4):
            rows = slice(b * 256, (b + 1) * 256)
            pre = lax.dot_general(
                iqr_ref[rows, :], ik_ref[i], (((1,), (1,)), ((), ())), preferred_element_type=f32
            )
            for j in range(16):
                w = jnp.concatenate([wb_ref[b * 16 + j]] * (SETT // 128), axis=1)
                acc = acc + w * jnp.maximum(pre[j * QROWS : (j + 1) * QROWS, :], 0.0)
        idx_ref[:, cols] = acc + bias_ref[:, cols]
        return carry

    lax.fori_loop(0, NH // 2, index_chunk, 0)
    next(gb)
    for n in (5, 6, 7):
        send_queries(n)
    lax.fori_loop(NH // 2, NH, index_chunk, 0)
    keys_out = pltpu.make_async_copy(ik_ref, ik_out, loc.at[5])
    keys_out.start()
    v = idx_ref[...]
    e = jnp.exp(v - jnp.max(v, axis=1, keepdims=True))
    idx_ref[...] = e / jnp.sum(e, axis=1, keepdims=True)
    tgt_ref[...] = jnp.zeros((QROWS, UNION), f32)
    finish(gb)

    def load_queries(g):
        for k in range(per):
            qt_ref[k * QROWS : (k + 1) * QROWS, 0:LAT] = mq_ref[g, :, k * LAT : (k + 1) * LAT]

    def arrive(n):
        query_copy(n, True).wait_recv()
        load_queries(peer_of(jnp.int32(n), True))

    def score_tile(t, s_ref, m_ref):
        cols = slice(t * TILE, (t + 1) * TILE)
        s = jnp.dot(qt_ref[...], kt_ref[:, cols], preferred_element_type=f32)
        s_ref[:, cols] = s
        m = jnp.maximum(s[:, 0:128], s[:, 128:256])
        m_ref[...] = m if t == 0 else jnp.maximum(m_ref[...], m)

    def soften(k, s_ref, m_ref):
        rows = slice(k * QROWS, (k + 1) * QROWS)
        high = jnp.max(m_ref[rows, :], axis=1, keepdims=True) * scale2
        high = jnp.broadcast_to(high, (QROWS, 128))
        den = jnp.zeros((QROWS, 128), f32)
        for t in range(UNION // 128):
            cols = slice(t * 128, (t + 1) * 128)
            p = jnp.exp2(s_ref[rows, cols] * scale2 - high)
            s_ref[rows, cols] = p
            den = den + p
        return jnp.broadcast_to(1.0 / jnp.sum(den, axis=1, keepdims=True), (QROWS, 128))

    def add_up(recips, s_ref, lo):
        for t in range(UNION // 128):
            cols = slice(t * 128, (t + 1) * 128)
            acc = tgt_ref[:, cols]
            for q, r in enumerate(recips):
                acc = acc + s_ref[(lo + q) * QROWS : (lo + q + 1) * QROWS, cols] * r
            tgt_ref[:, cols] = acc

    def both(s_ref, m_ref, next_s, next_m):
        recips = []
        for k in range(per):
            recips.append(soften(k, s_ref, m_ref))
            if next_s is not None:
                score_tile(k, next_s, next_m)
            if k % 8 == 7:
                add_up(recips, s_ref, k - 7)
                recips = []

    own_mq.wait()
    load_queries(me_h)
    for t in range(UNION // TILE):
        score_tile(t, sa_ref, ma_ref)

    def two_groups(i, carry):
        arrive(2 * i + 1)
        both(sa_ref, ma_ref, sb_ref, mb_ref)
        arrive(2 * i + 2)
        both(sb_ref, mb_ref, sa_ref, ma_ref)
        return carry

    lax.fori_loop(0, NH // 2 - 1, two_groups, 0)
    arrive(NH - 1)
    both(sa_ref, ma_ref, sb_ref, mb_ref)
    both(sb_ref, mb_ref, None, None)
    grad_ref[...] = cot * (idx_ref[...] - tgt_ref[...] * (1.0 / HEADS))
    keys_out.wait()
    for s in sends:
        s.wait_send()


def forward(tab, req, sel_t, lengths, cot, lat_t, index_key, main_query, index_query, weight_t):
    any_spec = pl.BlockSpec(memory_space=ANY)
    vm_spec = pl.BlockSpec(memory_space=VM)
    f32, bf, i32 = jnp.float32, jnp.bfloat16, jnp.int32
    rows = IHEADS * QROWS
    return pl.pallas_call(
        forward_kernel,
        name="forward",
        out_shape=(
            jax.ShapeDtypeStruct((QROWS, UNION), f32),
            jax.ShapeDtypeStruct((rows, 128), bf),
            jax.ShapeDtypeStruct((QROWS, 128), f32),
            jax.ShapeDtypeStruct((16, 128), i32),
            jax.ShapeDtypeStruct((NH, SETT, 128), bf),
        ),
        in_specs=[pl.BlockSpec(memory_space=pltpu.SMEM)] + [vm_spec] * 4 + [any_spec] * 5,
        out_specs=(vm_spec,) * 4 + (any_spec,),
        scratch_shapes=[
            VM((lat_t.shape[1] // 128, LAT, 128), bf),
            VM(index_key.shape, bf),
            VM((NC, SLOT, 128), bf),
            VM((NC, SPLIT, 128), bf),
            VM((NC, SLOT - SPLIT, 128), bf),
            VM((LAT, SETT), bf),
            VM((SETT, 128), bf),
            VM((NC, 8, 128), i32),
            pltpu.SMEM((16, 128), i32),
            VM((AUG, UNION), bf),
            VM((NH, SETT, 128), bf),
            VM((NH, QROWS, main_query.shape[1]), bf),
            VM((NH, QROWS, index_query.shape[1]), bf),
            VM((NH, 8, 128), f32),
            VM((256, UNION), f32),
            VM((256, UNION), f32),
            VM((256, 128), f32),
            VM((256, 128), f32),
            VM((256, AUG), bf),
            VM((QROWS, UNION), f32),
            VM((QROWS, UNION), f32),
            VM((QROWS, UNION), f32),
            VM((128, 128), f32),
            VM((32, QROWS, 128), f32),
            VM((IHEADS, QROWS, 128), f32),
            DMA((NH,)), DMA((NH,)), DMA((NH,)), DMA((NH,)), DMA((NH,)), DMA((NH,)),
            DMA((NC,)), DMA((NC,)), DMA((NC,)), DMA((NC,)), DMA((NC,)), DMA((NC,)),
            DMA((27,)), DMA((27,)), DMA((18,)), DMA((18,)), DMA((9,)), DMA((3,)), DMA((3,)),
            DMA((lat_t.shape[1] // 128,)),
        ],
        compiler_params=pltpu.CompilerParams(
            collective_id=0, has_side_effects=True, vmem_limit_bytes=60 << 20
        ),
    )(tab, req, sel_t, lengths, cot, lat_t, index_key, main_query, index_query, weight_t)


HB = BLK // 2


def return_kernel(
    tab_s, grad_ref, iqr_ref, row_ref, ik_ref,
    iqg_out, wg_out, kg_out,
    ea_ref, eb_ref, wq_ref, wb_ref, wcol_ref, iqg_acc, iqt_ref, iqg, wg, ug,
    urecv, sums, slots, brecv, own, wrecv,
    u_send, u_recv, i_send, i_recv, w_send, w_recv, b_send, b_recv, g_send, g_recv, h_send, h_recv, loc, loc_a, loc_b,
):
    f32, bf = jnp.float32, jnp.bfloat16
    me_h = lax.axis_index("head")
    me_c = lax.axis_index("ctx")
    my_q = pl.ds(pl.multiple_of(me_h * QROWS, QROWS), QROWS)
    start_barrier(me_h, me_c)
    lane = iota((QROWS, 128), 1)
    row = row_ref[...]
    for j in range(IHEADS):
        wb_ref[j] = jnp.broadcast_to(row[:, 64 + j : 65 + j], (QROWS, 128))
    wcol_ref[...] = jnp.zeros(wcol_ref.shape, f32)
    iqg_acc[...] = jnp.zeros(iqg_acc.shape, f32)
    iqt_ref[...] = iqr_ref[...].T

    def whose(n):
        return lax.rem(me_h + 1 + n, NH)

    def edges(n, e_ref):
        h = whose(n)
        grad = grad_ref[:, pl.ds(pl.multiple_of(h * SETT, SETT), SETT)]
        for b in range(4):
            pre_b = lax.dot_general(
                iqr_ref[b * 256 : (b + 1) * 256, :], ik_ref[h], (((1,), (1,)), ((), ())), preferred_element_type=f32
            )
            for q in range(16):
                j = b * 16 + q
                pre = pre_b[q * QROWS : (q + 1) * QROWS, :]
                w = jnp.concatenate([wb_ref[j]] * (SETT // 128), axis=1)
                part = jnp.maximum(pre, 0.0) * grad
                wcol_ref[j] = wcol_ref[j] + sum(part[:, t * 128 : (t + 1) * 128] for t in range(SETT // 128))
                e_ref[j * QROWS : (j + 1) * QROWS, :] = jnp.where(pre > 0.0, grad * w, 0.0).astype(bf)

    def products(n, e_ref):
        h = whose(n)
        part = jnp.dot(iqt_ref[...], e_ref[...], preferred_element_type=f32).T.reshape(SETB, 2, HB, 128)
        for q in range(2):
            ug[q, n] = part[:, q].reshape(SETT // 2, 128)
        for b in range(4):
            rows = slice(b * 256, (b + 1) * 256)
            iqg_acc[rows, :] = iqg_acc[rows, :] + jnp.dot(e_ref[rows, :], ik_ref[h], preferred_element_type=f32)

    def sum_copy(q, n):
        return remote(
            ug.at[q, n], urecv.at[q, n], u_send.at[q * NH + n], u_recv.at[q * NH + n], (whose(n), me_c)
        )

    edges(0, ea_ref)

    def two_sets(i, carry):
        edges(2 * i + 1, eb_ref)
        products(2 * i, ea_ref)
        sum_copy(0, 2 * i).start()
        edges(2 * i + 2, ea_ref)
        products(2 * i + 1, eb_ref)
        sum_copy(0, 2 * i + 1).start()
        return carry

    lax.fori_loop(0, NH // 2 - 1, two_sets, 0)
    edges(NH - 1, eb_ref)
    products(NH - 2, ea_ref)
    sum_copy(0, NH - 2).start()
    for n in range(NH - 1):
        sum_copy(1, n).start()
    products(NH - 1, eb_ref)
    wrow = jnp.zeros((QROWS, 128), f32)
    for j in range(IHEADS):
        wrow = jnp.where(lane == j, jnp.sum(wcol_ref[j], axis=1, keepdims=True), wrow)
    wq_ref[...] = jnp.zeros((128, 128), f32)
    wq_ref[my_q, :] = wrow
    wg[...] = wq_ref[...].T[0:IHEADS, :].reshape(NH, 8, 128)
    for g in range(NH):
        for k in range(8):
            j = g * 8 + k
            iqg[g, :, k * 128 : (k + 1) * 128] = iqg_acc[j * QROWS : (j + 1) * QROWS, :]
    own_copies = [
        pltpu.make_async_copy(iqg.at[me_h], iqg_out.at[my_q], loc.at[2]),
        pltpu.make_async_copy(wg.at[me_h], wrecv.at[me_h], loc.at[3]),
    ]
    for c in own_copies:
        c.start()
    sends = [sum_copy(q, n) for q in range(2) for n in range(NH - 1)]

    def take_sums(q):
        for n in range(NH - 1):
            sum_copy(q, n).wait_recv()

    def send_blocks(q):
        for j in range(SETB):
            rows = slice(j * HB, (j + 1) * HB)
            acc = ug[q, NH - 1, rows, :]
            for n in range(NH - 1):
                acc = acc + urecv[q, n, rows, :]
            sums[q, j] = acc
        sums[q, SETB] = jnp.zeros((HB, 128), jnp.float32)
        for o in range(1, NC + 1):
            c = lax.rem(me_c + o, NC)
            value = sums[q, tab_s[8 + me_h, c]]
            if o < NC:
                slots[q, o] = value
                s = remote(
                    slots.at[q, o], brecv.at[q, me_c], b_send.at[q * NC + o], b_recv.at[q * NC + o], (me_h, c)
                )
                s.start()
                sends.append(s)
            else:
                brecv[q, me_c] = value

    def take_blocks(q):
        for o in range(1, NC):
            c = lax.rem(me_c + NC - o, NC)
            remote(
                slots.at[q, o], brecv.at[q, c], b_send.at[q * NC + o], b_recv.at[q * NC + o], (me_h, c)
            ).wait_recv()
        for r in range(NC):
            at = (q * NC + r) * HB
            own[at : at + HB, :] = brecv[q, r].astype(own.dtype)

    rows = NC * HB

    def kg_of(h, start, count):
        return kg_out.at[h, pl.ds(start, count)]

    take_sums(0)
    send_blocks(0)
    take_blocks(0)
    ga = gather_sets([(own, kg_of, 0, rows)], me_h, me_c, g_send, g_recv, loc_a)
    next(ga)
    take_sums(1)
    send_blocks(1)
    for o in range(1, NH):
        h = lax.rem(me_h + o, NH)
        s = remote(iqg.at[h], iqg_out.at[my_q], i_send.at[o], i_recv.at[o], (h, me_c))
        s.start()
        sends.append(s)
        s = remote(wg.at[h], wrecv.at[me_h], w_send.at[o], w_recv.at[o], (h, me_c))
        s.start()
        sends.append(s)
    next(ga)
    take_blocks(1)
    gb = gather_sets([(own, kg_of, rows, rows)], me_h, me_c, h_send, h_recv, loc_b)
    next(gb)
    finish(ga, gb)
    for o in range(1, NH):
        h = lax.rem(me_h + NH - o, NH)
        remote(
            iqg.at[h], iqg_out.at[pl.ds(pl.multiple_of(h * QROWS, QROWS), QROWS)],
            i_send.at[o], i_recv.at[o], (h, me_c),
        ).wait_recv()
        remote(wg.at[h], wrecv.at[h], w_send.at[o], w_recv.at[o], (h, me_c)).wait_recv()
    for c in own_copies:
        c.wait()
    acc = wrecv[0]
    for h in range(1, NH):
        acc = acc + wrecv[h]
    wg_out[...] = acc
    for s in sends:
        s.wait_send()


SENT = jnp.bfloat16


def give_back(tab, grad, iqr, row, ik):
    f32, bf = jnp.float32, jnp.bfloat16
    any_spec = pl.BlockSpec(memory_space=ANY)
    vm_spec = pl.BlockSpec(memory_space=VM)
    rows = IHEADS * QROWS
    return pl.pallas_call(
        return_kernel,
        name="give_back",
        out_shape=(
            jax.ShapeDtypeStruct((NH * QROWS, 1024), f32),
            jax.ShapeDtypeStruct((8, 128), f32),
            jax.ShapeDtypeStruct((NH, NC * BLK, 128), SENT),
        ),
        in_specs=[pl.BlockSpec(memory_space=pltpu.SMEM)] + [vm_spec] * 4,
        out_specs=(any_spec, vm_spec, any_spec),
        scratch_shapes=[
            VM((rows, SETT), bf),
            VM((rows, SETT), bf),
            VM((128, 128), f32),
            VM((IHEADS, QROWS, 128), f32),
            VM((IHEADS, QROWS, 128), f32),
            VM((rows, 128), f32),
            VM((128, rows), bf),
            VM((NH, QROWS, 1024), f32),
            VM((NH, 8, 128), f32),
            VM((2, NH, SETT // 2, 128), f32),
            VM((2, NH - 1, SETT // 2, 128), f32),
            VM((2, SETB + 1, HB, 128), f32),
            VM((2, NC, HB, 128), f32),
            VM((2, NC, HB, 128), f32),
            VM((NC * BLK, 128), SENT),
            VM((NH, 8, 128), f32),
            DMA((2 * NH,)), DMA((2 * NH,)), DMA((NH,)), DMA((NH,)), DMA((NH,)), DMA((NH,)),
            DMA((2 * NC,)), DMA((2 * NC,)),
            DMA((9,)), DMA((9,)), DMA((9,)), DMA((9,)), DMA((4,)), DMA((1,)), DMA((1,)),
        ],
        compiler_params=pltpu.CompilerParams(
            collective_id=1, has_side_effects=True, vmem_limit_bytes=60 << 20
        ),
    )(tab, grad, iqr, row, ik)


def scatter_kernel(asked_s, kg_ref, out_ref):
    out_ref[...] = jnp.zeros(out_ref.shape, jnp.float32)

    def one(i, carry):
        h = lax.shift_right_logical(i, 4)
        r = lax.bitwise_and(i, 15)
        b = asked_s[r, h]
        for q in range(2):
            rows = pl.ds(pl.multiple_of(b * BLK + q * HB, HB), HB)
            part = kg_ref[h, pl.ds(pl.multiple_of((q * NC + r) * HB, HB), HB), :]
            out_ref[rows, :] = out_ref[rows, :] + part.astype(jnp.float32)
        return carry

    lax.fori_loop(0, NH * NC, one, 0)


def scatter(asked, kg, tokens):
    return pl.pallas_call(
        scatter_kernel,
        name="scatter",
        out_shape=jax.ShapeDtypeStruct((tokens, 128), jnp.float32),
        in_specs=[pl.BlockSpec(memory_space=pltpu.SMEM), pl.BlockSpec(memory_space=VM)],
        out_specs=pl.BlockSpec(memory_space=VM),
        compiler_params=pltpu.CompilerParams(vmem_limit_bytes=60 << 20),
    )(asked, kg)


def shards(main_query, latent, index_query, index_key, index_weight, selected, lengths, cotangent):
    sel_t = selected.T
    req, tab = make_plan(sel_t)
    grad, iqr, row, asked, ik = forward(
        tab, req, sel_t, lengths[None, :], cotangent[None, :],
        latent.T, index_key.reshape(-1, BLK, WIDTH), main_query, index_query, index_weight.T,
    )
    query_grad, weight_grad, kg = give_back(tab, grad, iqr, row, ik)
    key_grad = scatter(asked, kg, latent.shape[0])
    return query_grad, weight_grad.T, key_grad


def solution(mesh):
    return jax.shard_map(
        shards,
        mesh=mesh,
        in_specs=(
            P("ctx", "head"),
            P("ctx", None),
            P("ctx", "head"),
            P("ctx", None),
            P("ctx", "head"),
            P("ctx", None),
            P("ctx"),
            P("ctx"),
        ),
        out_specs=(P("ctx", "head"), P("ctx", "head"), P("ctx", None)),
        check_vma=False,
    )
```

```python
import functools
import math

import jax
import jax.numpy as jnp
from jax import lax
from jax.experimental import pallas as pl
from jax.experimental.pallas import tpu as pltpu
from jax.sharding import PartitionSpec as P

HEADS = 128
BLK = 64
POOL = 64
NH = 8
NC = 16
LAT = 576
WIDTH = 128
QROWS = 16
SETB = POOL // NH
SETT = SETB * BLK
HALF = LAT // 2
SLOT = HALF + BLK
UNION = POOL * BLK
IHEADS = 64

MESH = pl.DeviceIdType.MESH
ANY = pltpu.HBM
VM = pltpu.VMEM
DMA = pltpu.SemaphoreType.DMA

HIDDEN = -1e30
scale2 = 192.0 ** (-0.5) * math.log2(math.e)


def roll64(x):
    return pltpu.roll(x, 64, 1)


def start_barrier(me_h, me_c):
    barrier = pltpu.get_barrier_semaphore()
    for o in range(1, NH):
        pl.semaphore_signal(
            barrier, inc=1, device_id=(lax.rem(me_h + o, NH), me_c), device_id_type=MESH
        )
    for o in range(1, NC):
        pl.semaphore_signal(
            barrier, inc=1, device_id=(me_h, lax.rem(me_c + o, NC)), device_id_type=MESH
        )
    pl.semaphore_wait(barrier, NH + NC - 2)


def remote(src, dst, ssem, rsem, device):
    return pltpu.make_async_remote_copy(
        src_ref=src, dst_ref=dst, send_sem=ssem, recv_sem=rsem, device_id=device, device_id_type=MESH
    )


def gather_sets(pieces, me_h, me_c, ssem, rsem, lsem, between=None):
    right = (lax.rem(me_h + 2, NH), me_c)
    left = (lax.rem(me_h + 6, NH), me_c)
    flip = me_h + 1 - 2 * lax.rem(me_h, 2)
    partner = (flip, me_c)
    hl = lax.rem(me_h + 6, NH)
    hr = lax.rem(me_h + 2, NH)
    far = lax.rem(me_h + 4, NH)

    def flipped(h):
        return h + 1 - 2 * lax.rem(h, 2)

    count = len(pieces)
    sent = []

    def part(n, which):
        own, out, start, rows = pieces[n]
        half = rows // 32 * 16
        if which == 0:
            return start, rows
        return (start, half) if which == 1 else (start + half, rows - half)

    def copy(n, i, h, which, device, first=False):
        own, out, _, _ = pieces[n]
        start, rows = part(n, which)
        dst = out(h, start, rows)
        src = own.at[pl.ds(start, rows)] if first else dst
        return remote(src, dst, ssem.at[i * count + n], rsem.at[i * count + n], device)

    def go(i, h, which, device, first=False):
        for n in range(count):
            c = copy(n, i, h, which, device, first)
            c.start()
            sent.append(c)

    def wait(i, h, which, device):
        for n in range(count):
            copy(n, i, h, which, device).wait_recv()

    locals_ = [
        pltpu.make_async_copy(own.at[pl.ds(start, rows)], out(me_h, start, rows), lsem.at[n])
        for n, (own, out, start, rows) in enumerate(pieces)
    ]
    for c in locals_:
        c.start()
    go(0, me_h, 0, partner, True)
    go(1, me_h, 0, right, True)
    go(2, me_h, 0, left, True)
    yield
    for c in locals_:
        c.wait()
    wait(0, flip, 0, partner)
    go(3, flip, 0, right)
    go(4, flip, 0, left)
    yield
    wait(1, hl, 0, right)
    go(5, hl, 1, right)
    wait(2, hr, 0, left)
    go(6, hr, 2, left)
    yield
    wait(3, flipped(hl), 0, right)
    go(7, flipped(hl), 1, right)
    wait(4, flipped(hr), 0, left)
    go(8, flipped(hr), 2, left)
    yield
    wait(5, far, 1, right)
    wait(6, far, 2, left)
    wait(7, flipped(far), 1, right)
    wait(8, flipped(far), 2, left)
    for c in sent:
        c.wait_send()


def finish(*stages):
    left = list(stages)
    while left:
        for g in list(left):
            if next(g, 0) == 0:
                left.remove(g)


def iota(shape, dim):
    return lax.broadcasted_iota(jnp.int32, shape, dim)


def plan(sel, req_ref, tab_ref):
    hi = lax.shift_right_logical(sel, 7)
    lo = lax.bitwise_and(sel, 127)
    rows = sel.shape[0]
    owner_hot = jnp.concatenate(
        [jnp.where(iota((NC, 128), 0) == hi[i : i + 1, :], 1.0, 0.0) for i in range(rows)], axis=1
    ).astype(jnp.bfloat16)
    local_hot = jnp.concatenate(
        [jnp.where(iota((128, 128), 0) == lo[i : i + 1, :], 1.0, 0.0) for i in range(rows)], axis=1
    ).astype(jnp.bfloat16)
    counts = lax.dot_general(
        owner_hot, local_hot, (((1,), (1,)), ((), ())), preferred_element_type=jnp.float32
    )
    present = jnp.where(counts > 0.5, 1.0, 0.0)
    upper = jnp.where(iota((128, 128), 0) <= iota((128, 128), 1), 1.0, 0.0).astype(jnp.bfloat16)
    rank = jnp.dot(present.astype(jnp.bfloat16), upper, preferred_element_type=jnp.float32)
    total = rank[:, 127:128]
    lane = iota((NC, 128), 1)
    sub = iota((NC, 128), 0)
    spread = jnp.sum(jnp.where(lane == sub, total, 0.0), axis=0, keepdims=True)
    before = jnp.sum(jnp.where(lane < sub, jnp.broadcast_to(spread, (NC, 128)), 0.0), axis=1, keepdims=True)
    pos = (before + rank - 1.0).astype(jnp.int32)
    slot = lax.bitwise_and(pos, 7)
    step = lax.shift_right_logical(pos, 3).astype(jnp.float32)
    lane_f = lane.astype(jnp.float32)
    there = present > 0.5
    req = jnp.zeros((NC, 128), jnp.float32)
    ids = jnp.zeros((NC, 128), jnp.float32)
    owners = jnp.zeros((NC, 128), jnp.float32)
    sub_f = sub.astype(jnp.float32)
    for k in range(NH):
        hit = there & (slot == k)
        local = jnp.sum(jnp.where(hit, lane_f, 0.0), axis=1, keepdims=True)
        at = jnp.sum(jnp.where(hit, step, 0.0), axis=1, keepdims=True)
        has = jnp.sum(jnp.where(hit, 1.0, 0.0), axis=1, keepdims=True)
        req = jnp.where(lane == k, local, req)
        here = jnp.where(lane_f == at + float(SETB * k), has, 0.0)
        ids = ids + here * (sub_f * 128.0 + local)
        owners = owners + here * sub_f
        back = jnp.where(has > 0.5, at, float(SETB))
        row = jnp.sum(jnp.where(lane == sub, back, 0.0), axis=0, keepdims=True)
        tab_ref[8 + k : 9 + k, :] = row.astype(jnp.int32)
    tab_ref[0:1, :] = jnp.sum(ids, axis=0, keepdims=True).astype(jnp.int32)
    tab_ref[1:2, :] = jnp.sum(owners, axis=0, keepdims=True).astype(jnp.int32)
    tab_ref[2:8, :] = jnp.zeros((6, 128), jnp.int32)
    req_ref[...] = jnp.broadcast_to(req.astype(jnp.int32)[:, None, :], (NC, 8, 128))


def plan_kernel(sel_ref, req_ref, tab_ref):
    plan(sel_ref[...], req_ref, tab_ref)


def make_plan(sel_t):
    vm_spec = pl.BlockSpec(memory_space=VM)
    return pl.pallas_call(
        plan_kernel,
        name="plan",
        out_shape=(
            jax.ShapeDtypeStruct((NC, 8, 128), jnp.int32),
            jax.ShapeDtypeStruct((16, 128), jnp.int32),
        ),
        in_specs=[vm_spec],
        out_specs=(vm_spec, vm_spec),
        compiler_params=pltpu.CompilerParams(vmem_limit_bytes=60 << 20),
    )(sel_t)


SPLIT = SLOT // 2
FIRST = SPLIT - BLK
AUG = LAT + QROWS
TILE = 256


def forward_kernel(
    tab_s, req, sel_ref, len_ref, cot_ref, lat_hbm, ik_hbm, mq_hbm, iq_hbm, w_hbm,
    grad_ref, iqr_ref, wrow_ref, asked_out, ik_out,
    lat_v, ik_v, stage, recv_a, recv_b, own, own_ik, asked, asked_s,
    kt_ref, ik_ref, mq_ref, iq_ref, w_ref, passing,
    sa_ref, sb_ref, ma_ref, mb_ref, qt_ref, bias_ref, tgt_ref, idx_ref, meta_ref, selb_ref, wb_ref,
    q_send, q_recv, i_send, i_recv, w_send, w_recv, r_send, r_recv, b_send, b_recv, c_send, c_recv,
    g_send, g_recv, h_send, h_recv, loc, loc_a, loc_b, l_sem, p_send, p_recv,
):
    f32, bf = jnp.float32, jnp.bfloat16
    me_h = lax.axis_index("head")
    me_c = lax.axis_index("ctx")
    loads = [pltpu.make_async_copy(ik_hbm, ik_v, loc.at[1])] + [
        pltpu.make_async_copy(lat_hbm.at[:, pl.ds(i * 128, 128)], lat_v.at[i], l_sem.at[i])
        for i in range(lat_v.shape[0])
    ]
    for c in loads:
        c.start()
    mine = pl.ds(pl.multiple_of(me_h * QROWS, QROWS), QROWS)
    own_mq = pltpu.make_async_copy(mq_hbm.at[mine], mq_ref.at[me_h], loc.at[2])
    own_iq = pltpu.make_async_copy(iq_hbm.at[mine], iq_ref.at[me_h], loc.at[3])
    own_w = pltpu.make_async_copy(w_hbm, w_ref.at[me_h], loc.at[4])
    own_mq.start()
    own_iq.start()
    own_w.start()
    start_barrier(me_h, me_c)
    sends = []
    own_req = pltpu.make_async_copy(req.at[me_c], asked.at[me_c], loc.at[6])
    own_req.start()
    for o in range(1, NC):
        c = lax.rem(me_c + o, NC)
        s = remote(req.at[c], asked.at[me_c], r_send.at[o], r_recv.at[o], (me_h, c))
        s.start()
        sends.append(s)

    def peer_of(n, back=False):
        k = lax.rem(n, 4)
        dx = k + lax.div(k, 2) * (5 - 2 * k)
        dy = lax.div(n, 4)
        x = lax.div(me_h, 2) + (4 - dx if back else dx)
        y = lax.rem(me_h, 2) + dy
        return 2 * lax.rem(x, 4) + lax.rem(y, 2)

    def query_copy(n, back=False):
        h = peer_of(jnp.int32(n), back)
        rows = pl.ds(0, QROWS) if back else pl.ds(pl.multiple_of(h * QROWS, QROWS), QROWS)
        return remote(mq_hbm.at[rows], mq_ref.at[h if back else me_h], q_send.at[n], q_recv.at[n], (h, me_c))

    def send_queries(n):
        s = query_copy(n)
        s.start()
        sends.append(s)

    partner = me_h + 1 - 2 * lax.rem(me_h, 2)

    def relay_copy(n, back=False):
        h = peer_of(jnp.int32(n))
        rows = pl.ds(0, QROWS) if back else pl.ds(pl.multiple_of(h * QROWS, QROWS), QROWS)
        return remote(mq_hbm.at[rows], passing.at[n - 5], p_send.at[n - 5], p_recv.at[n - 5], (partner, me_c))

    def send_over(n):
        s = relay_copy(n)
        s.start()
        sends.append(s)

    def pass_on(n):
        relay_copy(n, True).wait_recv()
        dx = (1, 3, 2)[n - 5]
        to = lax.rem(me_h + 2 * dx, NH)
        s = remote(passing.at[n - 5], mq_ref.at[partner], q_send.at[n], q_recv.at[n], (to, me_c))
        s.start()
        sends.append(s)

    for o in range(1, NH):
        h = lax.rem(me_h + o, NH)
        rows = pl.ds(pl.multiple_of(h * QROWS, QROWS), QROWS)
        for src, dst, ss, rs in ((iq_hbm.at[rows], iq_ref, i_send, i_recv), (w_hbm, w_ref, w_send, w_recv)):
            s = remote(src, dst.at[me_h], ss.at[o], rs.at[o], (h, me_c))
            s.start()
            sends.append(s)
    for n in (1, 2, 3):
        send_queries(n)
    own_req.wait()
    for o in range(1, NC):
        c = lax.rem(me_c + NC - o, NC)
        remote(req.at[c], asked.at[c], r_send.at[o], r_recv.at[o], (me_h, c)).wait_recv()
    asked_out[...] = asked[:, 0, :]
    asked_copy = pltpu.make_async_copy(asked_out, asked_s, loc.at[7])
    asked_copy.start()
    for c in loads:
        c.wait()
    asked_copy.wait()
    first = iota((HALF, 128), 1) < 64
    lower = pl.ds(0, SPLIT)
    upper = pl.ds(SPLIT, SLOT - SPLIT)
    late = []
    for o in range(1, NC + 1):
        r = lax.rem(me_c + o, NC)
        b = asked_s[r, me_h]
        odd = jnp.full((HALF, 128), lax.bitwise_and(b, 1), jnp.int32) == 1
        pair = lax.shift_right_logical(b, 1)
        top = lat_v[pair, 0:HALF, :].astype(f32)
        bot = lat_v[pair, HALF:LAT, :].astype(f32)
        packed = jnp.where(
            first, jnp.where(odd, roll64(top), top), jnp.where(odd, bot, roll64(bot))
        ).astype(bf)
        keys = ik_v[b]
        if o < NC:
            stage[o, 0:BLK, :] = keys
            stage[o, BLK:SLOT, :] = packed
            s = remote(stage.at[o, lower], recv_a.at[me_c], b_send.at[o], b_recv.at[o], (me_h, r))
            s.start()
            sends.append(s)
            late.append(remote(stage.at[o, upper], recv_b.at[me_c], c_send.at[o], c_recv.at[o], (me_h, r)))
        else:
            recv_a[me_c, 0:BLK, :] = keys
            recv_a[me_c, BLK:SPLIT, :] = packed[0:FIRST]
            recv_b[me_c] = packed[FIRST:HALF]
    for s in late:
        s.start()
        sends.append(s)
    owners = [tab_s[1, me_h * SETB + j] for j in range(SETB)]

    own_w.wait()
    own_iq.wait()
    for o in range(1, NH):
        h = lax.rem(me_h + NH - o, NH)
        remote(iq_hbm.at[pl.ds(0, QROWS)], iq_ref.at[h], i_send.at[o], i_recv.at[o], (h, me_c)).wait_recv()
        remote(w_hbm, w_ref.at[h], w_send.at[o], w_recv.at[o], (h, me_c)).wait_recv()
    top = sel_ref.shape[0]
    meta_ref[...] = jnp.zeros((128, 128), f32)
    meta_ref[0:top, :] = sel_ref[...].astype(f32)
    meta_ref[top : top + 1, :] = len_ref[...].astype(f32)
    meta_ref[top + 1 : top + 2, :] = cot_ref[...]
    meta_ref[64 : 64 + IHEADS, :] = w_ref[...].reshape(IHEADS, 128)
    meta_ref[...] = meta_ref[...].T
    row = meta_ref[mine, :]
    wrow_ref[...] = row
    for i in range(top):
        selb_ref[i] = jnp.broadcast_to(row[:, i : i + 1], (QROWS, 128))
    limit = jnp.broadcast_to(row[:, top : top + 1], (QROWS, 128))
    cot = row[:, top + 1 : top + 2]
    for j in range(IHEADS):
        wb_ref[j] = jnp.broadcast_to(row[:, 64 + j : 65 + j], (QROWS, 128))
    lane = iota((QROWS, 128), 1)

    def mask_tile(i, carry):
        block = jnp.where(lane < 64, tab_s[0, 2 * i], tab_s[0, 2 * i + 1])
        block_f = block.astype(f32)
        hit = selb_ref[0] == block_f
        for q in range(1, top):
            hit = hit | (selb_ref[q] == block_f)
        token = (block * BLK + lax.bitwise_and(lane, 63)).astype(f32)
        ok = hit & (token < limit)
        cols = pl.ds(pl.multiple_of(i * 128, 128), 128)
        off = jnp.where(ok, 0.0, HIDDEN)
        bias_ref[:, cols] = off
        kt_ref[LAT:AUG, cols] = off.astype(bf)
        return carry

    lax.fori_loop(0, UNION // 128, mask_tile, 0)
    for h in range(NH):
        for k in range(8):
            iqr_ref[(h * 8 + k) * QROWS : (h * 8 + k + 1) * QROWS, :] = iq_ref[h, :, k * 128 : (k + 1) * 128]
    hot = jnp.where(iota((QROWS, QROWS), 0) == iota((QROWS, QROWS), 1), 1.0, 0.0).astype(bf)
    per = mq_ref.shape[2] // LAT
    for k in range(per):
        qt_ref[k * QROWS : (k + 1) * QROWS, LAT:AUG] = hot

    def merge(recv, skip, lo, hi):
        here = iota((hi - lo, 128), 1) < 64
        for i in range(SETB // 2):
            cols = slice(i * 128, (i + 1) * 128)
            a = recv[owners[2 * i], skip : skip + hi - lo, :].astype(f32)
            b = recv[owners[2 * i + 1], skip : skip + hi - lo, :].astype(f32)
            own[lo:hi, cols] = jnp.where(here, a, roll64(b)).astype(bf)
            own[HALF + lo : HALF + hi, cols] = jnp.where(here, roll64(a), b).astype(bf)

    def kt_of(h, start, rows):
        return kt_ref.at[pl.ds(start, rows), pl.ds(pl.multiple_of(h * SETT, SETT), SETT)]

    def ik_of(h, start, rows):
        return ik_ref.at[h, pl.ds(start, rows)]

    for o in range(1, NC):
        c = lax.rem(me_c + NC - o, NC)
        remote(stage.at[o, lower], recv_a.at[c], b_send.at[o], b_recv.at[o], (me_h, c)).wait_recv()
    merge(recv_a, BLK, 0, FIRST)
    for j in range(SETB):
        own_ik[j * BLK : (j + 1) * BLK, :] = recv_a[owners[j], 0:BLK, :]
    ga = gather_sets(
        [(own_ik, ik_of, 0, SETT), (own, kt_of, 0, FIRST), (own, kt_of, HALF, FIRST)],
        me_h, me_c, g_send, g_recv, loc_a,
    )
    next(ga)
    for o in range(1, NC):
        c = lax.rem(me_c + NC - o, NC)
        remote(stage.at[o, upper], recv_b.at[c], c_send.at[o], c_recv.at[o], (me_h, c)).wait_recv()
    merge(recv_b, 0, FIRST, HALF)
    next(ga)
    gb = gather_sets(
        [(own, kt_of, FIRST, HALF - FIRST), (own, kt_of, HALF + FIRST, HALF - FIRST)],
        me_h, me_c, h_send, h_recv, loc_b,
    )
    def index_scores(i):
        cols = pl.ds(pl.multiple_of(i * SETT, SETT), SETT)
        acc = jnp.zeros((QROWS, SETT), f32)
        for b in range(4):
            rows = slice(b * 256, (b + 1) * 256)
            pre = lax.dot_general(
                iqr_ref[rows, :], ik_ref[i], (((1,), (1,)), ((), ())), preferred_element_type=f32
            )
            for j in range(16):
                w = jnp.concatenate([wb_ref[b * 16 + j]] * (SETT // 128), axis=1)
                acc = acc + w * jnp.maximum(pre[j * QROWS : (j + 1) * QROWS, :], 0.0)
        idx_ref[:, cols] = acc + bias_ref[:, cols]

    flip = partner
    near_l, near_r, far = (lax.rem(me_h + o, NH) for o in (6, 2, 4))

    def other(h):
        return h + 1 - 2 * lax.rem(h, 2)

    next(gb)
    next(ga)
    next(gb)
    send_queries(4)
    for n in (5, 6, 7):
        send_over(n)
    index_scores(me_h)
    index_scores(flip)
    next(ga)
    next(gb)
    index_scores(near_l)
    index_scores(near_r)
    next(gb)
    for n in (5, 6, 7):
        pass_on(n)
    index_scores(other(near_l))
    index_scores(other(near_r))
    finish(ga)
    index_scores(far)
    index_scores(other(far))
    keys_out = pltpu.make_async_copy(ik_ref, ik_out, loc.at[5])
    keys_out.start()
    v = idx_ref[...]
    e = jnp.exp(v - jnp.max(v, axis=1, keepdims=True))
    idx_ref[...] = e / jnp.sum(e, axis=1, keepdims=True)
    tgt_ref[...] = jnp.zeros((QROWS, UNION), f32)
    finish(gb)

    def load_queries(g):
        for k in range(per):
            qt_ref[k * QROWS : (k + 1) * QROWS, 0:LAT] = mq_ref[g, :, k * LAT : (k + 1) * LAT]

    def arrive(n):
        query_copy(n, True).wait_recv()
        load_queries(peer_of(jnp.int32(n), True))

    def score_tile(t, s_ref, m_ref):
        cols = slice(t * TILE, (t + 1) * TILE)
        s = jnp.dot(qt_ref[...], kt_ref[:, cols], preferred_element_type=f32)
        s_ref[:, cols] = s
        m = jnp.maximum(s[:, 0:128], s[:, 128:256])
        m_ref[...] = m if t == 0 else jnp.maximum(m_ref[...], m)

    def soften(k, s_ref, m_ref):
        rows = slice(k * QROWS, (k + 1) * QROWS)
        high = jnp.max(m_ref[rows, :], axis=1, keepdims=True) * scale2
        high = jnp.broadcast_to(high, (QROWS, 128))
        den = jnp.zeros((QROWS, 128), f32)
        for t in range(UNION // 128):
            cols = slice(t * 128, (t + 1) * 128)
            p = jnp.exp2(s_ref[rows, cols] * scale2 - high)
            s_ref[rows, cols] = p
            den = den + p
        return jnp.broadcast_to(1.0 / jnp.sum(den, axis=1, keepdims=True), (QROWS, 128))

    def add_up(recips, s_ref, lo):
        for t in range(UNION // 128):
            cols = slice(t * 128, (t + 1) * 128)
            acc = tgt_ref[:, cols]
            for q, r in enumerate(recips):
                acc = acc + s_ref[(lo + q) * QROWS : (lo + q + 1) * QROWS, cols] * r
            tgt_ref[:, cols] = acc

    def both(s_ref, m_ref, next_s, next_m):
        recips = []
        for k in range(per):
            recips.append(soften(k, s_ref, m_ref))
            if next_s is not None:
                score_tile(k, next_s, next_m)
            if k % 8 == 7:
                add_up(recips, s_ref, k - 7)
                recips = []

    own_mq.wait()
    load_queries(me_h)
    for t in range(UNION // TILE):
        score_tile(t, sa_ref, ma_ref)

    def two_groups(i, carry):
        arrive(2 * i + 1)
        both(sa_ref, ma_ref, sb_ref, mb_ref)
        arrive(2 * i + 2)
        both(sb_ref, mb_ref, sa_ref, ma_ref)
        return carry

    lax.fori_loop(0, NH // 2 - 1, two_groups, 0)
    arrive(NH - 1)
    both(sa_ref, ma_ref, sb_ref, mb_ref)
    both(sb_ref, mb_ref, None, None)
    grad_ref[...] = cot * (idx_ref[...] - tgt_ref[...] * (1.0 / HEADS))
    keys_out.wait()
    for s in sends:
        s.wait_send()


def forward(tab, req, sel_t, lengths, cot, lat_t, index_key, main_query, index_query, weight_t):
    any_spec = pl.BlockSpec(memory_space=ANY)
    vm_spec = pl.BlockSpec(memory_space=VM)
    f32, bf, i32 = jnp.float32, jnp.bfloat16, jnp.int32
    rows = IHEADS * QROWS
    return pl.pallas_call(
        forward_kernel,
        name="forward",
        out_shape=(
            jax.ShapeDtypeStruct((QROWS, UNION), f32),
            jax.ShapeDtypeStruct((rows, 128), bf),
            jax.ShapeDtypeStruct((QROWS, 128), f32),
            jax.ShapeDtypeStruct((16, 128), i32),
            jax.ShapeDtypeStruct((NH, SETT, 128), bf),
        ),
        in_specs=[pl.BlockSpec(memory_space=pltpu.SMEM)] + [vm_spec] * 4 + [any_spec] * 5,
        out_specs=(vm_spec,) * 4 + (any_spec,),
        scratch_shapes=[
            VM((lat_t.shape[1] // 128, LAT, 128), bf),
            VM(index_key.shape, bf),
            VM((NC, SLOT, 128), bf),
            VM((NC, SPLIT, 128), bf),
            VM((NC, SLOT - SPLIT, 128), bf),
            VM((LAT, SETT), bf),
            VM((SETT, 128), bf),
            VM((NC, 8, 128), i32),
            pltpu.SMEM((16, 128), i32),
            VM((AUG, UNION), bf),
            VM((NH, SETT, 128), bf),
            VM((NH, QROWS, main_query.shape[1]), bf),
            VM((NH, QROWS, index_query.shape[1]), bf),
            VM((NH, 8, 128), f32),
            VM((3, QROWS, main_query.shape[1]), bf),
            VM((256, UNION), f32),
            VM((256, UNION), f32),
            VM((256, 128), f32),
            VM((256, 128), f32),
            VM((256, AUG), bf),
            VM((QROWS, UNION), f32),
            VM((QROWS, UNION), f32),
            VM((QROWS, UNION), f32),
            VM((128, 128), f32),
            VM((32, QROWS, 128), f32),
            VM((IHEADS, QROWS, 128), f32),
            DMA((NH,)), DMA((NH,)), DMA((NH,)), DMA((NH,)), DMA((NH,)), DMA((NH,)),
            DMA((NC,)), DMA((NC,)), DMA((NC,)), DMA((NC,)), DMA((NC,)), DMA((NC,)),
            DMA((27,)), DMA((27,)), DMA((18,)), DMA((18,)), DMA((9,)), DMA((3,)), DMA((3,)),
            DMA((lat_t.shape[1] // 128,)), DMA((3,)), DMA((3,)),
        ],
        compiler_params=pltpu.CompilerParams(
            collective_id=0, has_side_effects=True, vmem_limit_bytes=60 << 20
        ),
    )(tab, req, sel_t, lengths, cot, lat_t, index_key, main_query, index_query, weight_t)


HB = BLK // 2


def return_kernel(
    tab_s, grad_ref, iqr_ref, row_ref, ik_ref,
    iqg_out, wg_out, kg_out,
    ea_ref, eb_ref, wq_ref, wb_ref, wcol_ref, iqg_acc, iqt_ref, iqg, wg, ug,
    urecv, sums, slots, brecv, own, wrecv,
    u_send, u_recv, i_send, i_recv, w_send, w_recv, b_send, b_recv, g_send, g_recv, h_send, h_recv, loc, loc_a, loc_b,
):
    f32, bf = jnp.float32, jnp.bfloat16
    me_h = lax.axis_index("head")
    me_c = lax.axis_index("ctx")
    my_q = pl.ds(pl.multiple_of(me_h * QROWS, QROWS), QROWS)
    start_barrier(me_h, me_c)
    lane = iota((QROWS, 128), 1)
    row = row_ref[...]
    for j in range(IHEADS):
        wb_ref[j] = jnp.broadcast_to(row[:, 64 + j : 65 + j], (QROWS, 128))
    wcol_ref[...] = jnp.zeros(wcol_ref.shape, f32)
    iqg_acc[...] = jnp.zeros(iqg_acc.shape, f32)
    iqt_ref[...] = iqr_ref[...].T

    def whose(n):
        return lax.rem(me_h + 1 + n, NH)

    def edges(n, e_ref):
        h = whose(n)
        grad = grad_ref[:, pl.ds(pl.multiple_of(h * SETT, SETT), SETT)]
        for b in range(4):
            pre_b = lax.dot_general(
                iqr_ref[b * 256 : (b + 1) * 256, :], ik_ref[h], (((1,), (1,)), ((), ())), preferred_element_type=f32
            )
            for q in range(16):
                j = b * 16 + q
                pre = pre_b[q * QROWS : (q + 1) * QROWS, :]
                w = jnp.concatenate([wb_ref[j]] * (SETT // 128), axis=1)
                part = jnp.maximum(pre, 0.0) * grad
                wcol_ref[j] = wcol_ref[j] + sum(part[:, t * 128 : (t + 1) * 128] for t in range(SETT // 128))
                e_ref[j * QROWS : (j + 1) * QROWS, :] = jnp.where(pre > 0.0, grad * w, 0.0).astype(bf)

    def products(n, e_ref):
        h = whose(n)
        part = jnp.dot(iqt_ref[...], e_ref[...], preferred_element_type=f32).T.reshape(SETB, 2, HB, 128)
        for q in range(2):
            ug[q, n] = part[:, q].reshape(SETT // 2, 128)
        for b in range(4):
            rows = slice(b * 256, (b + 1) * 256)
            iqg_acc[rows, :] = iqg_acc[rows, :] + jnp.dot(e_ref[rows, :], ik_ref[h], preferred_element_type=f32)

    def sum_copy(q, n):
        return remote(
            ug.at[q, n], urecv.at[q, n], u_send.at[q * NH + n], u_recv.at[q * NH + n], (whose(n), me_c)
        )

    edges(0, ea_ref)

    def two_sets(i, carry):
        edges(2 * i + 1, eb_ref)
        products(2 * i, ea_ref)
        sum_copy(0, 2 * i).start()
        edges(2 * i + 2, ea_ref)
        products(2 * i + 1, eb_ref)
        sum_copy(0, 2 * i + 1).start()
        return carry

    lax.fori_loop(0, NH // 2 - 1, two_sets, 0)
    edges(NH - 1, eb_ref)
    products(NH - 2, ea_ref)
    sum_copy(0, NH - 2).start()
    for n in range(NH - 1):
        sum_copy(1, n).start()
    products(NH - 1, eb_ref)
    wrow = jnp.zeros((QROWS, 128), f32)
    for j in range(IHEADS):
        wrow = jnp.where(lane == j, jnp.sum(wcol_ref[j], axis=1, keepdims=True), wrow)
    wq_ref[...] = jnp.zeros((128, 128), f32)
    wq_ref[my_q, :] = wrow
    wg[...] = wq_ref[...].T[0:IHEADS, :].reshape(NH, 8, 128)
    for g in range(NH):
        for k in range(8):
            j = g * 8 + k
            iqg[g, :, k * 128 : (k + 1) * 128] = iqg_acc[j * QROWS : (j + 1) * QROWS, :]
    own_copies = [
        pltpu.make_async_copy(iqg.at[me_h], iqg_out.at[my_q], loc.at[2]),
        pltpu.make_async_copy(wg.at[me_h], wrecv.at[me_h], loc.at[3]),
    ]
    for c in own_copies:
        c.start()
    sends = [sum_copy(q, n) for q in range(2) for n in range(NH - 1)]

    def take_sums(q):
        for n in range(NH - 1):
            sum_copy(q, n).wait_recv()

    def send_blocks(q):
        for j in range(SETB):
            rows = slice(j * HB, (j + 1) * HB)
            acc = ug[q, NH - 1, rows, :]
            for n in range(NH - 1):
                acc = acc + urecv[q, n, rows, :]
            sums[q, j] = acc
        sums[q, SETB] = jnp.zeros((HB, 128), jnp.float32)
        for o in range(1, NC + 1):
            c = lax.rem(me_c + o, NC)
            value = sums[q, tab_s[8 + me_h, c]]
            if o < NC:
                slots[q, o] = value
                s = remote(
                    slots.at[q, o], brecv.at[q, me_c], b_send.at[q * NC + o], b_recv.at[q * NC + o], (me_h, c)
                )
                s.start()
                sends.append(s)
            else:
                brecv[q, me_c] = value

    def take_blocks(q):
        for o in range(1, NC):
            c = lax.rem(me_c + NC - o, NC)
            remote(
                slots.at[q, o], brecv.at[q, c], b_send.at[q * NC + o], b_recv.at[q * NC + o], (me_h, c)
            ).wait_recv()
        for r in range(NC):
            at = (q * NC + r) * HB
            own[at : at + HB, :] = brecv[q, r].astype(own.dtype)

    rows = NC * HB

    def kg_of(h, start, count):
        return kg_out.at[h, pl.ds(start, count)]

    take_sums(0)
    send_blocks(0)
    take_blocks(0)
    ga = gather_sets([(own, kg_of, 0, rows)], me_h, me_c, g_send, g_recv, loc_a)
    next(ga)
    take_sums(1)
    send_blocks(1)
    for o in range(1, NH):
        h = lax.rem(me_h + o, NH)
        s = remote(iqg.at[h], iqg_out.at[my_q], i_send.at[o], i_recv.at[o], (h, me_c))
        s.start()
        sends.append(s)
        s = remote(wg.at[h], wrecv.at[me_h], w_send.at[o], w_recv.at[o], (h, me_c))
        s.start()
        sends.append(s)
    next(ga)
    take_blocks(1)
    gb = gather_sets([(own, kg_of, rows, rows)], me_h, me_c, h_send, h_recv, loc_b)
    next(gb)
    finish(ga, gb)
    for o in range(1, NH):
        h = lax.rem(me_h + NH - o, NH)
        remote(
            iqg.at[h], iqg_out.at[pl.ds(pl.multiple_of(h * QROWS, QROWS), QROWS)],
            i_send.at[o], i_recv.at[o], (h, me_c),
        ).wait_recv()
        remote(wg.at[h], wrecv.at[h], w_send.at[o], w_recv.at[o], (h, me_c)).wait_recv()
    for c in own_copies:
        c.wait()
    acc = wrecv[0]
    for h in range(1, NH):
        acc = acc + wrecv[h]
    wg_out[...] = acc
    for s in sends:
        s.wait_send()


SENT = jnp.bfloat16


def give_back(tab, grad, iqr, row, ik):
    f32, bf = jnp.float32, jnp.bfloat16
    any_spec = pl.BlockSpec(memory_space=ANY)
    vm_spec = pl.BlockSpec(memory_space=VM)
    rows = IHEADS * QROWS
    return pl.pallas_call(
        return_kernel,
        name="give_back",
        out_shape=(
            jax.ShapeDtypeStruct((NH * QROWS, 1024), f32),
            jax.ShapeDtypeStruct((8, 128), f32),
            jax.ShapeDtypeStruct((NH, NC * BLK, 128), SENT),
        ),
        in_specs=[pl.BlockSpec(memory_space=pltpu.SMEM)] + [vm_spec] * 4,
        out_specs=(any_spec, vm_spec, any_spec),
        scratch_shapes=[
            VM((rows, SETT), bf),
            VM((rows, SETT), bf),
            VM((128, 128), f32),
            VM((IHEADS, QROWS, 128), f32),
            VM((IHEADS, QROWS, 128), f32),
            VM((rows, 128), f32),
            VM((128, rows), bf),
            VM((NH, QROWS, 1024), f32),
            VM((NH, 8, 128), f32),
            VM((2, NH, SETT // 2, 128), f32),
            VM((2, NH - 1, SETT // 2, 128), f32),
            VM((2, SETB + 1, HB, 128), f32),
            VM((2, NC, HB, 128), f32),
            VM((2, NC, HB, 128), f32),
            VM((NC * BLK, 128), SENT),
            VM((NH, 8, 128), f32),
            DMA((2 * NH,)), DMA((2 * NH,)), DMA((NH,)), DMA((NH,)), DMA((NH,)), DMA((NH,)),
            DMA((2 * NC,)), DMA((2 * NC,)),
            DMA((9,)), DMA((9,)), DMA((9,)), DMA((9,)), DMA((4,)), DMA((1,)), DMA((1,)),
        ],
        compiler_params=pltpu.CompilerParams(
            collective_id=1, has_side_effects=True, vmem_limit_bytes=60 << 20
        ),
    )(tab, grad, iqr, row, ik)


def scatter_kernel(asked_s, kg_ref, out_ref):
    out_ref[...] = jnp.zeros(out_ref.shape, jnp.float32)

    def one(i, carry):
        h = lax.shift_right_logical(i, 4)
        r = lax.bitwise_and(i, 15)
        b = asked_s[r, h]
        for q in range(2):
            rows = pl.ds(pl.multiple_of(b * BLK + q * HB, HB), HB)
            part = kg_ref[h, pl.ds(pl.multiple_of((q * NC + r) * HB, HB), HB), :]
            out_ref[rows, :] = out_ref[rows, :] + part.astype(jnp.float32)
        return carry

    lax.fori_loop(0, NH * NC, one, 0, unroll=4)


def scatter(asked, kg, tokens):
    return pl.pallas_call(
        scatter_kernel,
        name="scatter",
        out_shape=jax.ShapeDtypeStruct((tokens, 128), jnp.float32),
        in_specs=[pl.BlockSpec(memory_space=pltpu.SMEM), pl.BlockSpec(memory_space=VM)],
        out_specs=pl.BlockSpec(memory_space=VM),
        compiler_params=pltpu.CompilerParams(vmem_limit_bytes=60 << 20),
    )(asked, kg)


def shards(main_query, latent, index_query, index_key, index_weight, selected, lengths, cotangent):
    sel_t = selected.T
    req, tab = make_plan(sel_t)
    grad, iqr, row, asked, ik = forward(
        tab, req, sel_t, lengths[None, :], cotangent[None, :],
        latent.T, index_key.reshape(-1, BLK, WIDTH), main_query, index_query, index_weight.T,
    )
    query_grad, weight_grad, kg = give_back(tab, grad, iqr, row, ik)
    key_grad = scatter(asked, kg, latent.shape[0])
    return query_grad, weight_grad.T, key_grad


def solution(mesh):
    return jax.shard_map(
        shards,
        mesh=mesh,
        in_specs=(
            P("ctx", "head"),
            P("ctx", None),
            P("ctx", "head"),
            P("ctx", None),
            P("ctx", "head"),
            P("ctx", None),
            P("ctx"),
            P("ctx"),
        ),
        out_specs=(P("ctx", "head"), P("ctx", "head"), P("ctx", None)),
        check_vma=False,
    )
```

```python
import functools
import math

import jax
import jax.numpy as jnp
from jax import lax
from jax.experimental import pallas as pl
from jax.experimental.pallas import tpu as pltpu
from jax.sharding import PartitionSpec as P

HEADS = 128
BLK = 64
POOL = 64
NH = 8
NC = 16
LAT = 576
WIDTH = 128
QROWS = 16
SETB = POOL // NH
SETT = SETB * BLK
HALF = LAT // 2
SLOT = HALF + BLK
UNION = POOL * BLK
IHEADS = 64

MESH = pl.DeviceIdType.MESH
ANY = pltpu.HBM
VM = pltpu.VMEM
DMA = pltpu.SemaphoreType.DMA

HIDDEN = -1e30
scale2 = 192.0 ** (-0.5) * math.log2(math.e)


def roll64(x):
    return pltpu.roll(x, 64, 1)


def start_barrier(me_h, me_c):
    barrier = pltpu.get_barrier_semaphore()
    for o in range(1, NH):
        pl.semaphore_signal(
            barrier, inc=1, device_id=(lax.rem(me_h + o, NH), me_c), device_id_type=MESH
        )
    for o in range(1, NC):
        pl.semaphore_signal(
            barrier, inc=1, device_id=(me_h, lax.rem(me_c + o, NC)), device_id_type=MESH
        )
    pl.semaphore_wait(barrier, NH + NC - 2)


def remote(src, dst, ssem, rsem, device):
    return pltpu.make_async_remote_copy(
        src_ref=src, dst_ref=dst, send_sem=ssem, recv_sem=rsem, device_id=device, device_id_type=MESH
    )


def gather_sets(pieces, me_h, me_c, ssem, rsem, lsem, between=None):
    right = (lax.rem(me_h + 2, NH), me_c)
    left = (lax.rem(me_h + 6, NH), me_c)
    flip = me_h + 1 - 2 * lax.rem(me_h, 2)
    partner = (flip, me_c)
    hl = lax.rem(me_h + 6, NH)
    hr = lax.rem(me_h + 2, NH)
    far = lax.rem(me_h + 4, NH)

    def flipped(h):
        return h + 1 - 2 * lax.rem(h, 2)

    count = len(pieces)
    sent = []

    def part(n, which):
        own, out, start, rows = pieces[n]
        half = rows // 32 * 16
        if which == 0:
            return start, rows
        return (start, half) if which == 1 else (start + half, rows - half)

    def copy(n, i, h, which, device, first=False):
        own, out, _, _ = pieces[n]
        start, rows = part(n, which)
        dst = out(h, start, rows)
        src = own.at[pl.ds(start, rows)] if first else dst
        return remote(src, dst, ssem.at[i * count + n], rsem.at[i * count + n], device)

    def go(i, h, which, device, first=False):
        for n in range(count):
            c = copy(n, i, h, which, device, first)
            c.start()
            sent.append(c)

    def wait(i, h, which, device):
        for n in range(count):
            copy(n, i, h, which, device).wait_recv()

    locals_ = [
        pltpu.make_async_copy(own.at[pl.ds(start, rows)], out(me_h, start, rows), lsem.at[n])
        for n, (own, out, start, rows) in enumerate(pieces)
    ]
    for c in locals_:
        c.start()
    go(0, me_h, 0, partner, True)
    go(1, me_h, 0, right, True)
    go(2, me_h, 0, left, True)
    yield
    for c in locals_:
        c.wait()
    wait(0, flip, 0, partner)
    go(3, flip, 0, right)
    go(4, flip, 0, left)
    yield
    wait(1, hl, 0, right)
    go(5, hl, 1, right)
    wait(2, hr, 0, left)
    go(6, hr, 2, left)
    yield
    wait(3, flipped(hl), 0, right)
    go(7, flipped(hl), 1, right)
    wait(4, flipped(hr), 0, left)
    go(8, flipped(hr), 2, left)
    yield
    wait(5, far, 1, right)
    wait(6, far, 2, left)
    wait(7, flipped(far), 1, right)
    wait(8, flipped(far), 2, left)
    for c in sent:
        c.wait_send()


def finish(*stages):
    left = list(stages)
    while left:
        for g in list(left):
            if next(g, 0) == 0:
                left.remove(g)


def iota(shape, dim):
    return lax.broadcasted_iota(jnp.int32, shape, dim)


def plan(sel, req_ref, tab_ref):
    hi = lax.shift_right_logical(sel, 7)
    lo = lax.bitwise_and(sel, 127)
    rows = sel.shape[0]
    owner_hot = jnp.concatenate(
        [jnp.where(iota((NC, 128), 0) == hi[i : i + 1, :], 1.0, 0.0) for i in range(rows)], axis=1
    ).astype(jnp.bfloat16)
    local_hot = jnp.concatenate(
        [jnp.where(iota((128, 128), 0) == lo[i : i + 1, :], 1.0, 0.0) for i in range(rows)], axis=1
    ).astype(jnp.bfloat16)
    counts = lax.dot_general(
        owner_hot, local_hot, (((1,), (1,)), ((), ())), preferred_element_type=jnp.float32
    )
    present = jnp.where(counts > 0.5, 1.0, 0.0)
    upper = jnp.where(iota((128, 128), 0) <= iota((128, 128), 1), 1.0, 0.0).astype(jnp.bfloat16)
    rank = jnp.dot(present.astype(jnp.bfloat16), upper, preferred_element_type=jnp.float32)
    total = rank[:, 127:128]
    lane = iota((NC, 128), 1)
    sub = iota((NC, 128), 0)
    spread = jnp.sum(jnp.where(lane == sub, total, 0.0), axis=0, keepdims=True)
    before = jnp.sum(jnp.where(lane < sub, jnp.broadcast_to(spread, (NC, 128)), 0.0), axis=1, keepdims=True)
    pos = (before + rank - 1.0).astype(jnp.int32)
    slot = lax.bitwise_and(pos, 7)
    step = lax.shift_right_logical(pos, 3).astype(jnp.float32)
    lane_f = lane.astype(jnp.float32)
    there = present > 0.5
    req = jnp.zeros((NC, 128), jnp.float32)
    ids = jnp.zeros((NC, 128), jnp.float32)
    owners = jnp.zeros((NC, 128), jnp.float32)
    sub_f = sub.astype(jnp.float32)
    for k in range(NH):
        hit = there & (slot == k)
        local = jnp.sum(jnp.where(hit, lane_f, 0.0), axis=1, keepdims=True)
        at = jnp.sum(jnp.where(hit, step, 0.0), axis=1, keepdims=True)
        has = jnp.sum(jnp.where(hit, 1.0, 0.0), axis=1, keepdims=True)
        req = jnp.where(lane == k, local, req)
        here = jnp.where(lane_f == at + float(SETB * k), has, 0.0)
        ids = ids + here * (sub_f * 128.0 + local)
        owners = owners + here * sub_f
        back = jnp.where(has > 0.5, at, float(SETB))
        row = jnp.sum(jnp.where(lane == sub, back, 0.0), axis=0, keepdims=True)
        tab_ref[8 + k : 9 + k, :] = row.astype(jnp.int32)
    tab_ref[0:1, :] = jnp.sum(ids, axis=0, keepdims=True).astype(jnp.int32)
    tab_ref[1:2, :] = jnp.sum(owners, axis=0, keepdims=True).astype(jnp.int32)
    tab_ref[2:8, :] = jnp.zeros((6, 128), jnp.int32)
    req_ref[...] = jnp.broadcast_to(req.astype(jnp.int32)[:, None, :], (NC, 8, 128))


def plan_kernel(sel_ref, req_ref, tab_ref):
    plan(sel_ref[...], req_ref, tab_ref)


def make_plan(sel_t):
    vm_spec = pl.BlockSpec(memory_space=VM)
    return pl.pallas_call(
        plan_kernel,
        name="plan",
        out_shape=(
            jax.ShapeDtypeStruct((NC, 8, 128), jnp.int32),
            jax.ShapeDtypeStruct((16, 128), jnp.int32),
        ),
        in_specs=[vm_spec],
        out_specs=(vm_spec, vm_spec),
        compiler_params=pltpu.CompilerParams(vmem_limit_bytes=60 << 20),
    )(sel_t)


SPLIT = SLOT // 2
FIRST = SPLIT - BLK
AUG = LAT + QROWS
TILE = 256


def forward_kernel(
    tab_s, req, sel_ref, len_ref, cot_ref, lat_hbm, ik_hbm, mq_hbm, iq_hbm, w_hbm,
    grad_ref, iqr_ref, wrow_ref, asked_out, ik_out,
    lat_v, ik_v, stage, recv_a, recv_b, own, own_ik, asked, asked_s,
    kt_ref, ik_ref, mq_ref, iq_ref, w_ref, passing,
    sa_ref, sb_ref, ma_ref, mb_ref, qt_ref, bias_ref, tgt_ref, idx_ref, meta_ref, selb_ref, wb_ref,
    q_send, q_recv, i_send, i_recv, w_send, w_recv, r_send, r_recv, b_send, b_recv, c_send, c_recv,
    g_send, g_recv, h_send, h_recv, loc, loc_a, loc_b, l_sem, p_send, p_recv,
):
    f32, bf = jnp.float32, jnp.bfloat16
    me_h = lax.axis_index("head")
    me_c = lax.axis_index("ctx")
    loads = [pltpu.make_async_copy(ik_hbm, ik_v, loc.at[1])] + [
        pltpu.make_async_copy(lat_hbm.at[:, pl.ds(i * 128, 128)], lat_v.at[i], l_sem.at[i])
        for i in range(lat_v.shape[0])
    ]
    for c in loads:
        c.start()
    mine = pl.ds(pl.multiple_of(me_h * QROWS, QROWS), QROWS)
    own_mq = pltpu.make_async_copy(mq_hbm.at[mine], mq_ref.at[me_h], loc.at[2])
    own_iq = pltpu.make_async_copy(iq_hbm.at[mine], iq_ref.at[me_h], loc.at[3])
    own_w = pltpu.make_async_copy(w_hbm, w_ref.at[me_h], loc.at[4])
    own_mq.start()
    own_iq.start()
    own_w.start()
    start_barrier(me_h, me_c)
    sends = []
    own_req = pltpu.make_async_copy(req.at[me_c], asked.at[me_c], loc.at[6])
    own_req.start()
    for o in range(1, NC):
        c = lax.rem(me_c + o, NC)
        s = remote(req.at[c], asked.at[me_c], r_send.at[o], r_recv.at[o], (me_h, c))
        s.start()
        sends.append(s)

    def peer_of(n, back=False):
        k = lax.rem(n, 4)
        dx = k + lax.div(k, 2) * (5 - 2 * k)
        dy = lax.div(n, 4)
        x = lax.div(me_h, 2) + (4 - dx if back else dx)
        y = lax.rem(me_h, 2) + dy
        return 2 * lax.rem(x, 4) + lax.rem(y, 2)

    def query_copy(n, back=False):
        h = peer_of(jnp.int32(n), back)
        rows = pl.ds(0, QROWS) if back else pl.ds(pl.multiple_of(h * QROWS, QROWS), QROWS)
        return remote(mq_hbm.at[rows], mq_ref.at[h if back else me_h], q_send.at[n], q_recv.at[n], (h, me_c))

    def send_queries(n):
        s = query_copy(n)
        s.start()
        sends.append(s)

    partner = me_h + 1 - 2 * lax.rem(me_h, 2)

    def relay_copy(n, back=False):
        h = peer_of(jnp.int32(n))
        rows = pl.ds(0, QROWS) if back else pl.ds(pl.multiple_of(h * QROWS, QROWS), QROWS)
        return remote(mq_hbm.at[rows], passing.at[n - 5], p_send.at[n - 5], p_recv.at[n - 5], (partner, me_c))

    def send_over(n):
        s = relay_copy(n)
        s.start()
        sends.append(s)

    def pass_on(n):
        relay_copy(n, True).wait_recv()
        dx = (1, 3, 2)[n - 5]
        to = lax.rem(me_h + 2 * dx, NH)
        s = remote(passing.at[n - 5], mq_ref.at[partner], q_send.at[n], q_recv.at[n], (to, me_c))
        s.start()
        sends.append(s)

    for o in range(1, NH):
        h = lax.rem(me_h + o, NH)
        rows = pl.ds(pl.multiple_of(h * QROWS, QROWS), QROWS)
        for src, dst, ss, rs in ((iq_hbm.at[rows], iq_ref, i_send, i_recv), (w_hbm, w_ref, w_send, w_recv)):
            s = remote(src, dst.at[me_h], ss.at[o], rs.at[o], (h, me_c))
            s.start()
            sends.append(s)
    for n in (1, 2, 3):
        send_queries(n)
    own_req.wait()
    for o in range(1, NC):
        c = lax.rem(me_c + NC - o, NC)
        remote(req.at[c], asked.at[c], r_send.at[o], r_recv.at[o], (me_h, c)).wait_recv()
    asked_out[...] = asked[:, 0, :]
    asked_copy = pltpu.make_async_copy(asked_out, asked_s, loc.at[7])
    asked_copy.start()
    for c in loads:
        c.wait()
    asked_copy.wait()
    first = iota((HALF, 128), 1) < 64
    lower = pl.ds(0, SPLIT)
    upper = pl.ds(SPLIT, SLOT - SPLIT)
    late = []
    for o in range(1, NC + 1):
        r = lax.rem(me_c + o, NC)
        b = asked_s[r, me_h]
        odd = jnp.full((HALF, 128), lax.bitwise_and(b, 1), jnp.int32) == 1
        pair = lax.shift_right_logical(b, 1)
        top = lat_v[pair, 0:HALF, :].astype(f32)
        bot = lat_v[pair, HALF:LAT, :].astype(f32)
        packed = jnp.where(
            first, jnp.where(odd, roll64(top), top), jnp.where(odd, bot, roll64(bot))
        ).astype(bf)
        keys = ik_v[b]
        if o < NC:
            stage[o, 0:BLK, :] = keys
            stage[o, BLK:SLOT, :] = packed
            s = remote(stage.at[o, lower], recv_a.at[me_c], b_send.at[o], b_recv.at[o], (me_h, r))
            s.start()
            sends.append(s)
            late.append(remote(stage.at[o, upper], recv_b.at[me_c], c_send.at[o], c_recv.at[o], (me_h, r)))
        else:
            recv_a[me_c, 0:BLK, :] = keys
            recv_a[me_c, BLK:SPLIT, :] = packed[0:FIRST]
            recv_b[me_c] = packed[FIRST:HALF]
    for s in late:
        s.start()
        sends.append(s)
    owners = [tab_s[1, me_h * SETB + j] for j in range(SETB)]

    own_w.wait()
    own_iq.wait()
    for o in range(1, NH):
        h = lax.rem(me_h + NH - o, NH)
        remote(iq_hbm.at[pl.ds(0, QROWS)], iq_ref.at[h], i_send.at[o], i_recv.at[o], (h, me_c)).wait_recv()
        remote(w_hbm, w_ref.at[h], w_send.at[o], w_recv.at[o], (h, me_c)).wait_recv()
    top = sel_ref.shape[0]
    meta_ref[...] = jnp.zeros((128, 128), f32)
    meta_ref[0:top, :] = sel_ref[...].astype(f32)
    meta_ref[top : top + 1, :] = len_ref[...].astype(f32)
    meta_ref[top + 1 : top + 2, :] = cot_ref[...]
    meta_ref[64 : 64 + IHEADS, :] = w_ref[...].reshape(IHEADS, 128)
    meta_ref[...] = meta_ref[...].T
    row = meta_ref[mine, :]
    wrow_ref[...] = row
    for i in range(top):
        selb_ref[i] = jnp.broadcast_to(row[:, i : i + 1], (QROWS, 128))
    limit = jnp.broadcast_to(row[:, top : top + 1], (QROWS, 128))
    cot = row[:, top + 1 : top + 2]
    for j in range(IHEADS):
        wb_ref[j] = jnp.broadcast_to(row[:, 64 + j : 65 + j], (QROWS, 128))
    lane = iota((QROWS, 128), 1)

    def mask_tile(i, carry):
        block = jnp.where(lane < 64, tab_s[0, 2 * i], tab_s[0, 2 * i + 1])
        block_f = block.astype(f32)
        hit = selb_ref[0] == block_f
        for q in range(1, top):
            hit = hit | (selb_ref[q] == block_f)
        token = (block * BLK + lax.bitwise_and(lane, 63)).astype(f32)
        ok = hit & (token < limit)
        cols = pl.ds(pl.multiple_of(i * 128, 128), 128)
        off = jnp.where(ok, 0.0, HIDDEN)
        bias_ref[:, cols] = off
        kt_ref[LAT:AUG, cols] = off.astype(bf)
        return carry

    lax.fori_loop(0, UNION // 128, mask_tile, 0)
    for h in range(NH):
        for k in range(8):
            iqr_ref[(h * 8 + k) * QROWS : (h * 8 + k + 1) * QROWS, :] = iq_ref[h, :, k * 128 : (k + 1) * 128]
    hot = jnp.where(iota((QROWS, QROWS), 0) == iota((QROWS, QROWS), 1), 1.0, 0.0).astype(bf)
    per = mq_ref.shape[2] // LAT
    for k in range(per):
        qt_ref[k * QROWS : (k + 1) * QROWS, LAT:AUG] = hot

    def merge(recv, skip, lo, hi):
        here = iota((hi - lo, 128), 1) < 64
        for i in range(SETB // 2):
            cols = slice(i * 128, (i + 1) * 128)
            a = recv[owners[2 * i], skip : skip + hi - lo, :].astype(f32)
            b = recv[owners[2 * i + 1], skip : skip + hi - lo, :].astype(f32)
            own[lo:hi, cols] = jnp.where(here, a, roll64(b)).astype(bf)
            own[HALF + lo : HALF + hi, cols] = jnp.where(here, roll64(a), b).astype(bf)

    def kt_of(h, start, rows):
        return kt_ref.at[pl.ds(start, rows), pl.ds(pl.multiple_of(h * SETT, SETT), SETT)]

    def ik_of(h, start, rows):
        return ik_ref.at[h, pl.ds(start, rows)]

    for o in range(1, NC):
        c = lax.rem(me_c + NC - o, NC)
        remote(stage.at[o, lower], recv_a.at[c], b_send.at[o], b_recv.at[o], (me_h, c)).wait_recv()
    merge(recv_a, BLK, 0, FIRST)
    for j in range(SETB):
        own_ik[j * BLK : (j + 1) * BLK, :] = recv_a[owners[j], 0:BLK, :]
    ga = gather_sets(
        [(own_ik, ik_of, 0, SETT), (own, kt_of, 0, FIRST), (own, kt_of, HALF, FIRST)],
        me_h, me_c, g_send, g_recv, loc_a,
    )
    next(ga)
    for o in range(1, NC):
        c = lax.rem(me_c + NC - o, NC)
        remote(stage.at[o, upper], recv_b.at[c], c_send.at[o], c_recv.at[o], (me_h, c)).wait_recv()
    merge(recv_b, 0, FIRST, HALF)
    next(ga)
    gb = gather_sets(
        [(own, kt_of, FIRST, HALF - FIRST), (own, kt_of, HALF + FIRST, HALF - FIRST)],
        me_h, me_c, h_send, h_recv, loc_b,
    )
    def index_scores(i):
        cols = pl.ds(pl.multiple_of(i * SETT, SETT), SETT)
        acc = jnp.zeros((QROWS, SETT), f32)
        for b in range(4):
            rows = slice(b * 256, (b + 1) * 256)
            pre = lax.dot_general(
                iqr_ref[rows, :], ik_ref[i], (((1,), (1,)), ((), ())), preferred_element_type=f32
            )
            for j in range(16):
                w = jnp.concatenate([wb_ref[b * 16 + j]] * (SETT // 128), axis=1)
                acc = acc + w * jnp.maximum(pre[j * QROWS : (j + 1) * QROWS, :], 0.0)
        idx_ref[:, cols] = acc + bias_ref[:, cols]

    flip = partner
    near_l, near_r, far = (lax.rem(me_h + o, NH) for o in (6, 2, 4))

    def other(h):
        return h + 1 - 2 * lax.rem(h, 2)

    next(gb)
    next(ga)
    next(gb)
    send_queries(4)
    for n in (5, 6, 7):
        send_over(n)
    index_scores(me_h)
    index_scores(flip)
    next(ga)
    next(gb)
    index_scores(near_l)
    index_scores(near_r)
    next(gb)
    for n in (5, 6, 7):
        pass_on(n)
    index_scores(other(near_l))
    index_scores(other(near_r))
    finish(ga)
    index_scores(far)
    index_scores(other(far))
    keys_out = pltpu.make_async_copy(ik_ref, ik_out, loc.at[5])
    keys_out.start()
    v = idx_ref[...]
    e = jnp.exp(v - jnp.max(v, axis=1, keepdims=True))
    idx_ref[...] = e / jnp.sum(e, axis=1, keepdims=True)
    tgt_ref[...] = jnp.zeros((QROWS, UNION), f32)
    finish(gb)

    def load_queries(g):
        for k in range(per):
            qt_ref[k * QROWS : (k + 1) * QROWS, 0:LAT] = mq_ref[g, :, k * LAT : (k + 1) * LAT]

    def arrive(n):
        query_copy(n, True).wait_recv()
        load_queries(peer_of(jnp.int32(n), True))

    def score_tile(t, s_ref, m_ref):
        cols = slice(t * TILE, (t + 1) * TILE)
        s = jnp.dot(qt_ref[...], kt_ref[:, cols], preferred_element_type=f32)
        s_ref[:, cols] = s
        m = jnp.maximum(s[:, 0:128], s[:, 128:256])
        m_ref[...] = m if t == 0 else jnp.maximum(m_ref[...], m)

    def soften(k, s_ref, m_ref):
        rows = slice(k * QROWS, (k + 1) * QROWS)
        high = jnp.max(m_ref[rows, :], axis=1, keepdims=True) * scale2
        high = jnp.broadcast_to(high, (QROWS, 128))
        den = jnp.zeros((QROWS, 128), f32)
        for t in range(UNION // 128):
            cols = slice(t * 128, (t + 1) * 128)
            p = jnp.exp2(s_ref[rows, cols] * scale2 - high)
            s_ref[rows, cols] = p
            den = den + p
        return jnp.broadcast_to(1.0 / jnp.sum(den, axis=1, keepdims=True), (QROWS, 128))

    def add_up(recips, s_ref, lo):
        for t in range(UNION // 128):
            cols = slice(t * 128, (t + 1) * 128)
            acc = tgt_ref[:, cols]
            for q, r in enumerate(recips):
                acc = acc + s_ref[(lo + q) * QROWS : (lo + q + 1) * QROWS, cols] * r
            tgt_ref[:, cols] = acc

    def both(s_ref, m_ref, next_s, next_m):
        recips = []
        for k in range(per):
            recips.append(soften(k, s_ref, m_ref))
            if next_s is not None:
                score_tile(k, next_s, next_m)
            if k % 8 == 7:
                add_up(recips, s_ref, k - 7)
                recips = []

    own_mq.wait()
    load_queries(me_h)
    for t in range(UNION // TILE):
        score_tile(t, sa_ref, ma_ref)

    def two_groups(i, carry):
        arrive(2 * i + 1)
        both(sa_ref, ma_ref, sb_ref, mb_ref)
        arrive(2 * i + 2)
        both(sb_ref, mb_ref, sa_ref, ma_ref)
        return carry

    lax.fori_loop(0, NH // 2 - 1, two_groups, 0)
    arrive(NH - 1)
    both(sa_ref, ma_ref, sb_ref, mb_ref)
    both(sb_ref, mb_ref, None, None)
    grad_ref[...] = cot * (idx_ref[...] - tgt_ref[...] * (1.0 / HEADS))
    keys_out.wait()
    for s in sends:
        s.wait_send()


def forward(tab, req, sel_t, lengths, cot, lat_t, index_key, main_query, index_query, weight_t):
    any_spec = pl.BlockSpec(memory_space=ANY)
    vm_spec = pl.BlockSpec(memory_space=VM)
    f32, bf, i32 = jnp.float32, jnp.bfloat16, jnp.int32
    rows = IHEADS * QROWS
    return pl.pallas_call(
        forward_kernel,
        name="forward",
        out_shape=(
            jax.ShapeDtypeStruct((QROWS, UNION), f32),
            jax.ShapeDtypeStruct((rows, 128), bf),
            jax.ShapeDtypeStruct((QROWS, 128), f32),
            jax.ShapeDtypeStruct((16, 128), i32),
            jax.ShapeDtypeStruct((NH, SETT, 128), bf),
        ),
        in_specs=[pl.BlockSpec(memory_space=pltpu.SMEM)] + [vm_spec] * 4 + [any_spec] * 5,
        out_specs=(vm_spec,) * 4 + (any_spec,),
        scratch_shapes=[
            VM((lat_t.shape[1] // 128, LAT, 128), bf),
            VM(index_key.shape, bf),
            VM((NC, SLOT, 128), bf),
            VM((NC, SPLIT, 128), bf),
            VM((NC, SLOT - SPLIT, 128), bf),
            VM((LAT, SETT), bf),
            VM((SETT, 128), bf),
            VM((NC, 8, 128), i32),
            pltpu.SMEM((16, 128), i32),
            VM((AUG, UNION), bf),
            VM((NH, SETT, 128), bf),
            VM((NH, QROWS, main_query.shape[1]), bf),
            VM((NH, QROWS, index_query.shape[1]), bf),
            VM((NH, 8, 128), f32),
            VM((3, QROWS, main_query.shape[1]), bf),
            VM((256, UNION), f32),
            VM((256, UNION), f32),
            VM((256, 128), f32),
            VM((256, 128), f32),
            VM((256, AUG), bf),
            VM((QROWS, UNION), f32),
            VM((QROWS, UNION), f32),
            VM((QROWS, UNION), f32),
            VM((128, 128), f32),
            VM((32, QROWS, 128), f32),
            VM((IHEADS, QROWS, 128), f32),
            DMA((NH,)), DMA((NH,)), DMA((NH,)), DMA((NH,)), DMA((NH,)), DMA((NH,)),
            DMA((NC,)), DMA((NC,)), DMA((NC,)), DMA((NC,)), DMA((NC,)), DMA((NC,)),
            DMA((27,)), DMA((27,)), DMA((18,)), DMA((18,)), DMA((9,)), DMA((3,)), DMA((3,)),
            DMA((lat_t.shape[1] // 128,)), DMA((3,)), DMA((3,)),
        ],
        compiler_params=pltpu.CompilerParams(
            collective_id=0, has_side_effects=True, vmem_limit_bytes=60 << 20
        ),
    )(tab, req, sel_t, lengths, cot, lat_t, index_key, main_query, index_query, weight_t)


HB = BLK // 2


def return_kernel(
    tab_s, grad_ref, iqr_ref, row_ref, ik_ref,
    iqg_out, wg_out, kg_out,
    ea_ref, eb_ref, wq_ref, wb_ref, wcol_ref, iqg_acc, iqt_ref, iqg, wg, ug,
    urecv, sums, slots, brecv, own, wrecv,
    u_send, u_recv, i_send, i_recv, w_send, w_recv, b_send, b_recv, g_send, g_recv, h_send, h_recv, loc, loc_a, loc_b,
):
    f32, bf = jnp.float32, jnp.bfloat16
    me_h = lax.axis_index("head")
    me_c = lax.axis_index("ctx")
    my_q = pl.ds(pl.multiple_of(me_h * QROWS, QROWS), QROWS)
    start_barrier(me_h, me_c)
    lane = iota((QROWS, 128), 1)
    row = row_ref[...]
    for j in range(IHEADS):
        wb_ref[j] = jnp.broadcast_to(row[:, 64 + j : 65 + j], (QROWS, 128))
    wcol_ref[...] = jnp.zeros(wcol_ref.shape, f32)
    iqg_acc[...] = jnp.zeros(iqg_acc.shape, f32)
    iqt_ref[...] = iqr_ref[...].T

    partner = me_h + 1 - 2 * lax.rem(me_h, 2)

    def whose(n):
        k = lax.rem(n + 1, 4)
        x = lax.div(me_h, 2) + k + lax.div(k, 2) * (5 - 2 * k)
        y = lax.rem(me_h, 2) + 1 - lax.div(n, 4)
        return 2 * lax.rem(x, 4) + lax.rem(y, 2)

    def edges(n, e_ref):
        h = whose(jnp.int32(n))
        grad = grad_ref[:, pl.ds(pl.multiple_of(h * SETT, SETT), SETT)]
        for b in range(4):
            pre_b = lax.dot_general(
                iqr_ref[b * 256 : (b + 1) * 256, :], ik_ref[h], (((1,), (1,)), ((), ())), preferred_element_type=f32
            )
            for q in range(16):
                j = b * 16 + q
                pre = pre_b[q * QROWS : (q + 1) * QROWS, :]
                w = jnp.concatenate([wb_ref[j]] * (SETT // 128), axis=1)
                part = jnp.maximum(pre, 0.0) * grad
                wcol_ref[j] = wcol_ref[j] + sum(part[:, t * 128 : (t + 1) * 128] for t in range(SETT // 128))
                e_ref[j * QROWS : (j + 1) * QROWS, :] = jnp.where(pre > 0.0, grad * w, 0.0).astype(bf)

    def products(n, e_ref):
        h = whose(jnp.int32(n))
        part = jnp.dot(iqt_ref[...], e_ref[...], preferred_element_type=f32).T.reshape(SETB, 2, HB, 128)
        for q in range(2):
            ug[q, n] = part[:, q].reshape(SETT // 2, 128)
        for b in range(4):
            rows = slice(b * 256, (b + 1) * 256)
            iqg_acc[rows, :] = iqg_acc[rows, :] + jnp.dot(e_ref[rows, :], ik_ref[h], preferred_element_type=f32)

    def sum_copy(q, n, to):
        return remote(ug.at[q, n], urecv.at[q, n], u_send.at[q * NH + n], u_recv.at[q * NH + n], (to, me_c))

    edges(0, ea_ref)

    def two_sets(i, carry):
        edges(2 * i + 1, eb_ref)
        products(2 * i, ea_ref)
        sum_copy(0, 2 * i, partner).start()
        edges(2 * i + 2, ea_ref)
        products(2 * i + 1, eb_ref)
        sum_copy(0, 2 * i + 1, partner).start()
        return carry

    lax.fori_loop(0, 2, two_sets, 0)
    for n in range(4):
        sum_copy(1, n, partner).start()
    edges(5, eb_ref)
    products(4, ea_ref)
    edges(6, ea_ref)
    products(5, eb_ref)
    edges(7, eb_ref)
    products(6, ea_ref)
    products(NH - 1, eb_ref)
    wrow = jnp.zeros((QROWS, 128), f32)
    for j in range(IHEADS):
        wrow = jnp.where(lane == j, jnp.sum(wcol_ref[j], axis=1, keepdims=True), wrow)
    wq_ref[...] = jnp.zeros((128, 128), f32)
    wq_ref[my_q, :] = wrow
    wg[...] = wq_ref[...].T[0:IHEADS, :].reshape(NH, 8, 128)
    for g in range(NH):
        for k in range(8):
            j = g * 8 + k
            iqg[g, :, k * 128 : (k + 1) * 128] = iqg_acc[j * QROWS : (j + 1) * QROWS, :]
    own_copies = [
        pltpu.make_async_copy(iqg.at[me_h], iqg_out.at[my_q], loc.at[2]),
        pltpu.make_async_copy(wg.at[me_h], wrecv.at[me_h], loc.at[3]),
    ]
    for c in own_copies:
        c.start()
    sends = [sum_copy(q, n, partner) for q in range(2) for n in range(4)]

    def pass_sums(q):
        for n in range(4, 7):
            sum_copy(q, n - 4, partner).wait_recv()
            ug[q, n] = ug[q, n] + urecv[q, n - 4]
            s = sum_copy(q, n, whose(jnp.int32(n)))
            s.start()
            sends.append(s)

    def take_sums(q):
        sum_copy(q, 3, partner).wait_recv()
        for n in range(4, 7):
            sum_copy(q, n, partner).wait_recv()

    def send_blocks(q):
        for j in range(SETB):
            rows = slice(j * HB, (j + 1) * HB)
            acc = ug[q, NH - 1, rows, :]
            for n in range(3, NH - 1):
                acc = acc + urecv[q, n, rows, :]
            sums[q, j] = acc
        sums[q, SETB] = jnp.zeros((HB, 128), jnp.float32)
        for o in range(1, NC + 1):
            c = lax.rem(me_c + o, NC)
            value = sums[q, tab_s[8 + me_h, c]]
            if o < NC:
                slots[q, o] = value
                s = remote(
                    slots.at[q, o], brecv.at[q, me_c], b_send.at[q * NC + o], b_recv.at[q * NC + o], (me_h, c)
                )
                s.start()
                sends.append(s)
            else:
                brecv[q, me_c] = value

    def take_blocks(q):
        for o in range(1, NC):
            c = lax.rem(me_c + NC - o, NC)
            remote(
                slots.at[q, o], brecv.at[q, c], b_send.at[q * NC + o], b_recv.at[q * NC + o], (me_h, c)
            ).wait_recv()
        for r in range(NC):
            at = (q * NC + r) * HB
            own[at : at + HB, :] = brecv[q, r].astype(own.dtype)

    rows = NC * HB

    def kg_of(h, start, count):
        return kg_out.at[h, pl.ds(start, count)]

    pass_sums(0)
    take_sums(0)
    send_blocks(0)
    pass_sums(1)
    take_blocks(0)
    ga = gather_sets([(own, kg_of, 0, rows)], me_h, me_c, g_send, g_recv, loc_a)
    next(ga)
    take_sums(1)
    send_blocks(1)
    for o in range(1, NH):
        h = lax.rem(me_h + o, NH)
        s = remote(iqg.at[h], iqg_out.at[my_q], i_send.at[o], i_recv.at[o], (h, me_c))
        s.start()
        sends.append(s)
        s = remote(wg.at[h], wrecv.at[me_h], w_send.at[o], w_recv.at[o], (h, me_c))
        s.start()
        sends.append(s)
    next(ga)
    take_blocks(1)
    gb = gather_sets([(own, kg_of, rows, rows)], me_h, me_c, h_send, h_recv, loc_b)
    next(gb)
    finish(ga, gb)
    for o in range(1, NH):
        h = lax.rem(me_h + NH - o, NH)
        remote(
            iqg.at[h], iqg_out.at[pl.ds(pl.multiple_of(h * QROWS, QROWS), QROWS)],
            i_send.at[o], i_recv.at[o], (h, me_c),
        ).wait_recv()
        remote(wg.at[h], wrecv.at[h], w_send.at[o], w_recv.at[o], (h, me_c)).wait_recv()
    for c in own_copies:
        c.wait()
    acc = wrecv[0]
    for h in range(1, NH):
        acc = acc + wrecv[h]
    wg_out[...] = acc
    for s in sends:
        s.wait_send()


SENT = jnp.bfloat16


def give_back(tab, grad, iqr, row, ik):
    f32, bf = jnp.float32, jnp.bfloat16
    any_spec = pl.BlockSpec(memory_space=ANY)
    vm_spec = pl.BlockSpec(memory_space=VM)
    rows = IHEADS * QROWS
    return pl.pallas_call(
        return_kernel,
        name="give_back",
        out_shape=(
            jax.ShapeDtypeStruct((NH * QROWS, 1024), f32),
            jax.ShapeDtypeStruct((8, 128), f32),
            jax.ShapeDtypeStruct((NH, NC * BLK, 128), SENT),
        ),
        in_specs=[pl.BlockSpec(memory_space=pltpu.SMEM)] + [vm_spec] * 4,
        out_specs=(any_spec, vm_spec, any_spec),
        scratch_shapes=[
            VM((rows, SETT), bf),
            VM((rows, SETT), bf),
            VM((128, 128), f32),
            VM((IHEADS, QROWS, 128), f32),
            VM((IHEADS, QROWS, 128), f32),
            VM((rows, 128), f32),
            VM((128, rows), bf),
            VM((NH, QROWS, 1024), f32),
            VM((NH, 8, 128), f32),
            VM((2, NH, SETT // 2, 128), f32),
            VM((2, NH - 1, SETT // 2, 128), f32),
            VM((2, SETB + 1, HB, 128), f32),
            VM((2, NC, HB, 128), f32),
            VM((2, NC, HB, 128), f32),
            VM((NC * BLK, 128), SENT),
            VM((NH, 8, 128), f32),
            DMA((2 * NH,)), DMA((2 * NH,)), DMA((NH,)), DMA((NH,)), DMA((NH,)), DMA((NH,)),
            DMA((2 * NC,)), DMA((2 * NC,)),
            DMA((9,)), DMA((9,)), DMA((9,)), DMA((9,)), DMA((4,)), DMA((1,)), DMA((1,)),
        ],
        compiler_params=pltpu.CompilerParams(
            collective_id=1, has_side_effects=True, vmem_limit_bytes=60 << 20
        ),
    )(tab, grad, iqr, row, ik)


def scatter_kernel(asked_s, kg_ref, out_ref):
    out_ref[...] = jnp.zeros(out_ref.shape, jnp.float32)

    def one(i, carry):
        h = lax.shift_right_logical(i, 4)
        r = lax.bitwise_and(i, 15)
        b = asked_s[r, h]
        for q in range(2):
            rows = pl.ds(pl.multiple_of(b * BLK + q * HB, HB), HB)
            part = kg_ref[h, pl.ds(pl.multiple_of((q * NC + r) * HB, HB), HB), :]
            out_ref[rows, :] = out_ref[rows, :] + part.astype(jnp.float32)
        return carry

    lax.fori_loop(0, NH * NC, one, 0, unroll=4)


def scatter(asked, kg, tokens):
    return pl.pallas_call(
        scatter_kernel,
        name="scatter",
        out_shape=jax.ShapeDtypeStruct((tokens, 128), jnp.float32),
        in_specs=[pl.BlockSpec(memory_space=pltpu.SMEM), pl.BlockSpec(memory_space=VM)],
        out_specs=pl.BlockSpec(memory_space=VM),
        compiler_params=pltpu.CompilerParams(vmem_limit_bytes=60 << 20),
    )(asked, kg)


def shards(main_query, latent, index_query, index_key, index_weight, selected, lengths, cotangent):
    sel_t = selected.T
    req, tab = make_plan(sel_t)
    grad, iqr, row, asked, ik = forward(
        tab, req, sel_t, lengths[None, :], cotangent[None, :],
        latent.T, index_key.reshape(-1, BLK, WIDTH), main_query, index_query, index_weight.T,
    )
    query_grad, weight_grad, kg = give_back(tab, grad, iqr, row, ik)
    key_grad = scatter(asked, kg, latent.shape[0])
    return query_grad, weight_grad.T, key_grad


def solution(mesh):
    return jax.shard_map(
        shards,
        mesh=mesh,
        in_specs=(
            P("ctx", "head"),
            P("ctx", None),
            P("ctx", "head"),
            P("ctx", None),
            P("ctx", "head"),
            P("ctx", None),
            P("ctx"),
            P("ctx"),
        ),
        out_specs=(P("ctx", "head"), P("ctx", "head"), P("ctx", None)),
        check_vma=False,
    )
```

```python
import functools
import math

import jax
import jax.numpy as jnp
from jax import lax
from jax.experimental import pallas as pl
from jax.experimental.pallas import tpu as pltpu
from jax.sharding import PartitionSpec as P

HEADS = 128
BLK = 64
POOL = 64
NH = 8
NC = 16
LAT = 576
WIDTH = 128
QROWS = 16
SETB = POOL // NH
SETT = SETB * BLK
HALF = LAT // 2
SLOT = HALF + BLK
UNION = POOL * BLK
IHEADS = 64

MESH = pl.DeviceIdType.MESH
ANY = pltpu.HBM
VM = pltpu.VMEM
DMA = pltpu.SemaphoreType.DMA

HIDDEN = -1e30
scale2 = 192.0 ** (-0.5) * math.log2(math.e)


def roll64(x):
    return pltpu.roll(x, 64, 1)


def start_barrier(me_h, me_c):
    barrier = pltpu.get_barrier_semaphore()
    for o in range(1, NH):
        pl.semaphore_signal(
            barrier, inc=1, device_id=(lax.rem(me_h + o, NH), me_c), device_id_type=MESH
        )
    for o in range(1, NC):
        pl.semaphore_signal(
            barrier, inc=1, device_id=(me_h, lax.rem(me_c + o, NC)), device_id_type=MESH
        )
    pl.semaphore_wait(barrier, NH + NC - 2)


def remote(src, dst, ssem, rsem, device):
    return pltpu.make_async_remote_copy(
        src_ref=src, dst_ref=dst, send_sem=ssem, recv_sem=rsem, device_id=device, device_id_type=MESH
    )


def gather_sets(pieces, me_h, me_c, ssem, rsem, lsem, between=None):
    right = (lax.rem(me_h + 2, NH), me_c)
    left = (lax.rem(me_h + 6, NH), me_c)
    flip = me_h + 1 - 2 * lax.rem(me_h, 2)
    partner = (flip, me_c)
    hl = lax.rem(me_h + 6, NH)
    hr = lax.rem(me_h + 2, NH)
    far = lax.rem(me_h + 4, NH)

    def flipped(h):
        return h + 1 - 2 * lax.rem(h, 2)

    count = len(pieces)
    sent = []

    def part(n, which):
        own, out, start, rows = pieces[n]
        half = rows // 32 * 16
        if which == 0:
            return start, rows
        return (start, half) if which == 1 else (start + half, rows - half)

    def copy(n, i, h, which, device, first=False):
        own, out, _, _ = pieces[n]
        start, rows = part(n, which)
        dst = out(h, start, rows)
        src = own.at[pl.ds(start, rows)] if first else dst
        return remote(src, dst, ssem.at[i * count + n], rsem.at[i * count + n], device)

    def go(i, h, which, device, first=False):
        for n in range(count):
            c = copy(n, i, h, which, device, first)
            c.start()
            sent.append(c)

    def wait(i, h, which, device):
        for n in range(count):
            copy(n, i, h, which, device).wait_recv()

    locals_ = [
        pltpu.make_async_copy(own.at[pl.ds(start, rows)], out(me_h, start, rows), lsem.at[n])
        for n, (own, out, start, rows) in enumerate(pieces)
    ]
    for c in locals_:
        c.start()
    go(0, me_h, 0, partner, True)
    go(1, me_h, 0, right, True)
    go(2, me_h, 0, left, True)
    yield
    for c in locals_:
        c.wait()
    wait(0, flip, 0, partner)
    go(3, flip, 0, right)
    go(4, flip, 0, left)
    yield
    wait(1, hl, 0, right)
    go(5, hl, 1, right)
    wait(2, hr, 0, left)
    go(6, hr, 2, left)
    yield
    wait(3, flipped(hl), 0, right)
    go(7, flipped(hl), 1, right)
    wait(4, flipped(hr), 0, left)
    go(8, flipped(hr), 2, left)
    yield
    wait(5, far, 1, right)
    wait(6, far, 2, left)
    wait(7, flipped(far), 1, right)
    wait(8, flipped(far), 2, left)
    for c in sent:
        c.wait_send()


def finish(*stages):
    left = list(stages)
    while left:
        for g in list(left):
            if next(g, 0) == 0:
                left.remove(g)


def iota(shape, dim):
    return lax.broadcasted_iota(jnp.int32, shape, dim)


def plan(sel, req_ref, tab_ref):
    hi = lax.shift_right_logical(sel, 7)
    lo = lax.bitwise_and(sel, 127)
    rows = sel.shape[0]
    owner_hot = jnp.concatenate(
        [jnp.where(iota((NC, 128), 0) == hi[i : i + 1, :], 1.0, 0.0) for i in range(rows)], axis=1
    ).astype(jnp.bfloat16)
    local_hot = jnp.concatenate(
        [jnp.where(iota((128, 128), 0) == lo[i : i + 1, :], 1.0, 0.0) for i in range(rows)], axis=1
    ).astype(jnp.bfloat16)
    counts = lax.dot_general(
        owner_hot, local_hot, (((1,), (1,)), ((), ())), preferred_element_type=jnp.float32
    )
    present = jnp.where(counts > 0.5, 1.0, 0.0)
    upper = jnp.where(iota((128, 128), 0) <= iota((128, 128), 1), 1.0, 0.0).astype(jnp.bfloat16)
    rank = jnp.dot(present.astype(jnp.bfloat16), upper, preferred_element_type=jnp.float32)
    total = rank[:, 127:128]
    lane = iota((NC, 128), 1)
    sub = iota((NC, 128), 0)
    spread = jnp.sum(jnp.where(lane == sub, total, 0.0), axis=0, keepdims=True)
    before = jnp.sum(jnp.where(lane < sub, jnp.broadcast_to(spread, (NC, 128)), 0.0), axis=1, keepdims=True)
    pos = (before + rank - 1.0).astype(jnp.int32)
    slot = lax.bitwise_and(pos, 7)
    step = lax.shift_right_logical(pos, 3).astype(jnp.float32)
    lane_f = lane.astype(jnp.float32)
    there = present > 0.5
    req = jnp.zeros((NC, 128), jnp.float32)
    ids = jnp.zeros((NC, 128), jnp.float32)
    owners = jnp.zeros((NC, 128), jnp.float32)
    sub_f = sub.astype(jnp.float32)
    for k in range(NH):
        hit = there & (slot == k)
        local = jnp.sum(jnp.where(hit, lane_f, 0.0), axis=1, keepdims=True)
        at = jnp.sum(jnp.where(hit, step, 0.0), axis=1, keepdims=True)
        has = jnp.sum(jnp.where(hit, 1.0, 0.0), axis=1, keepdims=True)
        req = jnp.where(lane == k, local, req)
        here = jnp.where(lane_f == at + float(SETB * k), has, 0.0)
        ids = ids + here * (sub_f * 128.0 + local)
        owners = owners + here * sub_f
        back = jnp.where(has > 0.5, at, float(SETB))
        row = jnp.sum(jnp.where(lane == sub, back, 0.0), axis=0, keepdims=True)
        tab_ref[8 + k : 9 + k, :] = row.astype(jnp.int32)
    tab_ref[0:1, :] = jnp.sum(ids, axis=0, keepdims=True).astype(jnp.int32)
    tab_ref[1:2, :] = jnp.sum(owners, axis=0, keepdims=True).astype(jnp.int32)
    tab_ref[2:8, :] = jnp.zeros((6, 128), jnp.int32)
    req_ref[...] = jnp.broadcast_to(req.astype(jnp.int32)[:, None, :], (NC, 8, 128))


def plan_kernel(sel_ref, req_ref, tab_ref):
    plan(sel_ref[...], req_ref, tab_ref)


def make_plan(sel_t):
    vm_spec = pl.BlockSpec(memory_space=VM)
    return pl.pallas_call(
        plan_kernel,
        name="plan",
        out_shape=(
            jax.ShapeDtypeStruct((NC, 8, 128), jnp.int32),
            jax.ShapeDtypeStruct((16, 128), jnp.int32),
        ),
        in_specs=[vm_spec],
        out_specs=(vm_spec, vm_spec),
        compiler_params=pltpu.CompilerParams(vmem_limit_bytes=32 << 20),
    )(sel_t)


SPLIT = SLOT // 2
FIRST = SPLIT - BLK
AUG = LAT + QROWS
TILE = 256


def forward_kernel(
    tab_s, req, sel_ref, len_ref, cot_ref, lat_hbm, ik_hbm, mq_hbm, iq_hbm, w_hbm,
    grad_ref, iqr_ref, wrow_ref, asked_out, ik_out,
    lat_v, ik_v, stage, recv_a, recv_b, own, own_ik, asked, asked_s,
    kt_ref, ik_ref, mq_ref, iq_ref, w_ref, passing,
    sa_ref, sb_ref, ma_ref, mb_ref, qt_ref, bias_ref, tgt_ref, idx_ref, meta_ref, selb_ref, wb_ref,
    q_send, q_recv, i_send, i_recv, w_send, w_recv, r_send, r_recv, b_send, b_recv, c_send, c_recv,
    g_send, g_recv, h_send, h_recv, loc, loc_a, loc_b, l_sem, p_send, p_recv,
):
    f32, bf = jnp.float32, jnp.bfloat16
    me_h = lax.axis_index("head")
    me_c = lax.axis_index("ctx")
    loads = [pltpu.make_async_copy(ik_hbm, ik_v, loc.at[1])] + [
        pltpu.make_async_copy(lat_hbm.at[:, pl.ds(i * 128, 128)], lat_v.at[i], l_sem.at[i])
        for i in range(lat_v.shape[0])
    ]
    for c in loads:
        c.start()
    mine = pl.ds(pl.multiple_of(me_h * QROWS, QROWS), QROWS)
    own_mq = pltpu.make_async_copy(mq_hbm.at[mine], mq_ref.at[me_h], loc.at[2])
    own_iq = pltpu.make_async_copy(iq_hbm.at[mine], iq_ref.at[me_h], loc.at[3])
    own_w = pltpu.make_async_copy(w_hbm, w_ref.at[me_h], loc.at[4])
    own_mq.start()
    own_iq.start()
    own_w.start()
    start_barrier(me_h, me_c)
    sends = []
    own_req = pltpu.make_async_copy(req.at[me_c], asked.at[me_c], loc.at[6])
    own_req.start()
    for o in range(1, NC):
        c = lax.rem(me_c + o, NC)
        s = remote(req.at[c], asked.at[me_c], r_send.at[o], r_recv.at[o], (me_h, c))
        s.start()
        sends.append(s)

    def peer_of(n, back=False):
        k = lax.rem(n, 4)
        dx = k + lax.div(k, 2) * (5 - 2 * k)
        dy = lax.div(n, 4)
        x = lax.div(me_h, 2) + (4 - dx if back else dx)
        y = lax.rem(me_h, 2) + dy
        return 2 * lax.rem(x, 4) + lax.rem(y, 2)

    def query_copy(n, back=False):
        h = peer_of(jnp.int32(n), back)
        rows = pl.ds(0, QROWS) if back else pl.ds(pl.multiple_of(h * QROWS, QROWS), QROWS)
        return remote(mq_hbm.at[rows], mq_ref.at[h if back else me_h], q_send.at[n], q_recv.at[n], (h, me_c))

    def send_queries(n):
        s = query_copy(n)
        s.start()
        sends.append(s)

    partner = me_h + 1 - 2 * lax.rem(me_h, 2)

    def relay_copy(n, back=False):
        h = peer_of(jnp.int32(n))
        rows = pl.ds(0, QROWS) if back else pl.ds(pl.multiple_of(h * QROWS, QROWS), QROWS)
        return remote(mq_hbm.at[rows], passing.at[n - 5], p_send.at[n - 5], p_recv.at[n - 5], (partner, me_c))

    def send_over(n):
        s = relay_copy(n)
        s.start()
        sends.append(s)

    def pass_on(n):
        relay_copy(n, True).wait_recv()
        dx = (1, 3, 2)[n - 5]
        to = lax.rem(me_h + 2 * dx, NH)
        s = remote(passing.at[n - 5], mq_ref.at[partner], q_send.at[n], q_recv.at[n], (to, me_c))
        s.start()
        sends.append(s)

    other_row = []
    for o in range(1, NH):
        h = lax.rem(me_h + o, NH)
        rows = pl.ds(pl.multiple_of(h * QROWS, QROWS), QROWS)
        s = remote(w_hbm, w_ref.at[me_h], w_send.at[o], w_recv.at[o], (h, me_c))
        s.start()
        sends.append(s)
        s = remote(iq_hbm.at[rows], iq_ref.at[me_h], i_send.at[o], i_recv.at[o], (h, me_c))
        sends.append(s)
        if o % 2 == 0:
            s.start()
        else:
            other_row.append(s)
    for n in (1, 2, 3):
        send_queries(n)
    own_req.wait()
    for o in range(1, NC):
        c = lax.rem(me_c + NC - o, NC)
        remote(req.at[c], asked.at[c], r_send.at[o], r_recv.at[o], (me_h, c)).wait_recv()
    asked_out[...] = asked[:, 0, :]
    asked_copy = pltpu.make_async_copy(asked_out, asked_s, loc.at[7])
    asked_copy.start()
    for c in loads:
        c.wait()
    asked_copy.wait()
    first = iota((HALF, 128), 1) < 64
    lower = pl.ds(0, SPLIT)
    upper = pl.ds(SPLIT, SLOT - SPLIT)
    late = []
    for o in range(1, NC + 1):
        r = lax.rem(me_c + o, NC)
        b = asked_s[r, me_h]
        odd = jnp.full((HALF, 128), lax.bitwise_and(b, 1), jnp.int32) == 1
        pair = lax.shift_right_logical(b, 1)
        top = lat_v[pair, 0:HALF, :].astype(f32)
        bot = lat_v[pair, HALF:LAT, :].astype(f32)
        packed = jnp.where(
            first, jnp.where(odd, roll64(top), top), jnp.where(odd, bot, roll64(bot))
        ).astype(bf)
        keys = ik_v[b]
        if o < NC:
            stage[o, 0:BLK, :] = keys
            stage[o, BLK:SLOT, :] = packed
            s = remote(stage.at[o, lower], recv_a.at[me_c], b_send.at[o], b_recv.at[o], (me_h, r))
            s.start()
            sends.append(s)
            late.append(remote(stage.at[o, upper], recv_b.at[me_c], c_send.at[o], c_recv.at[o], (me_h, r)))
        else:
            recv_a[me_c, 0:BLK, :] = keys
            recv_a[me_c, BLK:SPLIT, :] = packed[0:FIRST]
            recv_b[me_c] = packed[FIRST:HALF]
    for s in late:
        s.start()
        sends.append(s)
    for s in other_row:
        s.start()
    owners = [tab_s[1, me_h * SETB + j] for j in range(SETB)]

    own_w.wait()
    for o in range(1, NH):
        h = lax.rem(me_h + NH - o, NH)
        remote(w_hbm, w_ref.at[h], w_send.at[o], w_recv.at[o], (h, me_c)).wait_recv()
    top = sel_ref.shape[0]
    meta_ref[...] = jnp.zeros((128, 128), f32)
    meta_ref[0:top, :] = sel_ref[...].astype(f32)
    meta_ref[top : top + 1, :] = len_ref[...].astype(f32)
    meta_ref[top + 1 : top + 2, :] = cot_ref[...]
    meta_ref[64 : 64 + IHEADS, :] = w_ref[...].reshape(IHEADS, 128)
    meta_ref[...] = meta_ref[...].T
    row = meta_ref[mine, :]
    wrow_ref[...] = row
    for i in range(top):
        selb_ref[i] = jnp.broadcast_to(row[:, i : i + 1], (QROWS, 128))
    limit = jnp.broadcast_to(row[:, top : top + 1], (QROWS, 128))
    cot = row[:, top + 1 : top + 2]
    for j in range(IHEADS):
        wb_ref[j] = jnp.broadcast_to(row[:, 64 + j : 65 + j], (QROWS, 128))
    lane = iota((QROWS, 128), 1)

    def mask_tile(i, carry):
        block = jnp.where(lane < 64, tab_s[0, 2 * i], tab_s[0, 2 * i + 1])
        block_f = block.astype(f32)
        hit = selb_ref[0] == block_f
        for q in range(1, top):
            hit = hit | (selb_ref[q] == block_f)
        token = (block * BLK + lax.bitwise_and(lane, 63)).astype(f32)
        ok = hit & (token < limit)
        cols = pl.ds(pl.multiple_of(i * 128, 128), 128)
        off = jnp.where(ok, 0.0, HIDDEN)
        bias_ref[:, cols] = off
        kt_ref[LAT:AUG, cols] = off.astype(bf)
        return carry

    lax.fori_loop(0, UNION // 128, mask_tile, 0)
    own_iq.wait()
    for o in range(1, NH):
        h = lax.rem(me_h + NH - o, NH)
        remote(iq_hbm.at[pl.ds(0, QROWS)], iq_ref.at[h], i_send.at[o], i_recv.at[o], (h, me_c)).wait_recv()
    for h in range(NH):
        for k in range(8):
            iqr_ref[(h * 8 + k) * QROWS : (h * 8 + k + 1) * QROWS, :] = iq_ref[h, :, k * 128 : (k + 1) * 128]
    hot = jnp.where(iota((QROWS, QROWS), 0) == iota((QROWS, QROWS), 1), 1.0, 0.0).astype(bf)
    per = mq_ref.shape[2] // LAT
    for k in range(per):
        qt_ref[k * QROWS : (k + 1) * QROWS, LAT:AUG] = hot

    def merge(recv, skip, lo, hi):
        here = iota((hi - lo, 128), 1) < 64
        for i in range(SETB // 2):
            cols = slice(i * 128, (i + 1) * 128)
            a = recv[owners[2 * i], skip : skip + hi - lo, :].astype(f32)
            b = recv[owners[2 * i + 1], skip : skip + hi - lo, :].astype(f32)
            own[lo:hi, cols] = jnp.where(here, a, roll64(b)).astype(bf)
            own[HALF + lo : HALF + hi, cols] = jnp.where(here, roll64(a), b).astype(bf)

    def kt_of(h, start, rows):
        return kt_ref.at[pl.ds(start, rows), pl.ds(pl.multiple_of(h * SETT, SETT), SETT)]

    def ik_of(h, start, rows):
        return ik_ref.at[h, pl.ds(start, rows)]

    for o in range(1, NC):
        c = lax.rem(me_c + NC - o, NC)
        remote(stage.at[o, lower], recv_a.at[c], b_send.at[o], b_recv.at[o], (me_h, c)).wait_recv()
    merge(recv_a, BLK, 0, FIRST)
    for j in range(SETB):
        own_ik[j * BLK : (j + 1) * BLK, :] = recv_a[owners[j], 0:BLK, :]
    ga = gather_sets(
        [(own_ik, ik_of, 0, SETT), (own, kt_of, 0, FIRST), (own, kt_of, HALF, FIRST)],
        me_h, me_c, g_send, g_recv, loc_a,
    )
    next(ga)
    for o in range(1, NC):
        c = lax.rem(me_c + NC - o, NC)
        remote(stage.at[o, upper], recv_b.at[c], c_send.at[o], c_recv.at[o], (me_h, c)).wait_recv()
    merge(recv_b, 0, FIRST, HALF)
    next(ga)
    gb = gather_sets(
        [(own, kt_of, FIRST, HALF - FIRST), (own, kt_of, HALF + FIRST, HALF - FIRST)],
        me_h, me_c, h_send, h_recv, loc_b,
    )
    def index_scores(i):
        cols = pl.ds(pl.multiple_of(i * SETT, SETT), SETT)
        acc = jnp.zeros((QROWS, SETT), f32)
        for b in range(4):
            rows = slice(b * 256, (b + 1) * 256)
            pre = lax.dot_general(
                iqr_ref[rows, :], ik_ref[i], (((1,), (1,)), ((), ())), preferred_element_type=f32
            )
            for j in range(16):
                w = jnp.concatenate([wb_ref[b * 16 + j]] * (SETT // 128), axis=1)
                acc = acc + w * jnp.maximum(pre[j * QROWS : (j + 1) * QROWS, :], 0.0)
        idx_ref[:, cols] = acc + bias_ref[:, cols]

    flip = partner
    near_l, near_r, far = (lax.rem(me_h + o, NH) for o in (6, 2, 4))

    def other(h):
        return h + 1 - 2 * lax.rem(h, 2)

    next(gb)
    next(ga)
    next(gb)
    send_queries(4)
    for n in (5, 6, 7):
        send_over(n)
    index_scores(me_h)
    index_scores(flip)
    next(ga)
    next(gb)
    index_scores(near_l)
    index_scores(near_r)
    next(gb)
    for n in (5, 6, 7):
        pass_on(n)
    index_scores(other(near_l))
    index_scores(other(near_r))
    finish(ga)
    index_scores(far)
    index_scores(other(far))
    keys_out = pltpu.make_async_copy(ik_ref, ik_out, loc.at[5])
    keys_out.start()
    v = idx_ref[...]
    e = jnp.exp(v - jnp.max(v, axis=1, keepdims=True))
    idx_ref[...] = e / jnp.sum(e, axis=1, keepdims=True)
    tgt_ref[...] = jnp.zeros((QROWS, UNION), f32)
    finish(gb)

    def load_queries(g):
        for k in range(per):
            qt_ref[k * QROWS : (k + 1) * QROWS, 0:LAT] = mq_ref[g, :, k * LAT : (k + 1) * LAT]

    def arrive(n):
        query_copy(n, True).wait_recv()
        load_queries(peer_of(jnp.int32(n), True))

    def score_tile(t, s_ref, m_ref):
        cols = slice(t * TILE, (t + 1) * TILE)
        s = jnp.dot(qt_ref[...], kt_ref[:, cols], preferred_element_type=f32)
        s_ref[:, cols] = s
        m = jnp.maximum(s[:, 0:128], s[:, 128:256])
        m_ref[...] = m if t == 0 else jnp.maximum(m_ref[...], m)

    def soften(k, s_ref, m_ref):
        rows = slice(k * QROWS, (k + 1) * QROWS)
        high = jnp.max(m_ref[rows, :], axis=1, keepdims=True) * scale2
        high = jnp.broadcast_to(high, (QROWS, 128))
        den = jnp.zeros((QROWS, 128), f32)
        for t in range(UNION // 128):
            cols = slice(t * 128, (t + 1) * 128)
            p = jnp.exp2(s_ref[rows, cols] * scale2 - high)
            s_ref[rows, cols] = p
            den = den + p
        return jnp.broadcast_to(1.0 / jnp.sum(den, axis=1, keepdims=True), (QROWS, 128))

    def add_up(recips, s_ref, lo):
        for t in range(UNION // 128):
            cols = slice(t * 128, (t + 1) * 128)
            acc = tgt_ref[:, cols]
            for q, r in enumerate(recips):
                acc = acc + s_ref[(lo + q) * QROWS : (lo + q + 1) * QROWS, cols] * r
            tgt_ref[:, cols] = acc

    def both(s_ref, m_ref, next_s, next_m):
        recips = []
        for k in range(per):
            recips.append(soften(k, s_ref, m_ref))
            if next_s is not None:
                score_tile(k, next_s, next_m)
            if k % 8 == 7:
                add_up(recips, s_ref, k - 7)
                recips = []

    own_mq.wait()
    load_queries(me_h)
    for t in range(UNION // TILE):
        score_tile(t, sa_ref, ma_ref)

    def two_groups(i, carry):
        arrive(2 * i + 1)
        both(sa_ref, ma_ref, sb_ref, mb_ref)
        arrive(2 * i + 2)
        both(sb_ref, mb_ref, sa_ref, ma_ref)
        return carry

    lax.fori_loop(0, NH // 2 - 1, two_groups, 0)
    arrive(NH - 1)
    both(sa_ref, ma_ref, sb_ref, mb_ref)
    both(sb_ref, mb_ref, None, None)
    grad_ref[...] = cot * (idx_ref[...] - tgt_ref[...] * (1.0 / HEADS))
    keys_out.wait()
    for s in sends:
        s.wait_send()


def forward(tab, req, sel_t, lengths, cot, lat_t, index_key, main_query, index_query, weight_t):
    any_spec = pl.BlockSpec(memory_space=ANY)
    vm_spec = pl.BlockSpec(memory_space=VM)
    f32, bf, i32 = jnp.float32, jnp.bfloat16, jnp.int32
    rows = IHEADS * QROWS
    return pl.pallas_call(
        forward_kernel,
        name="forward",
        out_shape=(
            jax.ShapeDtypeStruct((QROWS, UNION), f32),
            jax.ShapeDtypeStruct((rows, 128), bf),
            jax.ShapeDtypeStruct((QROWS, 128), f32),
            jax.ShapeDtypeStruct((16, 128), i32),
            jax.ShapeDtypeStruct((NH, SETT, 128), bf),
        ),
        in_specs=[pl.BlockSpec(memory_space=pltpu.SMEM)] + [vm_spec] * 4 + [any_spec] * 5,
        out_specs=(vm_spec,) * 4 + (any_spec,),
        scratch_shapes=[
            VM((lat_t.shape[1] // 128, LAT, 128), bf),
            VM(index_key.shape, bf),
            VM((NC, SLOT, 128), bf),
            VM((NC, SPLIT, 128), bf),
            VM((NC, SLOT - SPLIT, 128), bf),
            VM((LAT, SETT), bf),
            VM((SETT, 128), bf),
            VM((NC, 8, 128), i32),
            pltpu.SMEM((16, 128), i32),
            VM((AUG, UNION), bf),
            VM((NH, SETT, 128), bf),
            VM((NH, QROWS, main_query.shape[1]), bf),
            VM((NH, QROWS, index_query.shape[1]), bf),
            VM((NH, 8, 128), f32),
            VM((3, QROWS, main_query.shape[1]), bf),
            VM((256, UNION), f32),
            VM((256, UNION), f32),
            VM((256, 128), f32),
            VM((256, 128), f32),
            VM((256, AUG), bf),
            VM((QROWS, UNION), f32),
            VM((QROWS, UNION), f32),
            VM((QROWS, UNION), f32),
            VM((128, 128), f32),
            VM((32, QROWS, 128), f32),
            VM((IHEADS, QROWS, 128), f32),
            DMA((NH,)), DMA((NH,)), DMA((NH,)), DMA((NH,)), DMA((NH,)), DMA((NH,)),
            DMA((NC,)), DMA((NC,)), DMA((NC,)), DMA((NC,)), DMA((NC,)), DMA((NC,)),
            DMA((27,)), DMA((27,)), DMA((18,)), DMA((18,)), DMA((9,)), DMA((3,)), DMA((3,)),
            DMA((lat_t.shape[1] // 128,)), DMA((3,)), DMA((3,)),
        ],
        compiler_params=pltpu.CompilerParams(
            collective_id=0, has_side_effects=True, vmem_limit_bytes=60 << 20
        ),
    )(tab, req, sel_t, lengths, cot, lat_t, index_key, main_query, index_query, weight_t)


HB = BLK // 2


def return_kernel(
    tab_s, grad_ref, iqr_ref, row_ref, ik_ref,
    iqg_out, wg_out, kg_out,
    ea_ref, eb_ref, wq_ref, wb_ref, wcol_ref, iqg_acc, iqt_ref, iqg, wg, ug,
    urecv, sums, slots, brecv, own, wrecv,
    u_send, u_recv, i_send, i_recv, w_send, w_recv, b_send, b_recv, g_send, g_recv, h_send, h_recv, loc, loc_a, loc_b,
):
    f32, bf = jnp.float32, jnp.bfloat16
    me_h = lax.axis_index("head")
    me_c = lax.axis_index("ctx")
    my_q = pl.ds(pl.multiple_of(me_h * QROWS, QROWS), QROWS)
    start_barrier(me_h, me_c)
    lane = iota((QROWS, 128), 1)
    row = row_ref[...]
    for j in range(IHEADS):
        wb_ref[j] = jnp.broadcast_to(row[:, 64 + j : 65 + j], (QROWS, 128))
    wcol_ref[...] = jnp.zeros(wcol_ref.shape, f32)
    iqg_acc[...] = jnp.zeros(iqg_acc.shape, f32)
    iqt_ref[...] = iqr_ref[...].T

    partner = me_h + 1 - 2 * lax.rem(me_h, 2)

    def whose(n):
        k = lax.rem(n + 1, 4)
        x = lax.div(me_h, 2) + k + lax.div(k, 2) * (5 - 2 * k)
        y = lax.rem(me_h, 2) + 1 - lax.div(n, 4)
        return 2 * lax.rem(x, 4) + lax.rem(y, 2)

    def edges(n, e_ref):
        h = whose(jnp.int32(n))
        grad = grad_ref[:, pl.ds(pl.multiple_of(h * SETT, SETT), SETT)]
        for b in range(4):
            pre_b = lax.dot_general(
                iqr_ref[b * 256 : (b + 1) * 256, :], ik_ref[h], (((1,), (1,)), ((), ())), preferred_element_type=f32
            )
            for q in range(16):
                j = b * 16 + q
                pre = pre_b[q * QROWS : (q + 1) * QROWS, :]
                w = jnp.concatenate([wb_ref[j]] * (SETT // 128), axis=1)
                part = jnp.maximum(pre, 0.0) * grad
                wcol_ref[j] = wcol_ref[j] + sum(part[:, t * 128 : (t + 1) * 128] for t in range(SETT // 128))
                e_ref[j * QROWS : (j + 1) * QROWS, :] = jnp.where(pre > 0.0, grad * w, 0.0).astype(bf)

    def products(n, e_ref):
        h = whose(jnp.int32(n))
        part = jnp.dot(iqt_ref[...], e_ref[...], preferred_element_type=f32).T.reshape(SETB, 2, HB, 128)
        for q in range(2):
            ug[q, n] = part[:, q].reshape(SETT // 2, 128)
        for b in range(4):
            rows = slice(b * 256, (b + 1) * 256)
            iqg_acc[rows, :] = iqg_acc[rows, :] + jnp.dot(e_ref[rows, :], ik_ref[h], preferred_element_type=f32)

    def sum_copy(q, n, to):
        return remote(ug.at[q, n], urecv.at[q, n], u_send.at[q * NH + n], u_recv.at[q * NH + n], (to, me_c))

    edges(0, ea_ref)

    def two_sets(i, carry):
        edges(2 * i + 1, eb_ref)
        products(2 * i, ea_ref)
        sum_copy(0, 2 * i, partner).start()
        edges(2 * i + 2, ea_ref)
        products(2 * i + 1, eb_ref)
        sum_copy(0, 2 * i + 1, partner).start()
        return carry

    lax.fori_loop(0, 2, two_sets, 0)
    for n in range(4):
        sum_copy(1, n, partner).start()
    edges(5, eb_ref)
    products(4, ea_ref)
    edges(6, ea_ref)
    products(5, eb_ref)
    edges(7, eb_ref)
    products(6, ea_ref)
    products(NH - 1, eb_ref)
    wrow = jnp.zeros((QROWS, 128), f32)
    for j in range(IHEADS):
        wrow = jnp.where(lane == j, jnp.sum(wcol_ref[j], axis=1, keepdims=True), wrow)
    wq_ref[...] = jnp.zeros((128, 128), f32)
    wq_ref[my_q, :] = wrow
    wg[...] = wq_ref[...].T[0:IHEADS, :].reshape(NH, 8, 128)
    for g in range(NH):
        for k in range(8):
            j = g * 8 + k
            iqg[g, :, k * 128 : (k + 1) * 128] = iqg_acc[j * QROWS : (j + 1) * QROWS, :]
    own_copies = [
        pltpu.make_async_copy(iqg.at[me_h], iqg_out.at[my_q], loc.at[2]),
        pltpu.make_async_copy(wg.at[me_h], wrecv.at[me_h], loc.at[3]),
    ]
    for c in own_copies:
        c.start()
    sends = [sum_copy(q, n, partner) for q in range(2) for n in range(4)]

    def pass_sums(q):
        for n in range(4, 7):
            sum_copy(q, n - 4, partner).wait_recv()
            ug[q, n] = ug[q, n] + urecv[q, n - 4]
            s = sum_copy(q, n, whose(jnp.int32(n)))
            s.start()
            sends.append(s)

    def take_sums(q):
        sum_copy(q, 3, partner).wait_recv()
        for n in range(4, 7):
            sum_copy(q, n, partner).wait_recv()

    def send_blocks(q):
        for j in range(SETB):
            rows = slice(j * HB, (j + 1) * HB)
            acc = ug[q, NH - 1, rows, :]
            for n in range(3, NH - 1):
                acc = acc + urecv[q, n, rows, :]
            sums[q, j] = acc
        sums[q, SETB] = jnp.zeros((HB, 128), jnp.float32)
        for o in range(1, NC + 1):
            c = lax.rem(me_c + o, NC)
            value = sums[q, tab_s[8 + me_h, c]]
            if o < NC:
                slots[q, o] = value
                s = remote(
                    slots.at[q, o], brecv.at[q, me_c], b_send.at[q * NC + o], b_recv.at[q * NC + o], (me_h, c)
                )
                s.start()
                sends.append(s)
            else:
                brecv[q, me_c] = value

    def take_blocks(q):
        for o in range(1, NC):
            c = lax.rem(me_c + NC - o, NC)
            remote(
                slots.at[q, o], brecv.at[q, c], b_send.at[q * NC + o], b_recv.at[q * NC + o], (me_h, c)
            ).wait_recv()
        for r in range(NC):
            at = (q * NC + r) * HB
            own[at : at + HB, :] = brecv[q, r].astype(own.dtype)

    rows = NC * HB

    def kg_of(h, start, count):
        return kg_out.at[h, pl.ds(start, count)]

    pass_sums(0)
    take_sums(0)
    send_blocks(0)
    pass_sums(1)
    take_blocks(0)
    ga = gather_sets([(own, kg_of, 0, rows)], me_h, me_c, g_send, g_recv, loc_a)
    next(ga)
    take_sums(1)
    send_blocks(1)
    for o in range(1, NH):
        h = lax.rem(me_h + o, NH)
        s = remote(iqg.at[h], iqg_out.at[my_q], i_send.at[o], i_recv.at[o], (h, me_c))
        s.start()
        sends.append(s)
        s = remote(wg.at[h], wrecv.at[me_h], w_send.at[o], w_recv.at[o], (h, me_c))
        s.start()
        sends.append(s)
    next(ga)
    take_blocks(1)
    gb = gather_sets([(own, kg_of, rows, rows)], me_h, me_c, h_send, h_recv, loc_b)
    next(gb)
    finish(ga, gb)
    for o in range(1, NH):
        h = lax.rem(me_h + NH - o, NH)
        remote(
            iqg.at[h], iqg_out.at[pl.ds(pl.multiple_of(h * QROWS, QROWS), QROWS)],
            i_send.at[o], i_recv.at[o], (h, me_c),
        ).wait_recv()
        remote(wg.at[h], wrecv.at[h], w_send.at[o], w_recv.at[o], (h, me_c)).wait_recv()
    for c in own_copies:
        c.wait()
    acc = wrecv[0]
    for h in range(1, NH):
        acc = acc + wrecv[h]
    wg_out[...] = acc
    for s in sends:
        s.wait_send()


SENT = jnp.bfloat16


def give_back(tab, grad, iqr, row, ik):
    f32, bf = jnp.float32, jnp.bfloat16
    any_spec = pl.BlockSpec(memory_space=ANY)
    vm_spec = pl.BlockSpec(memory_space=VM)
    rows = IHEADS * QROWS
    return pl.pallas_call(
        return_kernel,
        name="give_back",
        out_shape=(
            jax.ShapeDtypeStruct((NH * QROWS, 1024), f32),
            jax.ShapeDtypeStruct((8, 128), f32),
            jax.ShapeDtypeStruct((NH, NC * BLK, 128), SENT),
        ),
        in_specs=[pl.BlockSpec(memory_space=pltpu.SMEM)] + [vm_spec] * 4,
        out_specs=(any_spec, vm_spec, any_spec),
        scratch_shapes=[
            VM((rows, SETT), bf),
            VM((rows, SETT), bf),
            VM((128, 128), f32),
            VM((IHEADS, QROWS, 128), f32),
            VM((IHEADS, QROWS, 128), f32),
            VM((rows, 128), f32),
            VM((128, rows), bf),
            VM((NH, QROWS, 1024), f32),
            VM((NH, 8, 128), f32),
            VM((2, NH, SETT // 2, 128), f32),
            VM((2, NH - 1, SETT // 2, 128), f32),
            VM((2, SETB + 1, HB, 128), f32),
            VM((2, NC, HB, 128), f32),
            VM((2, NC, HB, 128), f32),
            VM((NC * BLK, 128), SENT),
            VM((NH, 8, 128), f32),
            DMA((2 * NH,)), DMA((2 * NH,)), DMA((NH,)), DMA((NH,)), DMA((NH,)), DMA((NH,)),
            DMA((2 * NC,)), DMA((2 * NC,)),
            DMA((9,)), DMA((9,)), DMA((9,)), DMA((9,)), DMA((4,)), DMA((1,)), DMA((1,)),
        ],
        compiler_params=pltpu.CompilerParams(
            collective_id=1, has_side_effects=True, vmem_limit_bytes=60 << 20
        ),
    )(tab, grad, iqr, row, ik)


def scatter_kernel(asked_s, kg_ref, out_ref):
    out_ref[...] = jnp.zeros(out_ref.shape, jnp.float32)

    def one(i, carry):
        h = lax.shift_right_logical(i, 4)
        r = lax.bitwise_and(i, 15)
        b = asked_s[r, h]
        for q in range(2):
            rows = pl.ds(pl.multiple_of(b * BLK + q * HB, HB), HB)
            part = kg_ref[h, pl.ds(pl.multiple_of((q * NC + r) * HB, HB), HB), :]
            out_ref[rows, :] = out_ref[rows, :] + part.astype(jnp.float32)
        return carry

    lax.fori_loop(0, NH * NC, one, 0, unroll=4)


def scatter(asked, kg, tokens):
    return pl.pallas_call(
        scatter_kernel,
        name="scatter",
        out_shape=jax.ShapeDtypeStruct((tokens, 128), jnp.float32),
        in_specs=[pl.BlockSpec(memory_space=pltpu.SMEM), pl.BlockSpec(memory_space=VM)],
        out_specs=pl.BlockSpec(memory_space=VM),
        compiler_params=pltpu.CompilerParams(vmem_limit_bytes=60 << 20),
    )(asked, kg)


def shards(main_query, latent, index_query, index_key, index_weight, selected, lengths, cotangent):
    sel_t = selected.T
    req, tab = make_plan(sel_t)
    grad, iqr, row, asked, ik = forward(
        tab, req, sel_t, lengths[None, :], cotangent[None, :],
        latent.T, index_key.reshape(-1, BLK, WIDTH), main_query, index_query, index_weight.T,
    )
    query_grad, weight_grad, kg = give_back(tab, grad, iqr, row, ik)
    key_grad = scatter(asked, kg, latent.shape[0])
    return query_grad, weight_grad.T, key_grad


def solution(mesh):
    return jax.shard_map(
        shards,
        mesh=mesh,
        in_specs=(
            P("ctx", "head"),
            P("ctx", None),
            P("ctx", "head"),
            P("ctx", None),
            P("ctx", "head"),
            P("ctx", None),
            P("ctx"),
            P("ctx"),
        ),
        out_specs=(P("ctx", "head"), P("ctx", "head"), P("ctx", None)),
        check_vma=False,
    )
```
